32 devices in a mesh: tile: 2 (over y), pts: 4 (over z), head: 4 (over x, core).
Axes of the slice: x: 2, y: 2, z: 4, core: 2. Of those that a mesh axis runs over, the one named last changes fastest.
Arguments:
- z_feat: bfloat16 [24544, 512], P(('tile', 'pts')), parts along dimension 0, may hold values from -12 to 12
- shard_count: int32 [8], P(('tile', 'pts')), parts along dimension 0, may hold values from 1028 to 3068, as said below
- hilbert_rank: int32 [24544], P(('tile', 'pts')), parts along dimension 0, may hold values from 0 to 8191, as said below
- z_slot: int32 [16384], P(('tile', 'pts')), parts along dimension 0, may hold values from 0 to 12271, as said below
- ln1_gain: float32 [512], replicated, may hold values from 0.25 to 1.75
- ln1_bias: float32 [512], replicated, may hold values from -1.5 to 1.5
- w_qkv: bfloat16 [3, 512, 512], P(None, None, 'head'), may hold values from -16 to 16
- w_out: bfloat16 [512, 512], P(None, 'head'), may hold values from -0.25 to 0.25
- b_out: float32 [512], P('head'), may hold values from -2.5 to 2.5
- ln2_gain: float32 [512], replicated, may hold values from 0.25 to 1.75
- ln2_bias: float32 [512], replicated, may hold values from -1.5 to 1.5
- w_up: bfloat16 [512, 2048], P(None, 'head'), may hold values from -0.25 to 0.25
- b_up: float32 [2048], P('head'), may hold values from -2.5 to 2.5
- w_down: bfloat16 [2048, 512], P('head'), may hold values from -0.125 to 0.125
- b_down: float32 [512], P('head'), may hold values from -2.5 to 2.5
Outputs:
- z_out: bfloat16 [24544, 512], P(('tile', 'pts'), 'head'), parts along dimension 0
The draws below stay inside these ranges and needn't reach their ends.
There are 2 independent parts, one for each index of `tile`. The reference program is written for one: setup_inputs(seed, part) draws one part's arguments, and reference() takes and returns one part's arrays. A program takes and returns all parts, laid end to end along the dimension named above; an argument that names none is the same for every part. Nothing has to cross between parts.
Inputs may be any that keep to these rules, and one draw needn't show every extreme that they name: `shard_count`: the number of points of z-order shard s, held in the first that many of its 3068 slots; the counts sum to 8192; some shard holds 3068 points. `hilbert_rank`: on occupied slots, a one to one map onto the 8192 Hilbert positions; empty slots hold 0; of the points of one z-order shard at most 1022 lie among the 2048 Hilbert positions of one index of pts, and some shard and index reach 1022. `z_slot`: the inverse of hilbert_rank: for Hilbert position h, the occupied slot whose hilbert_rank is h.
All inputs are finite; a program needn't handle non-finite values.
Results may differ from the reference program's by a relative error of at most 0.013.
Values may be sent and summed in bfloat16 or wider, within the bound.
No kernel may reach another device: no remote copies, remote signals or barrier semaphores. Data moves between devices by JAX's collectives and lax.ppermute only.
A program may use at most 64 MiB of HBM per device.

```python
import jax
import jax.numpy as jnp
from jax import lax

C = 512
HEADS = 32
PATCH = 1024
FF = 2048
PTS_DEV = 2048
HEAD_DIM = 16
NPTS = 8192
SKEW_STEP = 85
CAP = 1022
ZCAP = 3068
N_PTS = 4


def shuffle_valid(key, labels, shards):
    width = labels.shape[1]
    column_ids = jnp.arange(width, dtype=jnp.int32)[None, :]
    scores = jax.random.randint(key, labels.shape, 0, 2 ** 18, dtype=jnp.int32) * width + column_ids
    scores = jnp.where(labels < shards, scores, 2 ** 30 + column_ids)
    order = jnp.argsort(scores, axis=1)
    return jnp.take_along_axis(labels, order, axis=1)


def occurrence(labels, classes):
    onehot = (labels[..., None] == jnp.arange(classes + 1, dtype=jnp.int32)).astype(jnp.int32)
    before = jnp.cumsum(onehot, axis=1) - onehot
    return jnp.sum(before * onehot, axis=-1)


def shared_layout(key):
    key = jax.random.fold_in(key, 1234)
    key_skew, key_dest, key_source, key_target = jax.random.split(key, 4)
    shards = N_PTS
    per_pair = PTS_DEV // N_PTS
    shard_ids = jnp.arange(shards, dtype=jnp.int32)
    offsets = SKEW_STEP * (2 * shard_ids - (shards - 1))
    offsets = jax.random.permutation(key_skew, offsets)
    dest_factor = jax.random.permutation(key_dest, 2 * (shard_ids % 2))
    pair_rows = per_pair + offsets[:, None] * dest_factor[None, :]
    counts = jnp.sum(pair_rows, axis=1).astype(jnp.int32)
    slot_ids = jnp.arange(ZCAP, dtype=jnp.int32)
    source_bounds = jnp.cumsum(pair_rows, axis=1)
    source_label = jnp.sum((source_bounds[:, None, :] <= slot_ids[None, :, None]).astype(jnp.int32), axis=2)
    source_label = shuffle_valid(key_source, source_label, shards)
    position_ids = jnp.arange(PTS_DEV, dtype=jnp.int32)
    target_bounds = jnp.cumsum(pair_rows, axis=0).T
    target_label = jnp.sum((target_bounds[:, None, :] <= position_ids[None, :, None]).astype(jnp.int32), axis=2)
    target_label = shuffle_valid(key_target, target_label, shards)
    source_occ = occurrence(source_label, shards)
    target_occ = occurrence(target_label, shards)
    target_rows = jnp.broadcast_to(shard_ids[:, None], (shards, PTS_DEV))
    position_table = jnp.zeros((shards, shards, CAP), jnp.int32).at[target_rows, target_label, target_occ].set(jnp.broadcast_to(position_ids[None, :], (shards, PTS_DEV)))
    source_rows = jnp.broadcast_to(shard_ids[:, None], (shards, ZCAP))
    occupied = source_label < shards
    capped_occ = jnp.minimum(source_occ, CAP - 1)
    slot_table = jnp.zeros((shards, shards + 1, CAP), jnp.int32).at[source_rows, source_label, capped_occ].set(jnp.broadcast_to(slot_ids[None, :], (shards, ZCAP)))
    clipped_label = jnp.minimum(source_label, shards - 1)
    ranks = clipped_label * PTS_DEV + position_table[clipped_label, source_rows, capped_occ]
    ranks = jnp.where(occupied, ranks, 0).astype(jnp.int32)
    slots = target_label * ZCAP + slot_table[target_label, target_rows, target_occ]
    return (counts, ranks.reshape(-1), slots.reshape(-1).astype(jnp.int32))


def draw_shard_count(key, part):
    return shared_layout(key)[0]


def draw_hilbert_rank(key, part):
    return shared_layout(key)[1]


def draw_z_slot(key, part):
    return shared_layout(key)[2]


def draw_z_feat(key, part):
    key = jax.random.fold_in(key, 77)
    key_noise = jax.random.fold_in(key, 3)
    rows = N_PTS * ZCAP
    noise = jax.random.normal(key_noise, (rows, C), jnp.float32)
    feats = jnp.clip(noise, -6.0, 6.0)
    return feats.astype(jnp.bfloat16)


def draw_w_qkv(key, part):
    key = jax.random.fold_in(key, 91)
    key_base = jax.random.fold_in(key, 0)
    sigma = C ** (-0.5)
    base = jnp.clip(jax.random.normal(key_base, (3, C, C), jnp.float32), -4.0, 4.0) * sigma
    mats = base
    return jnp.clip(mats, -16.0, 16.0).astype(jnp.bfloat16)


def level_of(own_key, dims, cuts, smallest, high):
    loudness, own = 1.0, jax.random.fold_in(own_key, 6)
    for dim, parts in cuts:
        draws = jnp.exp(jax.random.uniform(jax.random.fold_in(own, dim), (parts,), jnp.float32, smallest / len(cuts), high / len(cuts)))
        loudness = loudness * jnp.repeat(draws, dims[dim] // parts).reshape([-1 if axis == dim else 1 for axis in range(len(dims))])
    return loudness


def gaussian(rng, shape, scale, most, pieces=(), kind=jnp.bfloat16):
    values = jax.random.normal(rng, shape, jnp.float32) * scale
    if len(pieces) > 0:
        values = level_of(rng, shape, pieces, -0.22, 0.18) * values
    return jnp.clip(values, min=-most, max=most).astype(kind)


def setup_inputs(seed: int = 0, part: int = 0) -> dict:
    streams_of = jax.random.split(jax.random.key(seed), 16)
    own_keys = jax.random.split(jax.random.fold_in(streams_of[15], part), 16)
    z_feat = draw_z_feat(jax.random.fold_in(jax.random.fold_in(streams_of[15], part), 71), part)
    shard_count = draw_shard_count(jax.random.fold_in(jax.random.fold_in(streams_of[15], part), 71), part)
    hilbert_rank = draw_hilbert_rank(jax.random.fold_in(jax.random.fold_in(streams_of[15], part), 71), part)
    z_slot = draw_z_slot(jax.random.fold_in(jax.random.fold_in(streams_of[15], part), 71), part)
    ln1_gain = jnp.clip(1.0 + 0.15 * jax.random.normal(streams_of[4], (C,), jnp.float32), 0.25, 1.75)
    ln1_bias = gaussian(streams_of[5], (C,), 0.3, 1.5, (), jnp.float32)
    w_qkv = draw_w_qkv(jax.random.fold_in(streams_of[15], 71), part)
    w_out = gaussian(streams_of[7], (C, C), C ** -0.5, 0.25, ((1, 4),))
    b_out = gaussian(streams_of[8], (C,), 0.5, 2.5, ((0, 4),), jnp.float32)
    ln2_gain = jnp.clip(1.0 + 0.15 * jax.random.normal(streams_of[9], (C,), jnp.float32), 0.25, 1.75)
    ln2_bias = gaussian(streams_of[10], (C,), 0.3, 1.5, (), jnp.float32)
    w_up = gaussian(streams_of[11], (C, FF), C ** -0.5, 0.25, ((1, 4),))
    b_up = gaussian(streams_of[12], (FF,), 0.5, 2.5, ((0, 4),), jnp.float32)
    w_down = gaussian(streams_of[13], (FF, C), FF ** -0.5, 0.125, ((0, 4),))
    b_down = gaussian(streams_of[14], (C,), 0.5, 2.5, ((0, 4),), jnp.float32)
    return {"z_feat": z_feat, "shard_count": shard_count, "hilbert_rank": hilbert_rank, "z_slot": z_slot, "ln1_gain": ln1_gain, "ln1_bias": ln1_bias, "w_qkv": w_qkv, "w_out": w_out, "b_out": b_out, "ln2_gain": ln2_gain, "ln2_bias": ln2_bias, "w_up": w_up, "b_up": b_up, "w_down": w_down, "b_down": b_down}


def layer_norm(widened, norm_gain, norm_bias):
    width = widened.shape[1]
    row_mean = lax.optimization_barrier(jnp.sum(widened, axis=1, keepdims=True)) / width
    row_square = lax.optimization_barrier(jnp.sum(widened * widened, axis=1, keepdims=True)) / width
    row_var = row_square - row_mean * row_mean
    return (widened - row_mean) * lax.rsqrt(row_var + 1e-05) * norm_gain + norm_bias

def reference(z_feat, shard_count, hilbert_rank, z_slot, ln1_gain, ln1_bias, w_qkv, w_out, b_out, ln2_gain, ln2_bias, w_up, b_up, w_down, b_down):
    features = jnp.take(z_feat, z_slot, axis=0)
    normed = layer_norm(features.astype(jnp.float32), ln1_gain, ln1_bias).astype(jnp.bfloat16)
    projected = jnp.stack([jnp.dot(normed, w_qkv[0], preferred_element_type=jnp.float32), jnp.dot(normed, w_qkv[1], preferred_element_type=jnp.float32), jnp.dot(normed, w_qkv[2], preferred_element_type=jnp.float32)]).astype(jnp.bfloat16)
    patches = NPTS // PATCH
    projected = projected.reshape(3, patches, PATCH, HEADS, HEAD_DIM)
    projected = jnp.moveaxis(projected, 1, 0)
    score_scale = HEAD_DIM ** (-0.5)

    def attend(patch_block):
        queries = patch_block[0].astype(jnp.float32)
        key_rows = patch_block[1].astype(jnp.float32)
        value_rows = patch_block[2].astype(jnp.float32)
        scores = jnp.einsum('qhd,khd->hqk', queries, key_rows) * score_scale
        raised = jnp.exp(scores - lax.optimization_barrier(jnp.max(scores, axis=2, keepdims=True)))
        weights_bf = (raised / lax.optimization_barrier(jnp.sum(raised, axis=2, keepdims=True))).astype(jnp.bfloat16)
        return jnp.einsum('hqk,khd->qhd', weights_bf.astype(jnp.float32), value_rows).astype(jnp.bfloat16)
    attended = lax.map(attend, projected).reshape(NPTS, HEADS * HEAD_DIM)
    residual = (features.astype(jnp.float32) + jnp.dot(attended, w_out, preferred_element_type=jnp.float32) + b_out).astype(jnp.bfloat16)
    normed_two = layer_norm(residual.astype(jnp.float32), ln2_gain, ln2_bias).astype(jnp.bfloat16)
    hidden = jax.nn.gelu(jnp.dot(normed_two, w_up, preferred_element_type=jnp.float32) + b_up, approximate=False).astype(jnp.bfloat16)
    block_out = (residual.astype(jnp.float32) + jnp.dot(hidden, w_down, preferred_element_type=jnp.float32) + b_down).astype(jnp.bfloat16)
    slot_ids = jnp.arange(N_PTS * ZCAP, dtype=jnp.int32)
    occupied = slot_ids % ZCAP < jnp.repeat(shard_count, ZCAP)
    picked = jnp.take(block_out, hilbert_rank, axis=0)
    return jnp.where(occupied[:, None], picked, jnp.zeros_like(picked))
```

```python
import functools
import math

import jax
import jax.numpy as jnp
from jax import lax
from jax.experimental import pallas as pl
from jax.experimental.pallas import tpu as pltpu
from jax.sharding import PartitionSpec as P

PATCH = 1024
HEAD_DIM = 16
LANES = 128
F32 = jnp.float32
BF = jnp.bfloat16
I32 = jnp.int32
SMEM = pl.BlockSpec(memory_space=pltpu.SMEM)
VMEM = pl.BlockSpec(memory_space=pltpu.VMEM)
ANY = pl.BlockSpec(memory_space=pl.ANY)


def dot(lhs, rhs, dims=(1, 0)):
    return lax.dot_general(
        lhs, rhs, (((dims[0],), (dims[1],)), ((), ())), preferred_element_type=F32
    )


def round_up(value, unit):
    return (value + unit - 1) // unit * unit


def copies_in(sources, targets, sems):
    copies = [
        pltpu.make_async_copy(source, target, sems.at[i])
        for i, (source, target) in enumerate(zip(sources, targets))
    ]
    for copy in copies:
        copy.start()
    return copies


def convert_rows(source, source_at, target, target_at, rows, step):
    def one(i, carry):
        at = pl.multiple_of(i * step, step)
        target[pl.ds(target_at + at, step), :] = source[pl.ds(source_at + at, step), :].astype(
            target.dtype
        )
        return carry

    lax.fori_loop(0, rows // step, one, 0, unroll=2)


def pack_kernel(
    shards, cap, rows_here, columns_at, meta, rank, z_feat, *refs
):
    sends = refs[:shards]
    place_out = refs[shards]
    place, place_smem, narrow, wide, packed, sems = refs[shards + 1 :]
    here, count = meta[0], meta[2]
    slots = place.shape[1]
    zone_rows, width = narrow.shape
    if columns_at:
        column = pl.multiple_of(meta[1] * width, width)
        source = z_feat.at[:, pl.ds(column, width)]
    else:
        source = z_feat
    feature_copy = pltpu.make_async_copy(source, narrow, sems.at[0])
    feature_copy.start()

    grid_rows = shards * rows_here // LANES
    block = rows_here // LANES
    ranks = rank[...]
    occupied = lax.broadcasted_iota(I32, (1, slots), 1) < count
    major = jnp.where(occupied, ranks // LANES, -1)
    minor = ranks % LANES
    hot_major = (lax.broadcasted_iota(I32, (grid_rows, slots), 0) == major).astype(BF)
    hot_minor = (lax.broadcasted_iota(I32, (LANES, slots), 0) == minor).astype(BF)
    members = dot(hot_minor, hot_major, (1, 1)).astype(BF)
    minor_r = lax.broadcasted_iota(I32, (LANES, LANES), 0)
    minor_c = lax.broadcasted_iota(I32, (LANES, LANES), 1)
    below = (minor_c < minor_r).astype(BF)
    major_r = lax.broadcasted_iota(I32, (grid_rows, grid_rows), 0)
    major_c = lax.broadcasted_iota(I32, (grid_rows, grid_rows), 1)
    earlier = ((major_r < major_c) & (major_r // block == major_c // block)).astype(BF)
    row_wise = dot(members, earlier)
    counts = dot(below, members) + dot(jnp.ones((LANES, LANES), BF), row_wise.astype(BF))
    high = jnp.floor(counts * (1.0 / 32.0))
    low = counts - high * 32.0
    spread = dot(high.astype(BF), hot_major) * 32.0 + dot(low.astype(BF), hot_major)
    found = jnp.sum(jnp.where(hot_minor > 0, spread, 0.0), axis=0, keepdims=True)
    target = ranks // rows_here
    place[...] = jnp.where(occupied, target * cap + found.astype(I32), shards * cap)
    to_smem = pltpu.make_async_copy(place, place_smem, sems.at[1])
    to_smem.start()
    to_out = pltpu.make_async_copy(place, place_out, sems.at[2])
    to_out.start()
    feature_copy.wait()
    whole_rows = zone_rows // 16 * 16
    convert_rows(narrow, 0, wide, 0, whole_rows, 16)
    if whole_rows < zone_rows:
        wide[pl.ds(whole_rows, zone_rows - whole_rows), :] = narrow[
            pl.ds(whole_rows, zone_rows - whole_rows), :
        ].astype(F32)
    to_smem.wait()

    def place_rows(i, carry):
        base = pl.multiple_of(i * 8, 8)
        for k in range(8):
            packed[pl.ds(place_smem[0, base + k], 1), :] = wide[pl.ds(base + k, 1), :]
        return carry

    lax.fori_loop(0, (count + 7) // 8, place_rows, 0)
    for k in range(shards):
        at = pl.multiple_of(lax.rem(here + k, shards) * cap, cap)
        convert_rows(packed, at, sends[k], 0, cap, 16)
    to_out.wait()


def pack(meta, rank, z_feat, columns_at, width, shards, cap, rows_here):
    zone_rows = z_feat.shape[0]
    slots = rank.shape[1]
    return pl.pallas_call(
        functools.partial(pack_kernel, shards, cap, rows_here, columns_at),
        out_shape=[jax.ShapeDtypeStruct((cap, width), BF)] * shards
        + [jax.ShapeDtypeStruct((1, slots), I32)],
        in_specs=[SMEM, VMEM, ANY],
        out_specs=[VMEM] * shards + [ANY],
        scratch_shapes=[
            pltpu.VMEM((1, slots), I32),
            pltpu.SMEM((1, slots), I32),
            pltpu.VMEM((zone_rows, width), BF),
            pltpu.VMEM((slots, width), F32),
            pltpu.VMEM((shards * cap + 8, width), F32),
            pltpu.SemaphoreType.DMA((3,)),
        ],
        name="pack",
    )(meta, rank, z_feat)


def move_segment(source, source_at, target, target_at, length):
    def one(i, carry):
        for k in range(4):
            target[pl.ds(target_at + i * 32 + k * 8, 8), :] = source[
                pl.ds(source_at + i * 32 + k * 8, 8), :
            ]
        return carry

    lax.fori_loop(0, (length + 31) // 32, one, 0)


def segment_starts(pieces, patches, shards, cap):
    packed_at, patch_at = {}, {}
    for s in range(shards):
        at = s * cap
        for p in range(patches):
            packed_at[p, s] = at
            at = at + pieces[p, s]
    for p in range(patches):
        at = p * PATCH
        for s in range(shards):
            patch_at[p, s] = at
            at = at + pieces[p, s]
    return packed_at, patch_at


def compact_kernel(shards, patches, group, cap, meta, pieces, *refs):
    blocks = refs[:shards]
    outs = refs[shards : shards + patches]
    narrow, wide, patch_rows, sems = refs[shards + patches :]
    here, member = meta[0], meta[1]
    sources = [lax.rem(here - k + shards, shards) for k in range(shards)]
    arrivals = copies_in(blocks, [narrow.at[s] for s in sources], sems)
    for copy in arrivals:
        copy.wait()
    for s in range(shards):
        convert_rows(narrow.at[s], 0, wide, s * cap, cap, 16)
    packed_at, patch_at = segment_starts(pieces, patches, shards, cap)
    for p in range(patches):
        for s in range(shards):
            move_segment(wide, packed_at[p, s], patch_rows, patch_at[p, s], pieces[p, s])
    own_group = member // group
    for k in range(patches):
        at = pl.multiple_of(lax.rem(own_group + k, patches) * PATCH, PATCH)
        convert_rows(patch_rows, at, outs[k], 0, PATCH, 16)


def compact(meta, pieces, blocks, patches, group):
    shards = len(blocks)
    cap, width = blocks[0].shape
    return pl.pallas_call(
        functools.partial(compact_kernel, shards, patches, group, cap),
        out_shape=[jax.ShapeDtypeStruct((PATCH, width), BF)] * patches,
        in_specs=[SMEM, SMEM] + [ANY] * shards,
        out_specs=[VMEM] * patches,
        scratch_shapes=[
            pltpu.VMEM((shards, cap, width), BF),
            pltpu.VMEM((shards * cap + 64, width), F32),
            pltpu.VMEM((patches * PATCH + 64, width), F32),
            pltpu.SemaphoreType.DMA((shards,)),
        ],
        name="compact",
    )(meta, pieces, *blocks)


def spread_kernel(shards, patches, members, cap, meta, pieces, *refs):
    blocks = refs[:members]
    sends = refs[members : members + shards]
    narrow, patch_rows, wide, sems = refs[members + shards :]
    here, member = meta[0], meta[1]
    part_rows = narrow.shape[1]
    sources = [lax.rem(member - k + members, members) for k in range(members)]
    arrivals = copies_in(blocks, [narrow.at[s] for s in sources], sems)
    for copy in arrivals:
        copy.wait()
    for s in range(members):
        convert_rows(narrow.at[s], 0, patch_rows, s * part_rows, part_rows, 16)
    packed_at, patch_at = segment_starts(pieces, patches, shards, cap)
    for s in range(shards):
        for p in range(patches):
            move_segment(patch_rows, patch_at[p, s], wide, packed_at[p, s], pieces[p, s])
    for k in range(shards):
        at = pl.multiple_of(lax.rem(here + k, shards) * cap, cap)
        convert_rows(wide, at, sends[k], 0, cap, 16)


def spread(meta, pieces, blocks, patches, shards, cap):
    members = len(blocks)
    part_rows, width = blocks[0].shape
    return pl.pallas_call(
        functools.partial(spread_kernel, shards, patches, members, cap),
        out_shape=[jax.ShapeDtypeStruct((cap, width), BF)] * shards,
        in_specs=[SMEM, SMEM] + [ANY] * members,
        out_specs=[VMEM] * shards,
        scratch_shapes=[
            pltpu.VMEM((members, part_rows, width), BF),
            pltpu.VMEM((patches * PATCH + 64, width), F32),
            pltpu.VMEM((shards * cap + 64, width), F32),
            pltpu.SemaphoreType.DMA((members,)),
        ],
        name="spread",
    )(meta, pieces, *blocks)


def unpack_kernel(shards, cap, meta, place, *refs):
    blocks = refs[:shards]
    out = refs[shards]
    narrow, wide, picked, sems = refs[shards + 1 :]
    here, count = meta[0], meta[2]
    zone_rows, width = out.shape
    sources = [lax.rem(here - k + shards, shards) for k in range(shards)]
    arrivals = copies_in(blocks, [narrow.at[s] for s in sources], sems)
    for copy in arrivals:
        copy.wait()
    for s in range(shards):
        convert_rows(narrow.at[s], 0, wide, s * cap, cap, 16)

    def pick_rows(i, carry):
        base = pl.multiple_of(i * 8, 8)
        for k in range(8):
            picked[pl.ds(base + k, 1), :] = wide[pl.ds(place[0, base + k], 1), :]
        return carry

    lax.fori_loop(0, (count + 7) // 8, pick_rows, 0)

    def masked(at, rows):
        slot = at + lax.broadcasted_iota(I32, (rows, width), 0)
        out[pl.ds(at, rows), :] = jnp.where(slot < count, picked[pl.ds(at, rows), :], 0.0).astype(
            BF
        )

    def one(i, carry):
        masked(pl.multiple_of(i * 16, 16), 16)
        return carry

    whole_rows = zone_rows // 16 * 16
    lax.fori_loop(0, whole_rows // 16, one, 0, unroll=2)
    if whole_rows < zone_rows:
        masked(whole_rows, zone_rows - whole_rows)


def unpack(meta, place, blocks, zone_rows):
    shards = len(blocks)
    cap, width = blocks[0].shape
    slots = place.shape[1]
    return pl.pallas_call(
        functools.partial(unpack_kernel, shards, cap),
        out_shape=jax.ShapeDtypeStruct((zone_rows, width), BF),
        in_specs=[SMEM, SMEM] + [ANY] * shards,
        out_specs=VMEM,
        scratch_shapes=[
            pltpu.VMEM((shards, cap, width), BF),
            pltpu.VMEM((shards * cap + 8, width), F32),
            pltpu.VMEM((slots, width), F32),
            pltpu.SemaphoreType.DMA((shards,)),
        ],
        name="unpack",
    )(meta, place, *blocks)


def row_stats(parts, width):
    total = jnp.sum(sum(parts[1:], parts[0]), axis=1, keepdims=True)
    squares = jnp.sum(
        sum((x * x for x in parts[1:]), parts[0] * parts[0]), axis=1, keepdims=True
    )
    mean = total / width
    var = squares / width - mean * mean
    return mean, lax.rsqrt(var + 1e-05)


def attend_kernel(blocks, queries, chunk, ids, gain, bias, *refs):
    feats = refs[:blocks]
    weights = refs[blocks : 2 * blocks]
    out, kept = refs[2 * blocks : 2 * blocks + 2]
    features, weight, normed, keys, query, mixed, sems = refs[2 * blocks + 2 :]
    rows = features.shape[1]
    width = blocks * LANES
    places = [ids[k] for k in range(blocks)]
    feature_copies = copies_in(feats, [features.at[k] for k in places], sems)
    weight_copies = copies_in(weights, [weight.at[k] for k in places], sems.at[pl.ds(blocks, blocks)])
    for copy in feature_copies:
        copy.wait()
    first = pl.multiple_of(ids[blocks] * queries, queries)

    def norm(i, carry):
        at = pl.ds(pl.multiple_of(i * 128, 128), 128)
        parts = [features[b, at, :].astype(F32) for b in range(blocks)]
        mean, scale = row_stats(parts, width)
        for b in range(blocks):
            cols = slice(b * LANES, (b + 1) * LANES)
            normed[at, cols] = (
                (parts[b] - mean) * scale * gain[0:1, cols] + bias[0:1, cols]
            ).astype(BF)
        return carry

    lax.fori_loop(0, rows // 128, norm, 0, unroll=2)
    for b in range(blocks):
        kept[b] = features[b, pl.ds(first, queries), :]
    for copy in weight_copies:
        copy.wait()
    lane = lax.broadcasted_iota(I32, (1, LANES), 1)
    keys[:, 2 * LANES :] = jnp.ones((rows, LANES), BF)
    score_scale = HEAD_DIM ** (-0.5) * math.log2(math.e)

    def one_block(b, carry):
        key_value = jnp.concatenate([weight[b, 1], weight[b, 2]], axis=1)
        for i in range(rows // 256):
            at = pl.ds(i * 256, 256)
            keys[at, : 2 * LANES] = dot(normed[at, :], key_value).astype(BF)
        for i in range(queries // chunk):
            at = pl.ds(pl.multiple_of(first + i * chunk, chunk), chunk)
            query[pl.ds(i * chunk, chunk), :] = (
                dot(normed[at, :], weight[b, 0]) * score_scale
            ).astype(BF)

        def one_head(j, carry):
            mask = lane // HEAD_DIM == j
            for i in range(queries // chunk):
                at = pl.ds(i * chunk, chunk)
                own = jnp.where(mask, query[at, :], jnp.zeros((), BF))
                scores = dot(own, keys[:, :LANES], (1, 1))
                raised = jnp.exp2(scores - jnp.max(scores, axis=1, keepdims=True)).astype(BF)
                summed = dot(raised, keys[:, LANES:])
                mixed[at, :] = jnp.where(
                    mask, summed[:, :LANES] / summed[:, LANES:], mixed[at, :]
                )
            return carry

        lax.fori_loop(0, LANES // HEAD_DIM, one_head, 0)
        out[b] = mixed[...].astype(BF)
        return carry

    lax.fori_loop(0, blocks, one_block, 0)


def attend(ids, feats, weights, gain, bias, queries):
    blocks = len(feats)
    rows = feats[0].shape[0]
    width = weights[0].shape[1]
    chunk = min(128, queries)
    flops = 4 * queries * rows * LANES * blocks * (LANES // HEAD_DIM)
    return pl.pallas_call(
        functools.partial(attend_kernel, blocks, queries, chunk),
        out_shape=[jax.ShapeDtypeStruct((blocks, queries, LANES), BF)] * 2,
        in_specs=[SMEM, VMEM, VMEM] + [ANY] * (2 * blocks),
        out_specs=[VMEM, VMEM],
        scratch_shapes=[
            pltpu.VMEM((blocks, rows, LANES), BF),
            pltpu.VMEM((blocks, 3, width, LANES), BF),
            pltpu.VMEM((rows, width), BF),
            pltpu.VMEM((rows, 3 * LANES), BF),
            pltpu.VMEM((queries, LANES), BF),
            pltpu.VMEM((queries, LANES), F32),
            pltpu.SemaphoreType.DMA((2 * blocks,)),
        ],
        cost_estimate=pl.CostEstimate(
            flops=flops, bytes_accessed=4 * rows * width, transcendentals=0
        ),
        name="attend",
    )(ids, gain, bias, *feats, *weights)


def mlp_kernel(blocks, members, sends, chunk, ids, gain, bias, mixed, kept, *refs):
    projs = refs[:blocks]
    ups = refs[blocks : blocks + members]
    downs = refs[blocks + members : blocks + 2 * members]
    vectors = refs[blocks + 2 * members : blocks + 3 * members]
    results = refs[blocks + 3 * members : blocks + 3 * members + sends]
    proj, up, down, vector, final, sems = refs[blocks + 3 * members + sends :]
    rows = mixed.shape[1]
    width = blocks * LANES
    hidden_here = up.shape[2]
    share = width // members
    spots = [ids[blocks + 1 + k] for k in range(members)]
    copies = copies_in(projs, [proj.at[ids[k]] for k in range(blocks)], sems)
    copies += copies_in(
        vectors, [vector.at[k] for k in spots], sems.at[pl.ds(blocks, members)]
    )
    late = copies_in(
        ups, [up.at[k] for k in range(members)], sems.at[pl.ds(blocks + members, members)]
    )
    late += copies_in(
        downs, [down.at[k] for k in range(members)], sems.at[pl.ds(blocks + 2 * members, members)]
    )
    for copy in copies:
        copy.wait()
    for copy in late:
        copy.wait()
    out_bias = jnp.concatenate([vector[k, :, :share] for k in range(members)], axis=1)
    down_bias = jnp.concatenate([vector[k, :, share : 2 * share] for k in range(members)], axis=1)
    out_weight = jnp.concatenate([proj[b] for b in range(blocks)], axis=1)
    root_half = 0.5 ** 0.5

    def one(i, carry):
        at = pl.ds(pl.multiple_of(i * chunk, chunk), chunk)
        attended = jnp.concatenate([mixed[b, at, :] for b in range(blocks)], axis=1)
        features = jnp.concatenate([kept[b, at, :] for b in range(blocks)], axis=1)
        residual = (features.astype(F32) + dot(attended, out_weight) + out_bias).astype(BF)
        wide = residual.astype(F32)
        mean, scale = row_stats([wide], width)
        normed = ((wide - mean) * scale * gain[...] + bias[...]).astype(BF)
        total = wide + down_bias
        for k in range(members):
            spot = spots[k]
            before = dot(normed, up[k]) + vector[spot, :, 2 * share :]
            hidden = (0.5 * before * (1.0 + lax.erf(before * root_half))).astype(BF)
            total = total + dot(hidden, down[k])
        for b in range(blocks):
            final[b, at, :] = total[:, b * LANES : (b + 1) * LANES].astype(BF)
        return carry

    lax.fori_loop(0, rows // chunk, one, 0)
    if sends > 1:
        me = ids[blocks + 1]
        for k in range(sends):
            results[k][...] = final[lax.rem(me + k, sends)]
    else:
        results[0][...] = final[...]


def mlp(ids, gain, bias, mixed, kept, projs, ups, downs, vectors):
    blocks, rows, _ = mixed.shape
    members = len(ups)
    width = blocks * LANES
    hidden_here = ups[0].shape[1]
    sends = members if members == blocks else 1
    shape = (rows, LANES) if sends > 1 else (blocks, rows, LANES)
    chunk = min(256, rows)
    return pl.pallas_call(
        functools.partial(mlp_kernel, blocks, members, sends, chunk),
        out_shape=[jax.ShapeDtypeStruct(shape, BF)] * sends,
        in_specs=[SMEM, VMEM, VMEM, VMEM, VMEM] + [ANY] * (blocks + 3 * members),
        out_specs=[VMEM] * sends,
        scratch_shapes=[
            pltpu.VMEM((blocks, width, LANES), BF),
            pltpu.VMEM((members, width, hidden_here), BF),
            pltpu.VMEM((members, hidden_here, width), BF),
            pltpu.VMEM((members, 1, vectors[0].shape[1]), F32),
            pltpu.VMEM((blocks, rows, LANES), BF),
            pltpu.SemaphoreType.DMA((blocks + 3 * members,)),
        ],
        cost_estimate=pl.CostEstimate(
            flops=4 * rows * width * hidden_here * members,
            bytes_accessed=4 * width * hidden_here * members,
            transcendentals=0,
        ),
        name="mlp",
    )(ids, gain, bias, mixed, kept, *projs, *ups, *downs, *vectors)


def shift(array, axis, size, step):
    return lax.ppermute(array, axis, [(i, (i + step) % size) for i in range(size)])


def exchange(blocks, axis, size):
    if size <= 8:
        return [blocks[0]] + [shift(blocks[k], axis, size, k) for k in range(1, size)]
    me = lax.axis_index(axis)
    steps = jnp.arange(size, dtype=I32)
    stacked = jnp.stack(blocks)[(steps - me) % size]
    got = lax.all_to_all(stacked, axis, 0, 0, tiled=True)[(me - steps) % size]
    return [got[k] for k in range(size)]


def gather_members(array, groups, group):
    size = groups * group
    found = []
    for k in range(groups):
        pairs = [(i, (i // group + k) % groups * group + i % group) for i in range(size)]
        moved = array if k == 0 else lax.ppermute(array, "head", pairs)
        for j in range(group):
            pairs = [(i, i // group * group + (i % group + j) % group) for i in range(size)]
            found.append(moved if j == 0 else lax.ppermute(moved, "head", pairs))
    return found


def body(
    z_feat,
    shard_count,
    hilbert_rank,
    z_slot,
    ln1_gain,
    ln1_bias,
    w_qkv,
    w_out,
    b_out,
    ln2_gain,
    ln2_bias,
    w_up,
    b_up,
    w_down,
    b_down,
):
    shards = lax.axis_size("pts")
    members = lax.axis_size("head")
    rows_here = z_slot.shape[0]
    zone_rows, full_width = z_feat.shape
    width = w_out.shape[1]
    patches = rows_here // PATCH
    group = members // patches
    queries = PATCH // group
    blocks = full_width // LANES
    skew_step = rows_here // (2 * shards * (shards - 1))
    cap = round_up(rows_here // shards + 2 * skew_step * (shards - 1), 16)
    here = lax.axis_index("pts")
    member = lax.axis_index("head")
    meta = jnp.stack([here, member, shard_count[0]]).astype(I32)

    order = [
        (member // group - k) % patches * group + (member % group - j) % group
        for k in range(patches)
        for j in range(group)
    ]
    spots = jnp.stack(order).astype(I32)
    part = (member % group).astype(I32)[None]

    def natural(found):
        stacked = jnp.stack(found)
        back = jnp.zeros((members,), I32).at[spots].set(jnp.arange(members, dtype=I32))
        stacked = jnp.take(stacked, back, axis=0)
        joined = jnp.concatenate([stacked[i] for i in range(members)], axis=-1)
        return [joined[..., b * LANES : (b + 1) * LANES] for b in range(blocks)]

    qkv_found = gather_members(w_qkv, patches, group)
    out_found = gather_members(w_out, patches, group)
    up_found = gather_members(w_up, patches, group)
    down_found = gather_members(w_down, patches, group)
    vectors = gather_members(
        jnp.concatenate([b_out, b_down, b_up])[None, :], patches, group
    )

    slots = round_up(zone_rows, LANES)
    rank = jnp.pad(hilbert_rank, (0, slots - zone_rows))[None, :]
    if width % LANES == 0:
        z_source = z_feat
    else:
        z_source = lax.dynamic_slice_in_dim(z_feat, member * width, width, 1)
    *sends, place = pack(
        meta, rank, z_source, width % LANES == 0, width, shards, cap, rows_here
    )
    source = (z_slot // zone_rows).reshape(patches, PATCH, 1)
    pieces = jnp.sum((source == jnp.arange(shards, dtype=I32)).astype(I32), axis=1)
    arrived = exchange(sends, "pts", shards)
    patch_blocks = compact(meta, pieces, arrived, patches, group)
    feats = []
    for k in range(patches):
        pairs = [(i, (i // group + k) % patches * group + i % group) for i in range(members)]
        moved = patch_blocks[k] if k == 0 else lax.ppermute(patch_blocks[k], "head", pairs)
        for j in range(group):
            pairs = [(i, i // group * group + (i % group + j) % group) for i in range(members)]
            feats.append(moved if j == 0 else lax.ppermute(moved, "head", pairs))

    if width == LANES:
        block_ids = spots
        qkv_blocks, out_blocks = qkv_found, out_found
    else:
        block_ids = jnp.arange(blocks, dtype=I32)
        feats = natural(feats)
        qkv_blocks, out_blocks = natural(qkv_found), natural(out_found)
    ids = jnp.concatenate([block_ids, part, spots])

    mixed, kept = attend(
        ids, feats, qkv_blocks, ln1_gain[None, :], ln1_bias[None, :], queries
    )
    results = mlp(
        ids,
        ln2_gain[None, :],
        ln2_bias[None, :],
        mixed,
        kept,
        out_blocks,
        up_found,
        down_found,
        vectors,
    )
    if width != LANES:
        joined = jnp.concatenate([results[0][b] for b in range(blocks)], axis=1)
        results = [
            lax.dynamic_slice_in_dim(joined, (member + k) % members * width, width, 1)
            for k in range(members)
        ]
    parts = [results[0]] + [shift(results[k], "head", members, k) for k in range(1, members)]
    outgoing = spread(meta, pieces, parts, patches, shards, cap)
    returned = exchange(outgoing, "pts", shards)
    return unpack(meta, place, returned, zone_rows)


def solution(mesh):
    placed = (
        P(("tile", "pts"), None),
        P(("tile", "pts")),
        P(("tile", "pts")),
        P(("tile", "pts")),
        P(),
        P(),
        P(None, None, "head"),
        P(None, "head"),
        P("head"),
        P(),
        P(),
        P(None, "head"),
        P("head"),
        P("head", None),
        P("head"),
    )
    return jax.shard_map(
        body, mesh=mesh, in_specs=placed, out_specs=P(("tile", "pts"), "head"), check_vma=False
    )
```

```python
import functools
import math

import jax
import jax.numpy as jnp
from jax import lax
from jax.experimental import pallas as pl
from jax.experimental.pallas import tpu as pltpu
from jax.sharding import PartitionSpec as P

PATCH = 1024
HEAD_DIM = 16
LANES = 128
ROW_STEP = 32
F32 = jnp.float32
BF = jnp.bfloat16
I32 = jnp.int32
SMEM = pl.BlockSpec(memory_space=pltpu.SMEM)
VMEM = pl.BlockSpec(memory_space=pltpu.VMEM)
ANY = pl.BlockSpec(memory_space=pl.ANY)


def dot(lhs, rhs, dims=(1, 0)):
    return lax.dot_general(
        lhs, rhs, (((dims[0],), (dims[1],)), ((), ())), preferred_element_type=F32
    )


def round_up(value, unit):
    return (value + unit - 1) // unit * unit


def copies_in(sources, targets, sems):
    copies = [
        pltpu.make_async_copy(source, target, sems.at[i])
        for i, (source, target) in enumerate(zip(sources, targets))
    ]
    for copy in copies:
        copy.start()
    return copies


def convert_rows(source, source_at, target, target_at, rows):
    step = math.gcd(rows, 128)

    def one(i, carry):
        at = pl.multiple_of(i * step, step)
        target[pl.ds(target_at + at, step), :] = source[pl.ds(source_at + at, step), :].astype(
            target.dtype
        )
        return carry

    lax.fori_loop(0, rows // step, one, 0)


def pack_kernel(
    shards, cap, rows_here, columns_at, held, rank, z_feat, *refs
):
    sends = refs[:shards]
    place_out = refs[shards]
    place, place_smem, ranks_full, narrow, wide, packed, sems = refs[shards + 1 :]
    here, member, count = lax.axis_index("pts"), lax.axis_index("head"), held[0]
    slots = place.shape[1]
    zone_rows, width = narrow.shape
    if columns_at:
        column = pl.multiple_of(member * width, width)
        source = z_feat.at[:, pl.ds(column, width)]
    else:
        source = z_feat
    feature_copy = pltpu.make_async_copy(source, narrow, sems.at[0])
    feature_copy.start()

    grid_rows = shards * rows_here // LANES
    block = rows_here // LANES
    ranks_full[:, :zone_rows] = rank[...]
    ranks = ranks_full[...]
    occupied = lax.broadcasted_iota(I32, (1, slots), 1) < count
    major = jnp.where(occupied, ranks // LANES, -1)
    minor = ranks % LANES
    hot_major = (lax.broadcasted_iota(I32, (grid_rows, slots), 0) == major).astype(BF)
    hot_minor = (lax.broadcasted_iota(I32, (LANES, slots), 0) == minor).astype(BF)
    members = dot(hot_minor, hot_major, (1, 1)).astype(BF)
    minor_r = lax.broadcasted_iota(I32, (LANES, LANES), 0)
    minor_c = lax.broadcasted_iota(I32, (LANES, LANES), 1)
    below = (minor_c < minor_r).astype(BF)
    major_r = lax.broadcasted_iota(I32, (grid_rows, grid_rows), 0)
    major_c = lax.broadcasted_iota(I32, (grid_rows, grid_rows), 1)
    earlier = ((major_r < major_c) & (major_r // block == major_c // block)).astype(BF)
    row_wise = dot(members, earlier)
    counts = dot(below, members) + dot(jnp.ones((LANES, LANES), BF), row_wise.astype(BF))
    high = jnp.floor(counts * (1.0 / 32.0))
    low = counts - high * 32.0
    spread = dot(high.astype(BF), hot_major) * 32.0 + dot(low.astype(BF), hot_major)
    found = jnp.sum(jnp.where(hot_minor > 0, spread, 0.0), axis=0, keepdims=True)
    target = ranks // rows_here
    place[...] = jnp.where(occupied, target * cap + found.astype(I32), shards * cap)
    to_smem = pltpu.make_async_copy(place, place_smem, sems.at[1])
    to_smem.start()
    to_out = pltpu.make_async_copy(place, place_out, sems.at[2])
    to_out.start()
    feature_copy.wait()
    whole_rows = zone_rows // LANES * LANES
    convert_rows(narrow, 0, wide, 0, whole_rows)
    if whole_rows < zone_rows:
        wide[pl.ds(whole_rows, zone_rows - whole_rows), :] = narrow[
            pl.ds(whole_rows, zone_rows - whole_rows), :
        ].astype(F32)
    to_smem.wait()

    def place_rows(i, carry):
        base = pl.multiple_of(i * ROW_STEP, ROW_STEP)
        for k in range(ROW_STEP):
            packed[pl.ds(place_smem[0, base + k], 1), :] = wide[pl.ds(base + k, 1), :]
        return carry

    lax.fori_loop(0, (count + ROW_STEP - 1) // ROW_STEP, place_rows, 0)
    for k in range(shards):
        at = pl.multiple_of(lax.rem(here + k, shards) * cap, cap)
        convert_rows(packed, at, sends[k], 0, cap)
    to_out.wait()


def pack(held, rank, z_feat, columns_at, width, shards, cap, rows_here):
    zone_rows = z_feat.shape[0]
    slots = round_up(zone_rows, LANES)
    return pl.pallas_call(
        functools.partial(pack_kernel, shards, cap, rows_here, columns_at),
        out_shape=[jax.ShapeDtypeStruct((cap, width), BF)] * shards
        + [jax.ShapeDtypeStruct((1, slots), I32)],
        in_specs=[SMEM, VMEM, ANY],
        out_specs=[VMEM] * shards + [ANY],
        scratch_shapes=[
            pltpu.VMEM((1, slots), I32),
            pltpu.SMEM((1, slots), I32),
            pltpu.VMEM((1, slots), I32),
            pltpu.VMEM((zone_rows, width), BF),
            pltpu.VMEM((slots, width), F32),
            pltpu.VMEM((shards * cap + 8, width), F32),
            pltpu.SemaphoreType.DMA((3,)),
        ],
        name="pack",
    )(held, rank, z_feat)


def move_segment(source, source_at, target, target_at, length):
    def one(i, carry):
        for k in range(4):
            target[pl.ds(target_at + i * 32 + k * 8, 8), :] = source[
                pl.ds(source_at + i * 32 + k * 8, 8), :
            ]
        return carry

    lax.fori_loop(0, (length + 31) // 32, one, 0)


def segment_starts(pieces, patches, shards, cap):
    packed_at, patch_at = {}, {}
    for s in range(shards):
        at = s * cap
        for p in range(patches):
            packed_at[p, s] = at
            at = at + pieces[p, s]
    for p in range(patches):
        at = p * PATCH
        for s in range(shards):
            patch_at[p, s] = at
            at = at + pieces[p, s]
    return packed_at, patch_at


def compact_kernel(shards, patches, group, cap, pieces, *refs):
    blocks = refs[:shards]
    outs = refs[shards : shards + patches]
    wide, patch_rows = refs[shards + patches :]
    here, member = lax.axis_index("pts"), lax.axis_index("head")
    for k in range(shards):
        at = pl.multiple_of(lax.rem(here - k + shards, shards) * cap, cap)
        convert_rows(blocks[k], 0, wide, at, cap)
    packed_at, patch_at = segment_starts(pieces, patches, shards, cap)
    for p in range(patches):
        for s in range(shards):
            move_segment(wide, packed_at[p, s], patch_rows, patch_at[p, s], pieces[p, s])
    own_group = member // group
    for k in range(patches):
        at = pl.multiple_of(lax.rem(own_group + k, patches) * PATCH, PATCH)
        convert_rows(patch_rows, at, outs[k], 0, PATCH)


def compact(pieces, blocks, patches, group):
    shards = len(blocks)
    cap, width = blocks[0].shape
    return pl.pallas_call(
        functools.partial(compact_kernel, shards, patches, group, cap),
        out_shape=[jax.ShapeDtypeStruct((PATCH, width), BF)] * patches,
        in_specs=[SMEM] + [VMEM] * shards,
        out_specs=[VMEM] * patches,
        scratch_shapes=[
            pltpu.VMEM((shards * cap + 64, width), F32),
            pltpu.VMEM((patches * PATCH + 64, width), F32),
        ],
        name="compact",
    )(pieces, *blocks)


def spread_kernel(shards, patches, members, cap, pieces, *refs):
    blocks = refs[:members]
    sends = refs[members : members + shards]
    patch_rows, wide = refs[members + shards :]
    here, member = lax.axis_index("pts"), lax.axis_index("head")
    part_rows = blocks[0].shape[0]
    for k in range(members):
        at = pl.multiple_of(lax.rem(member - k + members, members) * part_rows, part_rows)
        convert_rows(blocks[k], 0, patch_rows, at, part_rows)
    packed_at, patch_at = segment_starts(pieces, patches, shards, cap)
    for s in range(shards):
        for p in range(patches):
            move_segment(patch_rows, patch_at[p, s], wide, packed_at[p, s], pieces[p, s])
    for k in range(shards):
        at = pl.multiple_of(lax.rem(here + k, shards) * cap, cap)
        convert_rows(wide, at, sends[k], 0, cap)


def spread(pieces, blocks, patches, shards, cap):
    members = len(blocks)
    part_rows, width = blocks[0].shape
    return pl.pallas_call(
        functools.partial(spread_kernel, shards, patches, members, cap),
        out_shape=[jax.ShapeDtypeStruct((cap, width), BF)] * shards,
        in_specs=[SMEM] + [VMEM] * members,
        out_specs=[VMEM] * shards,
        scratch_shapes=[
            pltpu.VMEM((patches * PATCH + 64, width), F32),
            pltpu.VMEM((shards * cap + 64, width), F32),
        ],
        name="spread",
    )(pieces, *blocks)


def unpack_kernel(shards, cap, held, place, *refs):
    blocks = refs[:shards]
    out = refs[shards]
    wide, picked = refs[shards + 1 :]
    here, count = lax.axis_index("pts"), held[0]
    zone_rows, width = out.shape
    for k in range(shards):
        at = pl.multiple_of(lax.rem(here - k + shards, shards) * cap, cap)
        convert_rows(blocks[k], 0, wide, at, cap)

    def pick_rows(i, carry):
        base = pl.multiple_of(i * ROW_STEP, ROW_STEP)
        for k in range(ROW_STEP):
            picked[pl.ds(base + k, 1), :] = wide[pl.ds(place[0, base + k], 1), :]
        return carry

    lax.fori_loop(0, (count + ROW_STEP - 1) // ROW_STEP, pick_rows, 0)

    def masked(at, rows):
        slot = at + lax.broadcasted_iota(I32, (rows, width), 0)
        out[pl.ds(at, rows), :] = jnp.where(slot < count, picked[pl.ds(at, rows), :], 0.0).astype(
            BF
        )

    def one(i, carry):
        masked(pl.multiple_of(i * LANES, LANES), LANES)
        return carry

    whole_rows = zone_rows // LANES * LANES
    lax.fori_loop(0, whole_rows // LANES, one, 0)
    if whole_rows < zone_rows:
        masked(whole_rows, zone_rows - whole_rows)


def unpack(held, place, blocks, zone_rows):
    shards = len(blocks)
    cap, width = blocks[0].shape
    slots = place.shape[1]
    return pl.pallas_call(
        functools.partial(unpack_kernel, shards, cap),
        out_shape=jax.ShapeDtypeStruct((zone_rows, width), BF),
        in_specs=[SMEM, SMEM] + [VMEM] * shards,
        out_specs=VMEM,
        scratch_shapes=[
            pltpu.VMEM((shards * cap + 8, width), F32),
            pltpu.VMEM((slots, width), F32),
        ],
        name="unpack",
    )(held, place, *blocks)


def row_stats(parts, width):
    total = jnp.sum(sum(parts[1:], parts[0]), axis=1, keepdims=True)
    squares = jnp.sum(
        sum((x * x for x in parts[1:]), parts[0] * parts[0]), axis=1, keepdims=True
    )
    mean = total / width
    var = squares / width - mean * mean
    return mean, lax.rsqrt(var + 1e-05)


def attend_kernel(blocks, queries, chunk, ids, gain, bias, *refs):
    feats = refs[:blocks]
    weights = refs[blocks : 2 * blocks]
    out, kept = refs[2 * blocks : 2 * blocks + 2]
    normed, keys, values, query, even, odd = refs[2 * blocks + 2 :]
    rows = feats[0].shape[0]
    width = blocks * LANES
    places = [ids[k] for k in range(blocks)]
    first = pl.multiple_of(ids[blocks] * queries, queries)

    def norm(i, carry):
        at = pl.ds(pl.multiple_of(i * 128, 128), 128)
        parts = [feats[b][at, :].astype(F32) for b in range(blocks)]
        mean, scale = row_stats(parts, width)
        for b in range(blocks):
            cols = pl.ds(pl.multiple_of(places[b] * LANES, LANES), LANES)
            normed[at, cols] = (
                (parts[b] - mean) * scale * gain[0:1, cols] + bias[0:1, cols]
            ).astype(BF)
        return carry

    lax.fori_loop(0, rows // 128, norm, 0, unroll=2)
    for b in range(blocks):
        kept[places[b]] = feats[b][pl.ds(first, queries), :]
    lane = lax.broadcasted_iota(I32, (1, LANES), 1)
    score_scale = HEAD_DIM ** (-0.5) * math.log2(math.e)
    for b in range(blocks):
        values[b, LANES:, :] = jnp.ones((HEAD_DIM, rows), BF)
        for i in range(rows // 256):
            at = pl.ds(i * 256, 256)
            keys[b, at, :] = dot(normed[at, :], weights[b][1]).astype(BF)
            values[b, :LANES, i * 256 : (i + 1) * 256] = dot(
                weights[b][2], normed[at, :], (0, 1)
            ).astype(BF)
        for i in range(queries // 256):
            at = pl.ds(pl.multiple_of(first + i * 256, 256), 256)
            query[b, pl.ds(i * 256, 256), :] = (
                dot(normed[at, :], weights[b][0]) * score_scale
            ).astype(BF)
    per_block = LANES // HEAD_DIM
    heads = blocks * per_block

    def score(head, scores):
        b, j = head // per_block, head % per_block
        mask = lane // HEAD_DIM == j
        tops = []
        for i in range(queries // chunk):
            own = jnp.where(mask, query[b, pl.ds(i * chunk, chunk), :], jnp.zeros((), BF))
            found = dot(keys[b], own, (1, 1))
            scores[:, i * chunk : (i + 1) * chunk] = found
            tops.append(jnp.max(found, axis=0, keepdims=True))
        return jnp.concatenate(tops, axis=1)

    def mix(head, scores, top):
        b, j = head // per_block, head % per_block
        at = pl.ds(pl.multiple_of(j * HEAD_DIM, HEAD_DIM), HEAD_DIM)
        own = jnp.concatenate([values[b, at, :], values[b, LANES:, :]], axis=0)
        for i in range(queries // chunk):
            cols = slice(i * chunk, (i + 1) * chunk)
            raised = jnp.exp2(scores[:, cols] - top[:, cols]).astype(BF)
            summed = dot(own, raised)
            out[ids[b], at, cols] = (summed[:HEAD_DIM] / summed[HEAD_DIM:]).astype(BF)

    def pair(i, top):
        next_top = score(2 * i + 1, odd)
        mix(2 * i, even, top)
        top = score(jnp.minimum(2 * i + 2, heads - 1), even)
        mix(2 * i + 1, odd, next_top)
        return top

    lax.fori_loop(0, heads // 2, pair, score(0, even))


def attend(ids, feats, weights, gain, bias, queries):
    blocks = len(feats)
    rows = feats[0].shape[0]
    width = weights[0].shape[1]
    chunk = min(512, queries)
    flops = 4 * queries * rows * LANES * blocks * (LANES // HEAD_DIM)
    return pl.pallas_call(
        functools.partial(attend_kernel, blocks, queries, chunk),
        out_shape=[
            jax.ShapeDtypeStruct((blocks, LANES, queries), BF),
            jax.ShapeDtypeStruct((blocks, queries, LANES), BF),
        ],
        in_specs=[SMEM, VMEM, VMEM] + [VMEM] * (2 * blocks),
        out_specs=[VMEM, VMEM],
        scratch_shapes=[
            pltpu.VMEM((rows, width), BF),
            pltpu.VMEM((blocks, rows, LANES), BF),
            pltpu.VMEM((blocks, LANES + HEAD_DIM, rows), BF),
            pltpu.VMEM((blocks, queries, LANES), BF),
            pltpu.VMEM((rows, queries), F32),
            pltpu.VMEM((rows, queries), F32),
        ],
        cost_estimate=pl.CostEstimate(
            flops=flops, bytes_accessed=4 * rows * width, transcendentals=0
        ),
        name="attend",
    )(ids, gain, bias, *feats, *weights)


def mlp_kernel(blocks, members, sends, chunk, ids, gain, bias, mixed, kept, *refs):
    projs = refs[:blocks]
    ups = refs[blocks : blocks + members]
    downs = refs[blocks + members : blocks + 2 * members]
    vectors = refs[blocks + 2 * members : blocks + 3 * members]
    results = refs[blocks + 3 * members : blocks + 3 * members + sends]
    proj, vector, final = refs[blocks + 3 * members + sends :]
    rows = kept.shape[1]
    width = blocks * LANES
    share = width // members
    spots = [ids[blocks + 1 + k] for k in range(members)]
    for k in range(blocks):
        proj[:, pl.ds(pl.multiple_of(ids[k] * LANES, LANES), LANES)] = projs[k][...]
    for k in range(members):
        vector[spots[k]] = vectors[k][...]
    out_bias = jnp.concatenate([vector[k, :, :share] for k in range(members)], axis=1)
    down_bias = jnp.concatenate([vector[k, :, share : 2 * share] for k in range(members)], axis=1)
    root_half = 0.5 ** 0.5

    def one(i, carry):
        at = pl.ds(pl.multiple_of(i * chunk, chunk), chunk)
        attended = jnp.concatenate([mixed[b, :, at] for b in range(blocks)], axis=0)
        features = jnp.concatenate([kept[b, at, :] for b in range(blocks)], axis=1)
        residual = (features.astype(F32) + dot(attended, proj[...], (0, 0)) + out_bias).astype(BF)
        wide = residual.astype(F32)
        mean, scale = row_stats([wide], width)
        normed = ((wide - mean) * scale * gain[...] + bias[...]).astype(BF)
        total = wide + down_bias
        for k in range(members):
            spot = spots[k]
            before = dot(normed, ups[k][...]) + vector[spot, :, 2 * share :]
            hidden = (0.5 * before * (1.0 + lax.erf(before * root_half))).astype(BF)
            total = total + dot(hidden, downs[k][...])
        for b in range(blocks):
            final[b, at, :] = total[:, b * LANES : (b + 1) * LANES].astype(BF)
        return carry

    lax.fori_loop(0, rows // chunk, one, 0)
    if sends > 1:
        me = ids[blocks + 1]
        for k in range(sends):
            results[k][...] = final[lax.rem(me + k, sends)]
    else:
        results[0][...] = final[...]


def mlp(ids, gain, bias, mixed, kept, projs, ups, downs, vectors):
    blocks, rows, _ = kept.shape
    members = len(ups)
    width = blocks * LANES
    hidden_here = ups[0].shape[1]
    sends = members if members == blocks else 1
    shape = (rows, LANES) if sends > 1 else (blocks, rows, LANES)
    chunk = min(256, rows)
    return pl.pallas_call(
        functools.partial(mlp_kernel, blocks, members, sends, chunk),
        out_shape=[jax.ShapeDtypeStruct(shape, BF)] * sends,
        in_specs=[SMEM, VMEM, VMEM, VMEM, VMEM] + [VMEM] * (blocks + 3 * members),
        out_specs=[VMEM] * sends,
        scratch_shapes=[
            pltpu.VMEM((width, width), BF),
            pltpu.VMEM((members, 1, vectors[0].shape[1]), F32),
            pltpu.VMEM((blocks, rows, LANES), BF),
        ],
        cost_estimate=pl.CostEstimate(
            flops=4 * rows * width * hidden_here * members,
            bytes_accessed=4 * width * hidden_here * members,
            transcendentals=0,
        ),
        name="mlp",
    )(ids, gain, bias, mixed, kept, *projs, *ups, *downs, *vectors)


def shift(array, axis, size, step):
    return lax.ppermute(array, axis, [(i, (i + step) % size) for i in range(size)])


def exchange(blocks, axis, size):
    if size <= 8:
        return [blocks[0]] + [shift(blocks[k], axis, size, k) for k in range(1, size)]
    me = lax.axis_index(axis)
    steps = jnp.arange(size, dtype=I32)
    stacked = jnp.stack(blocks)[(steps - me) % size]
    got = lax.all_to_all(stacked, axis, 0, 0, tiled=True)[(me - steps) % size]
    return [got[k] for k in range(size)]


def gather_members(array, groups, group):
    size = groups * group
    found = []
    for k in range(groups):
        pairs = [(i, (i // group + k) % groups * group + i % group) for i in range(size)]
        moved = array if k == 0 else lax.ppermute(array, "head", pairs)
        for j in range(group):
            pairs = [(i, i // group * group + (i % group + j) % group) for i in range(size)]
            found.append(moved if j == 0 else lax.ppermute(moved, "head", pairs))
    return found


def body(
    z_feat,
    shard_count,
    hilbert_rank,
    z_slot,
    ln1_gain,
    ln1_bias,
    w_qkv,
    w_out,
    b_out,
    ln2_gain,
    ln2_bias,
    w_up,
    b_up,
    w_down,
    b_down,
):
    shards = lax.axis_size("pts")
    members = lax.axis_size("head")
    rows_here = z_slot.shape[0]
    zone_rows, full_width = z_feat.shape
    width = w_out.shape[1]
    patches = rows_here // PATCH
    group = members // patches
    queries = PATCH // group
    blocks = full_width // LANES
    skew_step = rows_here // (2 * shards * (shards - 1))
    cap = round_up(rows_here // shards + 2 * skew_step * (shards - 1), 16)
    member = lax.axis_index("head")

    order = [
        (member // group - k) % patches * group + (member % group - j) % group
        for k in range(patches)
        for j in range(group)
    ]
    spots = jnp.stack(order).astype(I32)
    part = (member % group).astype(I32)[None]

    def natural(found):
        stacked = jnp.stack(found)
        back = jnp.zeros((members,), I32).at[spots].set(jnp.arange(members, dtype=I32))
        stacked = jnp.take(stacked, back, axis=0)
        joined = jnp.concatenate([stacked[i] for i in range(members)], axis=-1)
        return [joined[..., b * LANES : (b + 1) * LANES] for b in range(blocks)]

    qkv_found = gather_members(w_qkv, patches, group)
    out_found = gather_members(w_out, patches, group)
    up_found = gather_members(w_up, patches, group)
    down_found = gather_members(w_down, patches, group)
    vectors = gather_members(
        jnp.concatenate([b_out, b_down, b_up])[None, :], patches, group
    )

    rank = hilbert_rank[None, :]
    if width % LANES == 0:
        z_source = z_feat
    else:
        z_source = lax.dynamic_slice_in_dim(z_feat, member * width, width, 1)
    *sends, place = pack(
        shard_count, rank, z_source, width % LANES == 0, width, shards, cap, rows_here
    )
    source = (z_slot // zone_rows).reshape(patches, PATCH, 1)
    pieces = jnp.sum((source == jnp.arange(shards, dtype=I32)).astype(I32), axis=1)
    arrived = exchange(sends, "pts", shards)
    patch_blocks = compact(pieces, arrived, patches, group)
    feats = []
    for k in range(patches):
        pairs = [(i, (i // group + k) % patches * group + i % group) for i in range(members)]
        moved = patch_blocks[k] if k == 0 else lax.ppermute(patch_blocks[k], "head", pairs)
        for j in range(group):
            pairs = [(i, i // group * group + (i % group + j) % group) for i in range(members)]
            feats.append(moved if j == 0 else lax.ppermute(moved, "head", pairs))

    if width == LANES:
        block_ids = spots
        qkv_blocks, out_blocks = qkv_found, out_found
    else:
        block_ids = jnp.arange(blocks, dtype=I32)
        feats = natural(feats)
        qkv_blocks, out_blocks = natural(qkv_found), natural(out_found)
    ids = jnp.concatenate([block_ids, part, spots])

    mixed, kept = attend(
        ids, feats, qkv_blocks, ln1_gain[None, :], ln1_bias[None, :], queries
    )
    results = mlp(
        ids,
        ln2_gain[None, :],
        ln2_bias[None, :],
        mixed,
        kept,
        out_blocks,
        up_found,
        down_found,
        vectors,
    )
    if width != LANES:
        joined = jnp.concatenate([results[0][b] for b in range(blocks)], axis=1)
        results = [
            lax.dynamic_slice_in_dim(joined, (member + k) % members * width, width, 1)
            for k in range(members)
        ]
    parts = [results[0]] + [shift(results[k], "head", members, k) for k in range(1, members)]
    outgoing = spread(pieces, parts, patches, shards, cap)
    returned = exchange(outgoing, "pts", shards)
    return unpack(shard_count, place, returned, zone_rows)


def solution(mesh):
    placed = (
        P(("tile", "pts"), None),
        P(("tile", "pts")),
        P(("tile", "pts")),
        P(("tile", "pts")),
        P(),
        P(),
        P(None, None, "head"),
        P(None, "head"),
        P("head"),
        P(),
        P(),
        P(None, "head"),
        P("head"),
        P("head", None),
        P("head"),
    )
    return jax.shard_map(
        body, mesh=mesh, in_specs=placed, out_specs=P(("tile", "pts"), "head"), check_vma=False
    )
```

```python
import functools
import math

import jax
import jax.numpy as jnp
from jax import lax
from jax.experimental import pallas as pl
from jax.experimental.pallas import tpu as pltpu
from jax.sharding import PartitionSpec as P

PATCH = 1024
HEAD_DIM = 16
LANES = 128
ROW_STEP = 64
TILE = 512
DIRECT = 8
F32 = jnp.float32
BF = jnp.bfloat16
I32 = jnp.int32
SMEM = pl.BlockSpec(memory_space=pltpu.SMEM)
VMEM = pl.BlockSpec(memory_space=pltpu.VMEM)
ANY = pl.BlockSpec(memory_space=pl.ANY)


def dot(lhs, rhs, dims=(1, 0)):
    return lax.dot_general(
        lhs, rhs, (((dims[0],), (dims[1],)), ((), ())), preferred_element_type=F32
    )


def round_up(value, unit):
    return (value + unit - 1) // unit * unit


def grant(mib):
    return pltpu.CompilerParams(vmem_limit_bytes=mib * 2 ** 20)


def convert_rows(source, source_at, target, target_at, rows):
    step = math.gcd(rows, 128)

    def one(i, carry):
        at = pl.multiple_of(i * step, step)
        target[pl.ds(target_at + at, step), :] = source[pl.ds(source_at + at, step), :].astype(
            target.dtype
        )
        return carry

    lax.fori_loop(0, rows // step, one, 0)


def pack_kernel(
    shards, cap, rows_here, columns_at, held, rank, z_feat, *refs
):
    sends = refs[:shards]
    place_out = refs[shards]
    place, place_smem, ranks_full, narrow, wide, packed, sems = refs[shards + 1 :]
    here, member, count = lax.axis_index("pts"), lax.axis_index("head"), held[0]
    slots = place.shape[1]
    zone_rows, width = narrow.shape
    if columns_at:
        column = pl.multiple_of(member * width, width)
        source = z_feat.at[:, pl.ds(column, width)]
    else:
        source = z_feat
    feature_copy = pltpu.make_async_copy(source, narrow, sems.at[0])
    feature_copy.start()

    grid_rows = shards * rows_here // LANES
    block = rows_here // LANES
    ranks_full[:, :zone_rows] = rank[...]
    ranks = ranks_full[...]
    occupied = lax.broadcasted_iota(I32, (1, slots), 1) < count
    major = jnp.where(occupied, ranks // LANES, -1)
    minor = ranks % LANES
    hot_major = (lax.broadcasted_iota(I32, (grid_rows, slots), 0) == major).astype(BF)
    hot_minor = (lax.broadcasted_iota(I32, (LANES, slots), 0) == minor).astype(BF)
    members = dot(hot_minor, hot_major, (1, 1)).astype(BF)
    minor_r = lax.broadcasted_iota(I32, (LANES, LANES), 0)
    minor_c = lax.broadcasted_iota(I32, (LANES, LANES), 1)
    below = (minor_c < minor_r).astype(BF)
    major_r = lax.broadcasted_iota(I32, (grid_rows, grid_rows), 0)
    major_c = lax.broadcasted_iota(I32, (grid_rows, grid_rows), 1)
    earlier = ((major_r < major_c) & (major_r // block == major_c // block)).astype(BF)
    row_wise = dot(members, earlier)
    counts = dot(below, members) + dot(jnp.ones((LANES, LANES), BF), row_wise.astype(BF))
    high = jnp.floor(counts * (1.0 / 32.0))
    low = counts - high * 32.0
    spread = dot(high.astype(BF), hot_major) * 32.0 + dot(low.astype(BF), hot_major)
    found = jnp.sum(jnp.where(hot_minor > 0, spread, 0.0), axis=0, keepdims=True)
    target = ranks // rows_here
    place[...] = jnp.where(occupied, target * cap + found.astype(I32), shards * cap)
    to_smem = pltpu.make_async_copy(place, place_smem, sems.at[1])
    to_smem.start()
    to_out = pltpu.make_async_copy(place, place_out, sems.at[2])
    to_out.start()
    feature_copy.wait()
    whole_rows = zone_rows // LANES * LANES
    convert_rows(narrow, 0, wide, 0, whole_rows)
    if whole_rows < zone_rows:
        wide[pl.ds(whole_rows, zone_rows - whole_rows), :] = narrow[
            pl.ds(whole_rows, zone_rows - whole_rows), :
        ].astype(F32)
    to_smem.wait()

    def place_rows(i, carry):
        base = pl.multiple_of(i * ROW_STEP, ROW_STEP)
        for k in range(ROW_STEP):
            packed[pl.ds(place_smem[0, base + k], 1), :] = wide[pl.ds(base + k, 1), :]
        return carry

    lax.fori_loop(0, (count + ROW_STEP - 1) // ROW_STEP, place_rows, 0)
    for k in range(shards):
        at = pl.multiple_of(lax.rem(here + k, shards) * cap, cap)
        convert_rows(packed, at, sends[k], 0, cap)
    to_out.wait()


def pack(held, rank, z_feat, columns_at, width, shards, cap, rows_here):
    zone_rows = z_feat.shape[0]
    slots = round_up(zone_rows, LANES)
    return pl.pallas_call(
        functools.partial(pack_kernel, shards, cap, rows_here, columns_at),
        out_shape=[jax.ShapeDtypeStruct((cap, width), BF)] * shards
        + [jax.ShapeDtypeStruct((1, slots), I32)],
        in_specs=[SMEM, VMEM, ANY],
        out_specs=[VMEM] * shards + [ANY],
        scratch_shapes=[
            pltpu.VMEM((1, slots), I32),
            pltpu.SMEM((1, slots), I32),
            pltpu.VMEM((1, slots), I32),
            pltpu.VMEM((zone_rows, width), BF),
            pltpu.VMEM((slots, width), F32),
            pltpu.VMEM((shards * cap + 8, width), F32),
            pltpu.SemaphoreType.DMA((3,)),
        ],
        name="pack",
    )(held, rank, z_feat)


def move_segment(source, source_at, target, target_at, length):
    def one(i, carry):
        for k in range(4):
            target[pl.ds(target_at + i * 32 + k * 8, 8), :] = source[
                pl.ds(source_at + i * 32 + k * 8, 8), :
            ]
        return carry

    lax.fori_loop(0, (length + 31) // 32, one, 0)


def segment_starts(pieces, patches, shards, cap):
    packed_at, patch_at = {}, {}
    for s in range(shards):
        at = s * cap
        for p in range(patches):
            packed_at[p, s] = at
            at = at + pieces[p, s]
    for p in range(patches):
        at = p * PATCH
        for s in range(shards):
            patch_at[p, s] = at
            at = at + pieces[p, s]
    return packed_at, patch_at


def compact_kernel(shards, patches, group, cap, pieces, *refs):
    blocks = refs[:shards]
    outs = refs[shards : shards + patches]
    wide, patch_rows = refs[shards + patches :]
    here, member = lax.axis_index("pts"), lax.axis_index("head")
    for k in range(shards):
        at = pl.multiple_of(lax.rem(here - k + shards, shards) * cap, cap)
        convert_rows(blocks[k], 0, wide, at, cap)
    packed_at, patch_at = segment_starts(pieces, patches, shards, cap)
    for p in range(patches):
        for s in range(shards):
            move_segment(wide, packed_at[p, s], patch_rows, patch_at[p, s], pieces[p, s])
    own_group = member // group
    for k in range(patches):
        at = pl.multiple_of(lax.rem(own_group + k, patches) * PATCH, PATCH)
        convert_rows(patch_rows, at, outs[k], 0, PATCH)


def compact(pieces, blocks, patches, group):
    shards = len(blocks)
    cap, width = blocks[0].shape
    return pl.pallas_call(
        functools.partial(compact_kernel, shards, patches, group, cap),
        out_shape=[jax.ShapeDtypeStruct((PATCH, width), BF)] * patches,
        in_specs=[SMEM] + [VMEM] * shards,
        out_specs=[VMEM] * patches,
        scratch_shapes=[
            pltpu.VMEM((shards * cap + 64, width), F32),
            pltpu.VMEM((patches * PATCH + 64, width), F32),
        ],
        compiler_params=grant(12),
        name="compact",
    )(pieces, *blocks)


def spread_kernel(shards, patches, members, cap, pieces, *refs):
    blocks = refs[:members]
    sends = refs[members : members + shards]
    patch_rows, wide = refs[members + shards :]
    here, member = lax.axis_index("pts"), lax.axis_index("head")
    part_rows = blocks[0].shape[0]
    for k in range(members):
        at = pl.multiple_of(lax.rem(member - k + members, members) * part_rows, part_rows)
        convert_rows(blocks[k], 0, patch_rows, at, part_rows)
    packed_at, patch_at = segment_starts(pieces, patches, shards, cap)
    for s in range(shards):
        for p in range(patches):
            move_segment(patch_rows, patch_at[p, s], wide, packed_at[p, s], pieces[p, s])
    for k in range(shards):
        at = pl.multiple_of(lax.rem(here + k, shards) * cap, cap)
        convert_rows(wide, at, sends[k], 0, cap)


def spread(pieces, blocks, patches, shards, cap):
    members = len(blocks)
    _, width = blocks[0].shape
    return pl.pallas_call(
        functools.partial(spread_kernel, shards, patches, members, cap),
        out_shape=[jax.ShapeDtypeStruct((cap, width), BF)] * shards,
        in_specs=[SMEM] + [VMEM] * members,
        out_specs=[VMEM] * shards,
        scratch_shapes=[
            pltpu.VMEM((patches * PATCH + 64, width), F32),
            pltpu.VMEM((shards * cap + 64, width), F32),
        ],
        compiler_params=grant(12),
        name="spread",
    )(pieces, *blocks)


def unpack_kernel(shards, cap, held, place, *refs):
    blocks = refs[:shards]
    out = refs[shards]
    wide, picked = refs[shards + 1 :]
    here, count = lax.axis_index("pts"), held[0]
    zone_rows, width = out.shape
    for k in range(shards):
        at = pl.multiple_of(lax.rem(here - k + shards, shards) * cap, cap)
        convert_rows(blocks[k], 0, wide, at, cap)

    def pick_rows(i, carry):
        base = pl.multiple_of(i * ROW_STEP, ROW_STEP)
        for k in range(ROW_STEP):
            picked[pl.ds(base + k, 1), :] = wide[pl.ds(place[0, base + k], 1), :]
        return carry

    lax.fori_loop(0, (count + ROW_STEP - 1) // ROW_STEP, pick_rows, 0)

    def masked(at, rows):
        slot = at + lax.broadcasted_iota(I32, (rows, width), 0)
        out[pl.ds(at, rows), :] = jnp.where(slot < count, picked[pl.ds(at, rows), :], 0.0).astype(
            BF
        )

    def one(i, carry):
        masked(pl.multiple_of(i * LANES, LANES), LANES)
        return carry

    whole_rows = zone_rows // LANES * LANES
    lax.fori_loop(0, whole_rows // LANES, one, 0)
    if whole_rows < zone_rows:
        masked(whole_rows, zone_rows - whole_rows)


def unpack(held, place, blocks, zone_rows):
    shards = len(blocks)
    cap, width = blocks[0].shape
    slots = place.shape[1]
    return pl.pallas_call(
        functools.partial(unpack_kernel, shards, cap),
        out_shape=jax.ShapeDtypeStruct((zone_rows, width), BF),
        in_specs=[SMEM, SMEM] + [VMEM] * shards,
        out_specs=VMEM,
        scratch_shapes=[
            pltpu.VMEM((shards * cap + 8, width), F32),
            pltpu.VMEM((slots, width), F32),
        ],
        compiler_params=grant(14),
        name="unpack",
    )(held, place, *blocks)


def row_stats(parts, width):
    total = jnp.sum(sum(parts[1:], parts[0]), axis=1, keepdims=True)
    squares = jnp.sum(
        sum((x * x for x in parts[1:]), parts[0] * parts[0]), axis=1, keepdims=True
    )
    mean = total / width
    var = squares / width - mean * mean
    return mean, lax.rsqrt(var + 1e-05)


def block_places(blocks, patches, group):
    if blocks == patches * group:
        return arrival_order(patches, group)
    return list(range(blocks))


def place_of(places, index):
    found = places[0]
    for k in range(1, len(places)):
        found = jnp.where(index == k, places[k], found)
    return found


def attend_kernel(blocks, patches, group, tile, params, *refs):
    feats = refs[:blocks]
    weights = refs[blocks : 2 * blocks]
    out, kept = refs[2 * blocks : 2 * blocks + 2]
    normed, keys, values, query, even, odd = refs[2 * blocks + 2 :]
    rows = feats[0].shape[0]
    width = blocks * LANES
    queries = query.shape[1]
    places = block_places(blocks, patches, group)
    part = lax.rem(lax.axis_index("head"), group)
    first = pl.multiple_of(part * queries, queries)

    def norm(i, carry):
        at = pl.ds(pl.multiple_of(i * 128, 128), 128)
        parts = [feats[b][at, :].astype(F32) for b in range(blocks)]
        mean, scale = row_stats(parts, width)
        for b in range(blocks):
            cols = pl.ds(pl.multiple_of(places[b] * LANES, LANES), LANES)
            normed[at, cols] = (
                (parts[b] - mean) * scale * params[0:1, cols] + params[1:2, cols]
            ).astype(BF)
        return carry

    lax.fori_loop(0, rows // 128, norm, 0, unroll=2)
    for b in range(blocks):
        kept[places[b]] = feats[b][pl.ds(first, queries), :]
    lane = lax.broadcasted_iota(I32, (1, LANES), 1)
    score_scale = HEAD_DIM ** (-0.5) * math.log2(math.e)
    pair_of = 2 if blocks % 2 == 0 else 1
    for b in range(0, blocks, pair_of):
        both = range(b, b + pair_of)
        q_weight, k_weight, v_weight = (
            jnp.concatenate([weights[c][t] for c in both], axis=1) for t in range(3)
        )
        for i in range(rows // 256):
            at = pl.ds(i * 256, 256)
            found = dot(normed[at, :], k_weight).astype(BF)
            turned = dot(v_weight, normed[at, :], (0, 1)).astype(BF)
            for n, c in enumerate(both):
                keys[c, at, :] = found[:, n * LANES : (n + 1) * LANES]
                values[c, :, i * 256 : (i + 1) * 256] = turned[n * LANES : (n + 1) * LANES]
        for i in range(queries // 256):
            at = pl.ds(pl.multiple_of(first + i * 256, 256), 256)
            found = (dot(normed[at, :], q_weight) * score_scale).astype(BF)
            for n, c in enumerate(both):
                query[c, pl.ds(i * 256, 256), :] = found[:, n * LANES : (n + 1) * LANES]
    per_block = LANES // HEAD_DIM
    heads = blocks * per_block

    def select(head):
        b, j = head // per_block, head % per_block
        return jnp.where(lane // HEAD_DIM == j, query[b], jnp.zeros((), BF))

    def step(head, scores, top, coming, next_scores):
        b, j = head // per_block, head % per_block
        at = pl.ds(pl.multiple_of(j * HEAD_DIM, HEAD_DIM), HEAD_DIM)
        own = select(coming)
        next_keys = coming // per_block
        summed, next_top = None, None
        for i in range(rows // tile):
            part = pl.ds(i * tile, tile)
            found = dot(keys[next_keys, part, :], own, (1, 1))
            next_scores[part, :] = found
            most = jnp.max(found, axis=0, keepdims=True)
            next_top = most if i == 0 else jnp.maximum(next_top, most)
            if top is not None:
                raised = jnp.exp2(scores[part, :] - top).astype(BF)
                lhs = jnp.concatenate(
                    [values[b, at, i * tile : (i + 1) * tile], jnp.ones((HEAD_DIM, tile), BF)],
                    axis=0,
                )
                more = dot(lhs, raised)
                summed = more if i == 0 else summed + more
        if top is not None:
            out[place_of(places, b), at, :] = (summed[:HEAD_DIM] / summed[HEAD_DIM:]).astype(BF)
        return next_top

    def pair(i, top):
        once = jnp.minimum(i, 0) + 1
        next_top = lax.fori_loop(
            0, once, lambda _, most: step(2 * i, even, top, 2 * i + 1, odd), top
        )
        following = jnp.minimum(2 * i + 2, heads - 1)
        return lax.fori_loop(
            0, once, lambda _, most: step(2 * i + 1, odd, next_top, following, even), next_top
        )

    lax.fori_loop(0, heads // 2, pair, step(0, None, None, 0, even))


def attend(feats, weights, params, patches, group):
    blocks = len(feats)
    rows = feats[0].shape[0]
    queries = rows // group
    width = weights[0].shape[1]
    tile = TILE
    flops = 4 * queries * rows * LANES * blocks * (LANES // HEAD_DIM)
    return pl.pallas_call(
        functools.partial(attend_kernel, blocks, patches, group, tile),
        out_shape=[
            jax.ShapeDtypeStruct((blocks, LANES, queries), BF),
            jax.ShapeDtypeStruct((blocks, queries, LANES), BF),
        ],
        in_specs=[VMEM] * (1 + 2 * blocks),
        out_specs=[VMEM, VMEM],
        scratch_shapes=[
            pltpu.VMEM((rows, width), BF),
            pltpu.VMEM((blocks, rows, LANES), BF),
            pltpu.VMEM((blocks, LANES, rows), BF),
            pltpu.VMEM((blocks, queries, LANES), BF),
            pltpu.VMEM((rows, queries), F32),
            pltpu.VMEM((rows, queries), F32),
        ],
        cost_estimate=pl.CostEstimate(
            flops=flops, bytes_accessed=4 * rows * width, transcendentals=0
        ),
        compiler_params=grant(24),
        name="attend",
    )(params, *feats, *weights)


def mlp_kernel(blocks, members, patches, sends, chunk, params, mixed, kept, *refs):
    projs = refs[:blocks]
    ups = refs[blocks : blocks + members]
    downs = refs[blocks + members : blocks + 2 * members]
    vectors = refs[blocks + 2 * members : blocks + 3 * members]
    results = refs[blocks + 3 * members : blocks + 3 * members + sends]
    proj, vector, final = refs[blocks + 3 * members + sends :]
    rows = kept.shape[1]
    width = blocks * LANES
    share = width // members
    group = members // patches
    spots = arrival_order(patches, group)
    places = block_places(blocks, patches, group)
    for k in range(blocks):
        proj[:, pl.ds(pl.multiple_of(places[k] * LANES, LANES), LANES)] = projs[k][...]
    for k in range(members):
        vector[spots[k]] = vectors[k][...]
    out_bias = jnp.concatenate([vector[k, :, :share] for k in range(members)], axis=1)
    down_bias = jnp.concatenate([vector[k, :, share : 2 * share] for k in range(members)], axis=1)
    root_half = 0.5 ** 0.5

    def one(i, carry):
        at = pl.ds(pl.multiple_of(i * chunk, chunk), chunk)
        attended = jnp.concatenate([mixed[b, :, at] for b in range(blocks)], axis=0)
        features = jnp.concatenate([kept[b, at, :] for b in range(blocks)], axis=1)
        residual = (features.astype(F32) + dot(attended, proj[...], (0, 0)) + out_bias).astype(BF)
        wide = residual.astype(F32)
        mean, scale = row_stats([wide], width)
        normed = ((wide - mean) * scale * params[2:3, :] + params[3:4, :]).astype(BF)
        total = wide + down_bias
        for k in range(members):
            spot = spots[k]
            before = dot(normed, ups[k][...]) + vector[spot, :, 2 * share :]
            hidden = (0.5 * before * (1.0 + lax.erf(before * root_half))).astype(BF)
            total = total + dot(hidden, downs[k][...])
        for b in range(blocks):
            final[b, at, :] = total[:, b * LANES : (b + 1) * LANES].astype(BF)
        return carry

    lax.fori_loop(0, rows // chunk, one, 0)
    if sends > 1:
        me = lax.axis_index("head")
        for k in range(sends):
            results[k][...] = final[lax.rem(me + k, sends)]
    else:
        results[0][...] = final[...]


def mlp(patches, params, mixed, kept, projs, ups, downs, vectors):
    blocks, rows, _ = kept.shape
    members = len(ups)
    width = blocks * LANES
    hidden_here = ups[0].shape[1]
    sends = members if members == blocks else 1
    shape = (rows, LANES) if sends > 1 else (blocks, rows, LANES)
    chunk = min(256, rows)
    return pl.pallas_call(
        functools.partial(mlp_kernel, blocks, members, patches, sends, chunk),
        out_shape=[jax.ShapeDtypeStruct(shape, BF)] * sends,
        in_specs=[VMEM, VMEM, VMEM] + [VMEM] * (blocks + 3 * members),
        out_specs=[VMEM] * sends,
        scratch_shapes=[
            pltpu.VMEM((width, width), BF),
            pltpu.VMEM((members, 1, vectors[0].shape[1]), F32),
            pltpu.VMEM((blocks, rows, LANES), BF),
        ],
        cost_estimate=pl.CostEstimate(
            flops=4 * rows * width * hidden_here * members,
            bytes_accessed=4 * width * hidden_here * members,
            transcendentals=0,
        ),
        compiler_params=grant(22),
        name="mlp",
    )(params, mixed, kept, *projs, *ups, *downs, *vectors)


def shift(array, axis, size, step):
    return lax.ppermute(array, axis, [(i, (i + step) % size) for i in range(size)])


def exchange(blocks, axis, size):
    if size <= DIRECT:
        return [blocks[0]] + [shift(blocks[k], axis, size, k) for k in range(1, size)]
    me = lax.axis_index(axis)
    steps = jnp.arange(size, dtype=I32)
    stacked = jnp.stack(blocks)[(steps - me) % size]
    got = lax.all_to_all(stacked, axis, 0, 0, tiled=True)[(me - steps) % size]
    return [got[k] for k in range(size)]


def arrival_order(groups, group):
    member = lax.axis_index("head")
    return [
        lax.rem(member // group - k + groups, groups) * group
        + lax.rem(lax.rem(member, group) - j + group, group)
        for k in range(groups)
        for j in range(group)
    ]


def group_shift(array, groups, group, step):
    size = groups * group
    pairs = [(i, (i // group + step) % groups * group + i % group) for i in range(size)]
    return lax.ppermute(array, "head", pairs)


def member_shift(array, groups, group, step):
    size = groups * group
    pairs = [(i, i // group * group + (i % group + step) % group) for i in range(size)]
    return lax.ppermute(array, "head", pairs)


def gather_members(sources, groups, group):
    found = []
    for k in range(groups):
        moved = sources[k]
        if k > 0:
            moved = group_shift(moved, groups, group, k)
        for j in range(group):
            found.append(moved if j == 0 else member_shift(moved, groups, group, j))
    return found


def body(
    z_feat,
    shard_count,
    hilbert_rank,
    z_slot,
    ln1_gain,
    ln1_bias,
    w_qkv,
    w_out,
    b_out,
    ln2_gain,
    ln2_bias,
    w_up,
    b_up,
    w_down,
    b_down,
):
    shards = lax.axis_size("pts")
    members = lax.axis_size("head")
    rows_here = z_slot.shape[0]
    zone_rows, full_width = z_feat.shape
    width = w_out.shape[1]
    patches = rows_here // PATCH
    group = members // patches
    blocks = full_width // LANES
    skew_step = rows_here // (2 * shards * (shards - 1))
    cap = round_up(rows_here // shards + 2 * skew_step * (shards - 1), 16)
    member = lax.axis_index("head")

    def natural(found):
        spots = jnp.stack(arrival_order(patches, group)).astype(I32)
        stacked = jnp.stack(found)
        back = jnp.zeros((members,), I32).at[spots].set(jnp.arange(members, dtype=I32))
        stacked = jnp.take(stacked, back, axis=0)
        joined = jnp.concatenate([stacked[i] for i in range(members)], axis=-1)
        return [joined[..., b * LANES : (b + 1) * LANES] for b in range(blocks)]

    def everywhere(array):
        return gather_members([array] * patches, patches, group)

    qkv_found = everywhere(w_qkv)
    out_found = everywhere(w_out)
    up_found = everywhere(w_up)
    down_found = everywhere(w_down)
    vector = jnp.concatenate([b_out, b_down, b_up])[None, :]
    vectors = [vector]
    for step in range(1, members):
        k, j = step // group, step % group
        pairs = [
            (i, (i // group + k) % patches * group + (i % group + j) % group)
            for i in range(members)
        ]
        vectors.append(lax.ppermute(vector, "head", pairs))

    rank = hilbert_rank[None, :]
    if width % LANES == 0:
        z_source = z_feat
    else:
        z_source = lax.dynamic_slice_in_dim(z_feat, member * width, width, 1)
    *sends, place = pack(
        shard_count, rank, z_source, width % LANES == 0, width, shards, cap, rows_here
    )
    source = (z_slot // zone_rows).reshape(patches, PATCH, 1)
    pieces = jnp.sum((source == jnp.arange(shards, dtype=I32)).astype(I32), axis=1)
    params = jnp.stack([ln1_gain, ln1_bias, ln2_gain, ln2_bias])
    pieces, params = lax.optimization_barrier((pieces, params))
    arrived = exchange(sends, "pts", shards)
    patch_blocks = compact(pieces, arrived, patches, group)
    feats = gather_members(patch_blocks, patches, group)

    if width == LANES:
        qkv_blocks, out_blocks = qkv_found, out_found
    else:
        feats = natural(feats)
        qkv_blocks, out_blocks = natural(qkv_found), natural(out_found)

    mixed, kept = attend(feats, qkv_blocks, params, patches, group)
    results = mlp(
        patches,
        params,
        mixed,
        kept,
        out_blocks,
        up_found,
        down_found,
        vectors,
    )
    if width != LANES:
        joined = jnp.concatenate([results[0][b] for b in range(blocks)], axis=1)
        results = [
            lax.dynamic_slice_in_dim(joined, (member + k) % members * width, width, 1)
            for k in range(members)
        ]
    parts = [results[0]] + [shift(results[k], "head", members, k) for k in range(1, members)]
    outgoing = spread(pieces, parts, patches, shards, cap)
    returned = exchange(outgoing, "pts", shards)
    return unpack(shard_count, place, returned, zone_rows)


def solution(mesh):
    placed = (
        P(("tile", "pts"), None),
        P(("tile", "pts")),
        P(("tile", "pts")),
        P(("tile", "pts")),
        P(),
        P(),
        P(None, None, "head"),
        P(None, "head"),
        P("head"),
        P(),
        P(),
        P(None, "head"),
        P("head"),
        P("head", None),
        P("head"),
    )

    return jax.shard_map(
        body, mesh=mesh, in_specs=placed, out_specs=P(("tile", "pts"), "head"), check_vma=False
    )
```

```python
import functools
import math

import jax
import jax.numpy as jnp
from jax import lax
from jax.experimental import pallas as pl
from jax.experimental.pallas import tpu as pltpu
from jax.sharding import PartitionSpec as P

PATCH = 1024
HEAD_DIM = 16
LANES = 128
ROW_STEP = 64
TILE = 512
DIRECT = 8
F32 = jnp.float32
BF = jnp.bfloat16
I32 = jnp.int32
SMEM = pl.BlockSpec(memory_space=pltpu.SMEM)
VMEM = pl.BlockSpec(memory_space=pltpu.VMEM)
ANY = pl.BlockSpec(memory_space=pl.ANY)


def dot(lhs, rhs, dims=(1, 0)):
    return lax.dot_general(
        lhs, rhs, (((dims[0],), (dims[1],)), ((), ())), preferred_element_type=F32
    )


def exact_dot(values, choice):
    high = jnp.floor(values * (1.0 / LANES))
    low = values - high * LANES
    return dot(high.astype(BF), choice) * LANES + dot(low.astype(BF), choice)


def round_up(value, unit):
    return (value + unit - 1) // unit * unit


def grant(mib):
    return pltpu.CompilerParams(vmem_limit_bytes=mib * 2 ** 20)


def convert_rows(source, source_at, target, target_at, rows):
    step = math.gcd(rows, 128)

    def one(i, carry):
        at = pl.multiple_of(i * step, step)
        target[pl.ds(target_at + at, step), :] = source[pl.ds(source_at + at, step), :].astype(
            target.dtype
        )
        return carry

    lax.fori_loop(0, rows // step, one, 0)


def pack_kernel(
    shards, cap, rows_here, columns_at, held, rank, z_feat, *refs
):
    sends = refs[:shards]
    place_out = refs[shards]
    place, place_smem, ranks_full, narrow, wide, packed, sems = refs[shards + 1 :]
    here, member, count = lax.axis_index("pts"), lax.axis_index("head"), held[0]
    slots = place.shape[1]
    zone_rows, width = narrow.shape
    if columns_at:
        column = pl.multiple_of(member * width, width)
        source = z_feat.at[:, pl.ds(column, width)]
    else:
        source = z_feat
    feature_copy = pltpu.make_async_copy(source, narrow, sems.at[0])
    feature_copy.start()

    grid_rows = shards * rows_here // LANES
    block = rows_here // LANES
    ranks_full[:, :zone_rows] = rank[...]
    ranks = ranks_full[...]
    occupied = lax.broadcasted_iota(I32, (1, slots), 1) < count
    major = jnp.where(occupied, ranks // LANES, -1)
    minor = ranks % LANES
    hot_major = (lax.broadcasted_iota(I32, (grid_rows, slots), 0) == major).astype(BF)
    hot_minor = (lax.broadcasted_iota(I32, (LANES, slots), 0) == minor).astype(BF)
    members = dot(hot_minor, hot_major, (1, 1)).astype(BF)
    minor_r = lax.broadcasted_iota(I32, (LANES, LANES), 0)
    minor_c = lax.broadcasted_iota(I32, (LANES, LANES), 1)
    below = (minor_c < minor_r).astype(BF)
    ones = jnp.ones((LANES, LANES), BF)
    major_r = lax.broadcasted_iota(I32, (grid_rows, grid_rows), 0)
    major_c = lax.broadcasted_iota(I32, (grid_rows, grid_rows), 1)
    group = PATCH // LANES
    same_group = major_r // group == major_c // group
    earlier_row = (same_group & (major_r < major_c)).astype(BF)
    earlier_group = (
        (major_r // block == major_c // block)
        & (major_r // group < major_c // group)
        & (major_r % group == 0)
    ).astype(BF)
    before = dot(below, members) + dot(ones, dot(members, earlier_row).astype(BF))
    total = dot(ones, dot(members, same_group.astype(BF)).astype(BF))
    first_half = jnp.floor(total * 0.5)
    second_half = total - first_half
    first_base = exact_dot(first_half, earlier_group)
    second_base = exact_dot(second_half, earlier_group)
    target = lax.broadcasted_iota(I32, (LANES, grid_rows), 1) // block * cap
    spot = target.astype(F32) + jnp.where(
        before < first_half,
        first_base + before,
        second_base + before - first_half + cap // 2,
    )
    spread_out = exact_dot(spot, hot_major)
    found = jnp.sum(jnp.where(hot_minor > 0, spread_out, 0.0), axis=0, keepdims=True)
    place[...] = jnp.where(occupied, found.astype(I32), shards * cap)
    to_smem = pltpu.make_async_copy(place, place_smem, sems.at[1])
    to_smem.start()
    to_out = pltpu.make_async_copy(place, place_out, sems.at[2])
    to_out.start()
    feature_copy.wait()
    whole_rows = zone_rows // LANES * LANES
    convert_rows(narrow, 0, wide, 0, whole_rows)
    if whole_rows < zone_rows:
        wide[pl.ds(whole_rows, zone_rows - whole_rows), :] = narrow[
            pl.ds(whole_rows, zone_rows - whole_rows), :
        ].astype(F32)
    to_smem.wait()

    def place_rows(i, carry):
        base = pl.multiple_of(i * ROW_STEP, ROW_STEP)
        for k in range(ROW_STEP):
            packed[pl.ds(place_smem[0, base + k], 1), :] = wide[pl.ds(base + k, 1), :]
        return carry

    lax.fori_loop(0, (count + ROW_STEP - 1) // ROW_STEP, place_rows, 0)
    for k in range(shards):
        at = pl.multiple_of(lax.rem(here + k, shards) * cap, cap)
        convert_rows(packed, at, sends[k], 0, cap)
    to_out.wait()


def pack(held, rank, z_feat, columns_at, width, shards, cap, rows_here):
    zone_rows = z_feat.shape[0]
    slots = round_up(zone_rows, LANES)
    return pl.pallas_call(
        functools.partial(pack_kernel, shards, cap, rows_here, columns_at),
        out_shape=[jax.ShapeDtypeStruct((cap, width), BF)] * shards
        + [jax.ShapeDtypeStruct((1, slots), I32)],
        in_specs=[SMEM, VMEM, ANY],
        out_specs=[VMEM] * shards + [ANY],
        scratch_shapes=[
            pltpu.VMEM((1, slots), I32),
            pltpu.SMEM((1, slots), I32),
            pltpu.VMEM((1, slots), I32),
            pltpu.VMEM((zone_rows, width), BF),
            pltpu.VMEM((slots, width), F32),
            pltpu.VMEM((shards * cap + 8, width), F32),
            pltpu.SemaphoreType.DMA((3,)),
        ],
        name="pack",
    )(held, rank, z_feat)


def move_segment(source, source_at, target, target_at, length):
    def one(i, carry):
        for k in range(4):
            target[pl.ds(target_at + i * 32 + k * 8, 8), :] = source[
                pl.ds(source_at + i * 32 + k * 8, 8), :
            ]
        return carry

    lax.fori_loop(0, (length + 31) // 32, one, 0)


def segment_table(pieces, patches, shards, cap):
    packed_at, patch_at, lengths = {}, {}, {}
    for s in range(shards):
        ends = [s * cap, s * cap + cap // 2]
        for p in range(patches):
            count = pieces[p, s]
            lengths[0, p, s] = lax.shift_right_logical(count, 1)
            lengths[1, p, s] = count - lengths[0, p, s]
            for half in range(2):
                packed_at[half, p, s] = ends[half]
                ends[half] = ends[half] + lengths[half, p, s]
    for p in range(patches):
        at = p * PATCH
        for half in range(2):
            for s in range(shards):
                patch_at[half, p, s] = at
                at = at + lengths[half, p, s]
    return packed_at, patch_at, lengths


def compact_kernel(shards, patches, group, cap, pieces, *refs):
    blocks = refs[:shards]
    outs = refs[shards : shards + patches]
    wide, patch_rows = refs[shards + patches :]
    here, member = lax.axis_index("pts"), lax.axis_index("head")
    for k in range(shards):
        at = pl.multiple_of(lax.rem(here - k + shards, shards) * cap, cap)
        convert_rows(blocks[k], 0, wide, at, cap)
    packed_at, patch_at, lengths = segment_table(pieces, patches, shards, cap)
    for p in range(patches):
        for half in range(2):
            for s in range(shards):
                key = half, p, s
                move_segment(wide, packed_at[key], patch_rows, patch_at[key], lengths[key])
    own_group = member // group
    for k in range(patches):
        at = pl.multiple_of(lax.rem(own_group + k, patches) * PATCH, PATCH)
        convert_rows(patch_rows, at, outs[k], 0, PATCH)


def compact(pieces, blocks, patches, group):
    shards = len(blocks)
    cap, width = blocks[0].shape
    return pl.pallas_call(
        functools.partial(compact_kernel, shards, patches, group, cap),
        out_shape=[jax.ShapeDtypeStruct((PATCH, width), BF)] * patches,
        in_specs=[SMEM] + [VMEM] * shards,
        out_specs=[VMEM] * patches,
        scratch_shapes=[
            pltpu.VMEM((shards * cap + 64, width), F32),
            pltpu.VMEM((patches * PATCH + 64, width), F32),
        ],
        compiler_params=grant(12),
        name="compact",
    )(pieces, *blocks)


def spread_kernel(shards, patches, members, cap, half, pieces, *refs):
    given = members * (half + 1)
    blocks = refs[:given]
    sends = refs[given : given + shards]
    patch_rows, wide = refs[given + shards :]
    here, member = lax.axis_index("pts"), lax.axis_index("head")
    group = members // patches
    part_rows = blocks[0].shape[0]
    for phase in range(half + 1):
        for k in range(members):
            source = lax.rem(member - k + members, members)
            at = source // group * PATCH + phase * (PATCH // 2)
            at = pl.multiple_of(at + lax.rem(source, group) * part_rows, part_rows)
            convert_rows(blocks[phase * members + k], 0, patch_rows, at, part_rows)
    packed_at, patch_at, lengths = segment_table(pieces, patches, shards, cap)
    size = cap // 2
    for s in range(shards):
        for p in range(patches):
            key = half, p, s
            move_segment(
                patch_rows,
                patch_at[key],
                wide,
                packed_at[key] - s * cap - half * size + s * size,
                lengths[key],
            )
    for k in range(shards):
        at = pl.multiple_of(lax.rem(here + k, shards) * size, size)
        convert_rows(wide, at, sends[k], 0, size)


def spread(pieces, blocks, patches, members, shards, cap, half):
    width = blocks[0].shape[1]
    return pl.pallas_call(
        functools.partial(spread_kernel, shards, patches, members, cap, half),
        out_shape=[jax.ShapeDtypeStruct((cap // 2, width), BF)] * shards,
        in_specs=[SMEM] + [VMEM] * len(blocks),
        out_specs=[VMEM] * shards,
        scratch_shapes=[
            pltpu.VMEM((patches * PATCH + 64, width), F32),
            pltpu.VMEM((shards * cap // 2 + 64, width), F32),
        ],
        compiler_params=grant(12),
        name="spread",
    )(pieces, *blocks)


def unpack_kernel(shards, cap, held, place, *refs):
    blocks = refs[: 2 * shards]
    out = refs[2 * shards]
    wide, picked = refs[2 * shards + 1 :]
    here, count = lax.axis_index("pts"), held[0]
    zone_rows, width = out.shape
    size = cap // 2
    for half in range(2):
        for k in range(shards):
            at = lax.rem(here - k + shards, shards) * cap + half * size
            convert_rows(blocks[half * shards + k], 0, wide, pl.multiple_of(at, size), size)

    def pick_rows(i, carry):
        base = pl.multiple_of(i * ROW_STEP, ROW_STEP)
        for k in range(ROW_STEP):
            picked[pl.ds(base + k, 1), :] = wide[pl.ds(place[0, base + k], 1), :]
        return carry

    lax.fori_loop(0, (count + ROW_STEP - 1) // ROW_STEP, pick_rows, 0)

    def masked(at, rows):
        slot = at + lax.broadcasted_iota(I32, (rows, width), 0)
        out[pl.ds(at, rows), :] = jnp.where(slot < count, picked[pl.ds(at, rows), :], 0.0).astype(
            BF
        )

    def one(i, carry):
        masked(pl.multiple_of(i * LANES, LANES), LANES)
        return carry

    whole_rows = zone_rows // LANES * LANES
    lax.fori_loop(0, whole_rows // LANES, one, 0)
    if whole_rows < zone_rows:
        masked(whole_rows, zone_rows - whole_rows)


def unpack(held, place, blocks, zone_rows):
    shards = len(blocks) // 2
    size, width = blocks[0].shape
    cap = 2 * size
    slots = place.shape[1]
    return pl.pallas_call(
        functools.partial(unpack_kernel, shards, cap),
        out_shape=jax.ShapeDtypeStruct((zone_rows, width), BF),
        in_specs=[SMEM, SMEM] + [VMEM] * (2 * shards),
        out_specs=VMEM,
        scratch_shapes=[
            pltpu.VMEM((shards * cap + 8, width), F32),
            pltpu.VMEM((slots, width), F32),
        ],
        compiler_params=grant(14),
        name="unpack",
    )(held, place, *blocks)


def row_stats(parts, width):
    total = jnp.sum(sum(parts[1:], parts[0]), axis=1, keepdims=True)
    squares = jnp.sum(
        sum((x * x for x in parts[1:]), parts[0] * parts[0]), axis=1, keepdims=True
    )
    mean = total / width
    var = squares / width - mean * mean
    return mean, lax.rsqrt(var + 1e-05)


def block_places(blocks, patches, group):
    if blocks == patches * group:
        return arrival_order(patches, group)
    return list(range(blocks))


def project_kernel(blocks, patches, group, params, *refs):
    feats = refs[:blocks]
    weights = refs[blocks : 2 * blocks]
    keys, values, query, kept, normed = refs[2 * blocks :]
    rows = feats[0].shape[0]
    width = blocks * LANES
    queries = query.shape[1] // 2
    places = block_places(blocks, patches, group)
    part = lax.rem(lax.axis_index("head"), group)

    def norm(i, carry):
        at = pl.ds(pl.multiple_of(i * 128, 128), 128)
        parts = [feats[b][at, :].astype(F32) for b in range(blocks)]
        mean, scale = row_stats(parts, width)
        for b in range(blocks):
            cols = pl.ds(pl.multiple_of(places[b] * LANES, LANES), LANES)
            normed[at, cols] = (
                (parts[b] - mean) * scale * params[0:1, cols] + params[1:2, cols]
            ).astype(BF)
        return carry

    lax.fori_loop(0, rows // 128, norm, 0, unroll=2)
    starts = [
        pl.multiple_of(part * queries + half * (rows // 2), queries) for half in range(2)
    ]
    for b in range(blocks):
        for half in range(2):
            kept[places[b], pl.ds(half * queries, queries), :] = feats[b][
                pl.ds(starts[half], queries), :
            ]
    score_scale = HEAD_DIM ** (-0.5) * math.log2(math.e)
    pair_of = 2 if blocks % 2 == 0 else 1
    for b in range(0, blocks, pair_of):
        both = range(b, b + pair_of)
        q_weight, k_weight, v_weight = (
            jnp.concatenate([weights[c][t] for c in both], axis=1) for t in range(3)
        )
        for i in range(rows // 256):
            at = pl.ds(i * 256, 256)
            found = dot(normed[at, :], k_weight).astype(BF)
            turned = dot(v_weight, normed[at, :], (0, 1)).astype(BF)
            for n, c in enumerate(both):
                keys[c, at, :] = found[:, n * LANES : (n + 1) * LANES]
                values[c, :, i * 256 : (i + 1) * 256] = turned[n * LANES : (n + 1) * LANES]
        for half in range(2):
            at = pl.ds(starts[half], queries)
            found = (dot(normed[at, :], q_weight) * score_scale).astype(BF)
            for n, c in enumerate(both):
                query[c, pl.ds(half * queries, queries), :] = found[
                    :, n * LANES : (n + 1) * LANES
                ]


def project(feats, weights, params, patches, group):
    blocks = len(feats)
    rows = feats[0].shape[0]
    width = weights[0].shape[1]
    own = jax.ShapeDtypeStruct((blocks, rows // group, LANES), BF)
    return pl.pallas_call(
        functools.partial(project_kernel, blocks, patches, group),
        out_shape=[
            jax.ShapeDtypeStruct((blocks, rows, LANES), BF),
            jax.ShapeDtypeStruct((blocks, LANES, rows), BF),
            own,
            own,
        ],
        in_specs=[VMEM] * (1 + 2 * blocks),
        out_specs=[VMEM] * 4,
        scratch_shapes=[pltpu.VMEM((rows, width), BF)],
        compiler_params=grant(14),
        cost_estimate=pl.CostEstimate(
            flops=6 * rows * width * width, bytes_accessed=8 * rows * width, transcendentals=0
        ),
        name="project",
    )(params, *feats, *weights)


def attend_kernel(low, high, half, tile, keys, values, query, out, even, odd):
    rows = keys.shape[1]
    queries = query.shape[1] // 2
    lane = lax.broadcasted_iota(I32, (1, LANES), 1)
    per_block = LANES // HEAD_DIM // 2
    steps = (high - low) * per_block

    def select(index):
        b, j = low + index // per_block, index % per_block
        own = query[b, pl.ds(half * queries, queries), :]
        zero = jnp.zeros((), BF)
        return jnp.concatenate(
            [jnp.where(lane // HEAD_DIM == 2 * j + n, own, zero) for n in range(2)], axis=0
        )

    def step(index, scores, top, coming, next_scores):
        b, j = index // per_block, index % per_block
        at = [
            pl.ds(pl.multiple_of((2 * j + n) * HEAD_DIM, HEAD_DIM), HEAD_DIM) for n in range(2)
        ]
        own = select(coming)
        next_keys = low + coming // per_block
        summed, next_top = [None, None], None
        for i in range(rows // tile):
            part = pl.ds(i * tile, tile)
            found = dot(keys[next_keys, part, :], own, (1, 1))
            next_scores[part, :] = found
            most = jnp.max(found, axis=0, keepdims=True)
            next_top = most if i == 0 else jnp.maximum(next_top, most)
            if top is not None:
                raised = jnp.exp2(scores[part, :] - top).astype(BF)
                for n in range(2):
                    lhs = jnp.concatenate(
                        [
                            values[low + b, at[n], i * tile : (i + 1) * tile],
                            jnp.ones((HEAD_DIM, tile), BF),
                        ],
                        axis=0,
                    )
                    more = dot(lhs, raised[:, n * queries : (n + 1) * queries])
                    summed[n] = more if i == 0 else summed[n] + more
        if top is not None:
            for n in range(2):
                out[b, at[n], :] = (summed[n][:HEAD_DIM] / summed[n][HEAD_DIM:]).astype(BF)
        return next_top

    def pair(i, top):
        once = jnp.minimum(i, 0) + 1
        next_top = lax.fori_loop(
            0, once, lambda _, most: step(2 * i, even, top, 2 * i + 1, odd), top
        )
        following = jnp.minimum(2 * i + 2, steps - 1)
        return lax.fori_loop(
            0, once, lambda _, most: step(2 * i + 1, odd, next_top, following, even), next_top
        )

    lax.fori_loop(0, steps // 2, pair, step(0, None, None, 0, even))


def attend(keys, values, query, low, high, half):
    rows = keys.shape[1]
    queries = query.shape[1] // 2
    return pl.pallas_call(
        functools.partial(attend_kernel, low, high, half, min(TILE, rows)),
        out_shape=jax.ShapeDtypeStruct((high - low, LANES, queries), BF),
        in_specs=[VMEM] * 3,
        out_specs=VMEM,
        scratch_shapes=[pltpu.VMEM((rows, 2 * queries), F32)] * 2,
        compiler_params=grant(14),
        cost_estimate=pl.CostEstimate(
            flops=4 * queries * rows * LANES * (high - low) * (LANES // HEAD_DIM),
            bytes_accessed=4 * rows * LANES * (high - low),
            transcendentals=0,
        ),
        name="attend",
    )(keys, values, query)


def mlp_kernel(blocks, members, patches, sends, chunk, half, pieces_of, params, kept, *refs):
    mixed = refs[:pieces_of]
    refs = refs[pieces_of:]
    projs = refs[:blocks]
    ups = refs[blocks : blocks + members]
    downs = refs[blocks + members : blocks + 2 * members]
    vectors = refs[blocks + 2 * members : blocks + 3 * members]
    results = refs[blocks + 3 * members : blocks + 3 * members + sends]
    proj, vector, final = refs[blocks + 3 * members + sends :]
    rows = kept.shape[1] // 2
    width = blocks * LANES
    share = width // members
    group = members // patches
    spots = arrival_order(patches, group)
    places = block_places(blocks, patches, group)
    for k in range(blocks):
        cols = pl.ds(pl.multiple_of(places[k] * LANES, LANES), LANES)
        for r in range(blocks):
            from_rows = pl.ds(pl.multiple_of(places[r] * LANES, LANES), LANES)
            proj[r * LANES : (r + 1) * LANES, cols] = projs[k][from_rows, :]
    for k in range(members):
        vector[spots[k]] = vectors[k][...]
    out_bias = jnp.concatenate([vector[k, :, :share] for k in range(members)], axis=1)
    down_bias = jnp.concatenate([vector[k, :, share : 2 * share] for k in range(members)], axis=1)
    root_half = 0.5 ** 0.5

    def one(i, carry):
        at = pl.ds(pl.multiple_of(i * chunk, chunk), chunk)
        attended = jnp.concatenate(
            [m[b, :, at] for m in mixed for b in range(m.shape[0])], axis=0
        )
        own = pl.ds(pl.multiple_of(half * rows + i * chunk, chunk), chunk)
        features = jnp.concatenate([kept[b, own, :] for b in range(blocks)], axis=1)
        residual = (features.astype(F32) + dot(attended, proj[...], (0, 0)) + out_bias).astype(BF)
        wide = residual.astype(F32)
        mean, scale = row_stats([wide], width)
        normed = ((wide - mean) * scale * params[2:3, :] + params[3:4, :]).astype(BF)
        total = wide + down_bias
        for k in range(members):
            spot = spots[k]
            before = dot(normed, ups[k][...]) + vector[spot, :, 2 * share :]
            hidden = (0.5 * before * (1.0 + lax.erf(before * root_half))).astype(BF)
            total = total + dot(hidden, downs[k][...])
        for b in range(blocks):
            final[b, at, :] = total[:, b * LANES : (b + 1) * LANES].astype(BF)
        return carry

    lax.fori_loop(0, rows // chunk, one, 0)
    if sends > 1:
        me = lax.axis_index("head")
        for k in range(sends):
            results[k][...] = final[lax.rem(me + k, sends)]
    else:
        results[0][...] = final[...]


def mlp(patches, half, params, mixed, kept, projs, ups, downs, vectors):
    blocks, rows = kept.shape[0], kept.shape[1] // 2
    members = len(ups)
    width = blocks * LANES
    hidden_here = ups[0].shape[1]
    sends = members if members == blocks else 1
    shape = (rows, LANES) if sends > 1 else (blocks, rows, LANES)
    chunk = min(256, rows)
    return pl.pallas_call(
        functools.partial(
            mlp_kernel, blocks, members, patches, sends, chunk, half, len(mixed)
        ),
        out_shape=[jax.ShapeDtypeStruct(shape, BF)] * sends,
        in_specs=[VMEM] * (2 + len(mixed) + blocks + 3 * members),
        out_specs=[VMEM] * sends,
        scratch_shapes=[
            pltpu.VMEM((width, width), BF),
            pltpu.VMEM((members, 1, vectors[0].shape[1]), F32),
            pltpu.VMEM((blocks, rows, LANES), BF),
        ],
        cost_estimate=pl.CostEstimate(
            flops=4 * rows * width * hidden_here * members,
            bytes_accessed=4 * width * hidden_here * members,
            transcendentals=0,
        ),
        compiler_params=grant(22),
        name="mlp",
    )(params, kept, *mixed, *projs, *ups, *downs, *vectors)


def shift(array, axis, size, step):
    return lax.ppermute(array, axis, [(i, (i + step) % size) for i in range(size)])


def exchange(blocks, axis, size):
    if size <= DIRECT:
        return [blocks[0]] + [shift(blocks[k], axis, size, k) for k in range(1, size)]
    me = lax.axis_index(axis)
    steps = jnp.arange(size, dtype=I32)
    stacked = jnp.stack(blocks)[(steps - me) % size]
    got = lax.all_to_all(stacked, axis, 0, 0, tiled=True)[(me - steps) % size]
    return [got[k] for k in range(size)]


def arrival_order(groups, group):
    member = lax.axis_index("head")
    return [
        lax.rem(member // group - k + groups, groups) * group
        + lax.rem(lax.rem(member, group) - j + group, group)
        for k in range(groups)
        for j in range(group)
    ]


def group_shift(array, groups, group, step):
    size = groups * group
    pairs = [(i, (i // group + step) % groups * group + i % group) for i in range(size)]
    return lax.ppermute(array, "head", pairs)


def member_shift(array, groups, group, step):
    size = groups * group
    pairs = [(i, i // group * group + (i % group + step) % group) for i in range(size)]
    return lax.ppermute(array, "head", pairs)


def gather_members(sources, groups, group):
    found = []
    for k in range(groups):
        moved = sources[k]
        if k > 0:
            moved = group_shift(moved, groups, group, k)
        for j in range(group):
            found.append(moved if j == 0 else member_shift(moved, groups, group, j))
    return found


def body(
    z_feat,
    shard_count,
    hilbert_rank,
    z_slot,
    ln1_gain,
    ln1_bias,
    w_qkv,
    w_out,
    b_out,
    ln2_gain,
    ln2_bias,
    w_up,
    b_up,
    w_down,
    b_down,
):
    shards = lax.axis_size("pts")
    members = lax.axis_size("head")
    rows_here = z_slot.shape[0]
    zone_rows, full_width = z_feat.shape
    width = w_out.shape[1]
    patches = rows_here // PATCH
    group = members // patches
    blocks = full_width // LANES
    skew_step = rows_here // (2 * shards * (shards - 1))
    cap = round_up(rows_here // shards + 2 * skew_step * (shards - 1), 32)
    member = lax.axis_index("head")

    def natural(found):
        spots = jnp.stack(arrival_order(patches, group)).astype(I32)
        stacked = jnp.stack(found)
        back = jnp.zeros((members,), I32).at[spots].set(jnp.arange(members, dtype=I32))
        stacked = jnp.take(stacked, back, axis=0)
        joined = jnp.concatenate([stacked[i] for i in range(members)], axis=-1)
        return [joined[..., b * LANES : (b + 1) * LANES] for b in range(blocks)]

    def everywhere(array):
        return gather_members([array] * patches, patches, group)

    qkv_found = everywhere(w_qkv)
    out_found = everywhere(w_out)
    up_found = everywhere(w_up)
    down_found = everywhere(w_down)
    vector = jnp.concatenate([b_out, b_down, b_up])[None, :]
    vectors = [vector]
    for step in range(1, members):
        k, j = step // group, step % group
        pairs = [
            (i, (i // group + k) % patches * group + (i % group + j) % group)
            for i in range(members)
        ]
        vectors.append(lax.ppermute(vector, "head", pairs))

    rank = hilbert_rank[None, :]
    if width % LANES == 0:
        z_source = z_feat
    else:
        z_source = lax.dynamic_slice_in_dim(z_feat, member * width, width, 1)
    *sends, place = pack(
        shard_count, rank, z_source, width % LANES == 0, width, shards, cap, rows_here
    )
    source = (z_slot // zone_rows).reshape(patches, PATCH, 1)
    pieces = jnp.sum((source == jnp.arange(shards, dtype=I32)).astype(I32), axis=1)
    params = jnp.stack([ln1_gain, ln1_bias, ln2_gain, ln2_bias])
    pieces, params = lax.optimization_barrier((pieces, params))
    arrived = exchange(sends, "pts", shards)
    patch_blocks = compact(pieces, arrived, patches, group)
    feats = gather_members(patch_blocks, patches, group)

    if width == LANES:
        qkv_blocks, out_blocks = qkv_found, out_found
    else:
        feats = natural(feats)
        qkv_blocks, out_blocks = natural(qkv_found), natural(out_found)

    keys, values, query, kept = project(feats, qkv_blocks, params, patches, group)

    def columns_back(half, mixed):
        results = mlp(
            patches, half, params, mixed, kept, out_blocks, up_found, down_found, vectors
        )
        if width != LANES:
            joined = jnp.concatenate([results[0][b] for b in range(blocks)], axis=1)
            results = [
                lax.dynamic_slice_in_dim(joined, (member + k) % members * width, width, 1)
                for k in range(members)
            ]
        return [results[0]] + [shift(results[k], "head", members, k) for k in range(1, members)]

    mixed = attend(keys, values, query, 0, blocks, 0)
    parts = columns_back(0, [mixed])
    middle = blocks // 2
    mixed_low = attend(keys, values, query, 0, middle, 1)
    outgoing = spread(pieces, parts, patches, members, shards, cap, 0)
    returned = exchange(outgoing, "pts", shards)
    mixed_high = attend(keys, values, query, middle, blocks, 1)
    parts = parts + columns_back(1, [mixed_low, mixed_high])
    outgoing = spread(pieces, parts, patches, members, shards, cap, 1)
    returned = returned + exchange(outgoing, "pts", shards)
    return unpack(shard_count, place, returned, zone_rows)


def solution(mesh):
    placed = (
        P(("tile", "pts"), None),
        P(("tile", "pts")),
        P(("tile", "pts")),
        P(("tile", "pts")),
        P(),
        P(),
        P(None, None, "head"),
        P(None, "head"),
        P("head"),
        P(),
        P(),
        P(None, "head"),
        P("head"),
        P("head", None),
        P("head"),
    )

    return jax.shard_map(
        body, mesh=mesh, in_specs=placed, out_specs=P(("tile", "pts"), "head"), check_vma=False
    )
```

```python
import functools
import math

import jax
import jax.numpy as jnp
from jax import lax
from jax.experimental import pallas as pl
from jax.experimental.pallas import tpu as pltpu
from jax.sharding import PartitionSpec as P

PATCH = 1024
HEAD_DIM = 16
LANES = 128
ROW_STEP = 64
TILE = 512
FAST_TILE = 256
AHEAD = 4
UNROLL = 4
SAFE_LOG2 = 96.0
DIRECT = 8
F32 = jnp.float32
BF = jnp.bfloat16
I32 = jnp.int32
SMEM = pl.BlockSpec(memory_space=pltpu.SMEM)
VMEM = pl.BlockSpec(memory_space=pltpu.VMEM)
ANY = pl.BlockSpec(memory_space=pl.ANY)


def dot(lhs, rhs, dims=(1, 0)):
    return lax.dot_general(
        lhs, rhs, (((dims[0],), (dims[1],)), ((), ())), preferred_element_type=F32
    )


def exact_dot(values, choice):
    high = jnp.floor(values * (1.0 / LANES))
    low = values - high * LANES
    return dot(high.astype(BF), choice) * LANES + dot(low.astype(BF), choice)


def round_up(value, unit):
    return (value + unit - 1) // unit * unit


def grant(mib):
    return pltpu.CompilerParams(vmem_limit_bytes=mib * 2 ** 20)


def convert_rows(source, source_at, target, target_at, rows):
    step = math.gcd(rows, 128)

    def one(i, carry):
        at = pl.multiple_of(i * step, step)
        target[pl.ds(target_at + at, step), :] = source[pl.ds(source_at + at, step), :].astype(
            target.dtype
        )
        return carry

    lax.fori_loop(0, rows // step, one, 0)


def pack_kernel(
    shards, cap, rows_here, columns_at, held, rank, z_feat, *refs
):
    sends = refs[:shards]
    place_out = refs[shards]
    place, place_smem, ranks_full, narrow, wide, packed, sems = refs[shards + 1 :]
    here, member, count = lax.axis_index("pts"), lax.axis_index("head"), held[0]
    slots = place.shape[1]
    zone_rows, width = narrow.shape
    if columns_at:
        column = pl.multiple_of(member * width, width)
        source = z_feat.at[:, pl.ds(column, width)]
    else:
        source = z_feat
    feature_copy = pltpu.make_async_copy(source, narrow, sems.at[0])
    feature_copy.start()

    grid_rows = shards * rows_here // LANES
    block = rows_here // LANES
    ranks_full[:, :zone_rows] = rank[...]
    ranks = ranks_full[...]
    occupied = lax.broadcasted_iota(I32, (1, slots), 1) < count
    major = jnp.where(occupied, ranks // LANES, -1)
    minor = ranks % LANES
    hot_major = (lax.broadcasted_iota(I32, (grid_rows, slots), 0) == major).astype(BF)
    hot_minor = (lax.broadcasted_iota(I32, (LANES, slots), 0) == minor).astype(BF)
    members = dot(hot_minor, hot_major, (1, 1)).astype(BF)
    minor_r = lax.broadcasted_iota(I32, (LANES, LANES), 0)
    minor_c = lax.broadcasted_iota(I32, (LANES, LANES), 1)
    below = (minor_c < minor_r).astype(BF)
    ones = jnp.ones((LANES, LANES), BF)
    major_r = lax.broadcasted_iota(I32, (grid_rows, grid_rows), 0)
    major_c = lax.broadcasted_iota(I32, (grid_rows, grid_rows), 1)
    group = PATCH // LANES
    same_group = major_r // group == major_c // group
    earlier_row = (same_group & (major_r < major_c)).astype(BF)
    earlier_group = (
        (major_r // block == major_c // block)
        & (major_r // group < major_c // group)
        & (major_r % group == 0)
    ).astype(BF)
    before = dot(below, members) + dot(ones, dot(members, earlier_row).astype(BF))
    total = dot(ones, dot(members, same_group.astype(BF)).astype(BF))
    first_half = jnp.floor(total * 0.5)
    second_half = total - first_half
    first_base = exact_dot(first_half, earlier_group)
    second_base = exact_dot(second_half, earlier_group)
    target = lax.broadcasted_iota(I32, (LANES, grid_rows), 1) // block * cap
    spot = target.astype(F32) + jnp.where(
        before < first_half,
        first_base + before,
        second_base + before - first_half + cap // 2,
    )
    spread_out = exact_dot(spot, hot_major)
    found = jnp.sum(jnp.where(hot_minor > 0, spread_out, 0.0), axis=0, keepdims=True)
    place[...] = jnp.where(occupied, found.astype(I32), shards * cap)
    to_smem = pltpu.make_async_copy(place, place_smem, sems.at[1])
    to_smem.start()
    to_out = pltpu.make_async_copy(place, place_out, sems.at[2])
    to_out.start()
    feature_copy.wait()
    whole_rows = zone_rows // LANES * LANES
    convert_rows(narrow, 0, wide, 0, whole_rows)
    if whole_rows < zone_rows:
        wide[pl.ds(whole_rows, zone_rows - whole_rows), :] = narrow[
            pl.ds(whole_rows, zone_rows - whole_rows), :
        ].astype(F32)
    to_smem.wait()

    def place_rows(i, carry):
        base = pl.multiple_of(i * ROW_STEP, ROW_STEP)
        for k in range(ROW_STEP):
            packed[pl.ds(place_smem[0, base + k], 1), :] = wide[pl.ds(base + k, 1), :]
        return carry

    lax.fori_loop(0, (count + ROW_STEP - 1) // ROW_STEP, place_rows, 0)
    for k in range(shards):
        at = pl.multiple_of(lax.rem(here + k, shards) * cap, cap)
        convert_rows(packed, at, sends[k], 0, cap)
    to_out.wait()


def pack(held, rank, z_feat, columns_at, width, shards, cap, rows_here):
    zone_rows = z_feat.shape[0]
    slots = round_up(zone_rows, LANES)
    return pl.pallas_call(
        functools.partial(pack_kernel, shards, cap, rows_here, columns_at),
        out_shape=[jax.ShapeDtypeStruct((cap, width), BF)] * shards
        + [jax.ShapeDtypeStruct((1, slots), I32)],
        in_specs=[SMEM, VMEM, ANY],
        out_specs=[VMEM] * shards + [ANY],
        scratch_shapes=[
            pltpu.VMEM((1, slots), I32),
            pltpu.SMEM((1, slots), I32),
            pltpu.VMEM((1, slots), I32),
            pltpu.VMEM((zone_rows, width), BF),
            pltpu.VMEM((slots, width), F32),
            pltpu.VMEM((shards * cap + 8, width), F32),
            pltpu.SemaphoreType.DMA((3,)),
        ],
        name="pack",
    )(held, rank, z_feat)


def move_segment(source, source_at, target, target_at, length):
    def one(i, carry):
        for k in range(4):
            target[pl.ds(target_at + i * 32 + k * 8, 8), :] = source[
                pl.ds(source_at + i * 32 + k * 8, 8), :
            ]
        return carry

    lax.fori_loop(0, (length + 31) // 32, one, 0)


def segment_table(pieces, patches, shards, cap):
    packed_at, patch_at, lengths = {}, {}, {}
    for s in range(shards):
        ends = [s * cap, s * cap + cap // 2]
        for p in range(patches):
            count = pieces[p, s]
            lengths[0, p, s] = lax.shift_right_logical(count, 1)
            lengths[1, p, s] = count - lengths[0, p, s]
            for half in range(2):
                packed_at[half, p, s] = ends[half]
                ends[half] = ends[half] + lengths[half, p, s]
    for p in range(patches):
        at = p * PATCH
        for half in range(2):
            for s in range(shards):
                patch_at[half, p, s] = at
                at = at + lengths[half, p, s]
    return packed_at, patch_at, lengths


def compact_kernel(shards, patches, group, cap, pieces, *refs):
    blocks = refs[:shards]
    outs = refs[shards : shards + patches]
    wide, patch_rows = refs[shards + patches :]
    here, member = lax.axis_index("pts"), lax.axis_index("head")
    for k in range(shards):
        at = pl.multiple_of(lax.rem(here - k + shards, shards) * cap, cap)
        convert_rows(blocks[k], 0, wide, at, cap)
    packed_at, patch_at, lengths = segment_table(pieces, patches, shards, cap)
    for p in range(patches):
        for half in range(2):
            for s in range(shards):
                key = half, p, s
                move_segment(wide, packed_at[key], patch_rows, patch_at[key], lengths[key])
    own_group = member // group
    for k in range(patches):
        at = pl.multiple_of(lax.rem(own_group + k, patches) * PATCH, PATCH)
        convert_rows(patch_rows, at, outs[k], 0, PATCH)


def compact(pieces, blocks, patches, group):
    shards = len(blocks)
    cap, width = blocks[0].shape
    return pl.pallas_call(
        functools.partial(compact_kernel, shards, patches, group, cap),
        out_shape=[jax.ShapeDtypeStruct((PATCH, width), BF)] * patches,
        in_specs=[SMEM] + [VMEM] * shards,
        out_specs=[VMEM] * patches,
        scratch_shapes=[
            pltpu.VMEM((shards * cap + 64, width), F32),
            pltpu.VMEM((patches * PATCH + 64, width), F32),
        ],
        compiler_params=grant(12),
        name="compact",
    )(pieces, *blocks)


def spread_kernel(shards, patches, members, cap, half, pieces, *refs):
    given = members * (half + 1)
    blocks = refs[:given]
    sends = refs[given : given + shards]
    patch_rows, wide = refs[given + shards :]
    here, member = lax.axis_index("pts"), lax.axis_index("head")
    group = members // patches
    part_rows = blocks[0].shape[0]
    for phase in range(half + 1):
        for k in range(members):
            source = lax.rem(member - k + members, members)
            at = source // group * PATCH + phase * (PATCH // 2)
            at = pl.multiple_of(at + lax.rem(source, group) * part_rows, part_rows)
            convert_rows(blocks[phase * members + k], 0, patch_rows, at, part_rows)
    packed_at, patch_at, lengths = segment_table(pieces, patches, shards, cap)
    size = cap // 2
    for s in range(shards):
        for p in range(patches):
            key = half, p, s
            move_segment(
                patch_rows,
                patch_at[key],
                wide,
                packed_at[key] - s * cap - half * size + s * size,
                lengths[key],
            )
    for k in range(shards):
        at = pl.multiple_of(lax.rem(here + k, shards) * size, size)
        convert_rows(wide, at, sends[k], 0, size)


def spread(pieces, blocks, patches, members, shards, cap, half):
    width = blocks[0].shape[1]
    return pl.pallas_call(
        functools.partial(spread_kernel, shards, patches, members, cap, half),
        out_shape=[jax.ShapeDtypeStruct((cap // 2, width), BF)] * shards,
        in_specs=[SMEM] + [VMEM] * len(blocks),
        out_specs=[VMEM] * shards,
        scratch_shapes=[
            pltpu.VMEM((patches * PATCH + 64, width), F32),
            pltpu.VMEM((shards * cap // 2 + 64, width), F32),
        ],
        compiler_params=grant(12),
        name="spread",
    )(pieces, *blocks)


def unpack_kernel(shards, cap, held, place, *refs):
    blocks = refs[: 2 * shards]
    out = refs[2 * shards]
    wide, picked = refs[2 * shards + 1 :]
    here, count = lax.axis_index("pts"), held[0]
    zone_rows, width = out.shape
    size = cap // 2
    for half in range(2):
        for k in range(shards):
            at = lax.rem(here - k + shards, shards) * cap + half * size
            convert_rows(blocks[half * shards + k], 0, wide, pl.multiple_of(at, size), size)

    def pick_rows(i, carry):
        base = pl.multiple_of(i * ROW_STEP, ROW_STEP)
        for k in range(ROW_STEP):
            picked[pl.ds(base + k, 1), :] = wide[pl.ds(place[0, base + k], 1), :]
        return carry

    lax.fori_loop(0, (count + ROW_STEP - 1) // ROW_STEP, pick_rows, 0)

    def masked(at, rows):
        slot = at + lax.broadcasted_iota(I32, (rows, width), 0)
        out[pl.ds(at, rows), :] = jnp.where(slot < count, picked[pl.ds(at, rows), :], 0.0).astype(
            BF
        )

    def one(i, carry):
        masked(pl.multiple_of(i * LANES, LANES), LANES)
        return carry

    whole_rows = zone_rows // LANES * LANES
    lax.fori_loop(0, whole_rows // LANES, one, 0)
    if whole_rows < zone_rows:
        masked(whole_rows, zone_rows - whole_rows)


def unpack(held, place, blocks, zone_rows):
    shards = len(blocks) // 2
    size, width = blocks[0].shape
    cap = 2 * size
    slots = place.shape[1]
    return pl.pallas_call(
        functools.partial(unpack_kernel, shards, cap),
        out_shape=jax.ShapeDtypeStruct((zone_rows, width), BF),
        in_specs=[SMEM, SMEM] + [VMEM] * (2 * shards),
        out_specs=VMEM,
        scratch_shapes=[
            pltpu.VMEM((shards * cap + 8, width), F32),
            pltpu.VMEM((slots, width), F32),
        ],
        compiler_params=grant(14),
        name="unpack",
    )(held, place, *blocks)


def row_stats(parts, width):
    total = jnp.sum(sum(parts[1:], parts[0]), axis=1, keepdims=True)
    squares = jnp.sum(
        sum((x * x for x in parts[1:]), parts[0] * parts[0]), axis=1, keepdims=True
    )
    mean = total / width
    var = squares / width - mean * mean
    return mean, lax.rsqrt(var + 1e-05)


def block_places(blocks, patches, group):
    if blocks == patches * group:
        return arrival_order(patches, group)
    return list(range(blocks))


def project_kernel(blocks, patches, group, params, *refs):
    feats = refs[:blocks]
    weights = refs[blocks : 2 * blocks]
    keys, values, query, kept, small, normed = refs[2 * blocks :]
    rows = feats[0].shape[0]
    width = blocks * LANES
    queries = query.shape[1] // 2
    places = block_places(blocks, patches, group)
    part = lax.rem(lax.axis_index("head"), group)

    def norm(i, carry):
        at = pl.ds(pl.multiple_of(i * 128, 128), 128)
        parts = [feats[b][at, :].astype(F32) for b in range(blocks)]
        mean, scale = row_stats(parts, width)
        for b in range(blocks):
            cols = pl.ds(pl.multiple_of(places[b] * LANES, LANES), LANES)
            normed[at, cols] = (
                (parts[b] - mean) * scale * params[0:1, cols] + params[1:2, cols]
            ).astype(BF)
        return carry

    lax.fori_loop(0, rows // 128, norm, 0, unroll=2)
    starts = [
        pl.multiple_of(part * queries + half * (rows // 2), queries) for half in range(2)
    ]
    for b in range(blocks):
        for half in range(2):
            kept[places[b], pl.ds(half * queries, queries), :] = feats[b][
                pl.ds(starts[half], queries), :
            ]
    score_scale = HEAD_DIM ** (-0.5) * math.log2(math.e)
    pair_of = 2 if blocks % 2 == 0 else 1
    span = pair_of * LANES
    head_r = lax.broadcasted_iota(I32, (span, span), 0) // HEAD_DIM
    head_c = lax.broadcasted_iota(I32, (span, span), 1) // HEAD_DIM
    same_head = (head_r == head_c).astype(BF)

    def largest(found):
        return jnp.max(jnp.abs(found), axis=0, keepdims=True)

    worst = None
    for b in range(0, blocks, pair_of):
        both = range(b, b + pair_of)
        key_most, query_most = None, None
        q_weight, k_weight, v_weight = (
            jnp.concatenate([weights[c][t] for c in both], axis=1) for t in range(3)
        )
        for i in range(rows // 256):
            at = pl.ds(i * 256, 256)
            found = dot(normed[at, :], k_weight)
            most = largest(found)
            key_most = most if i == 0 else jnp.maximum(key_most, most)
            found = found.astype(BF)
            turned = dot(v_weight, normed[at, :], (0, 1)).astype(BF)
            for n, c in enumerate(both):
                keys[c, at, :] = found[:, n * LANES : (n + 1) * LANES]
                values[c, :, i * 256 : (i + 1) * 256] = turned[n * LANES : (n + 1) * LANES]
        for half in range(2):
            at = pl.ds(starts[half], queries)
            found = dot(normed[at, :], q_weight) * score_scale
            most = largest(found)
            query_most = most if half == 0 else jnp.maximum(query_most, most)
            found = found.astype(BF)
            for n, c in enumerate(both):
                query[c, pl.ds(half * queries, queries), :] = found[
                    :, n * LANES : (n + 1) * LANES
                ]
        product = jnp.broadcast_to(key_most * query_most, (8, span)).astype(BF)
        bound = dot(product, same_head)
        worst = bound if b == 0 else jnp.maximum(worst, bound)
    small[0] = (jnp.max(worst) * 1.05 < SAFE_LOG2).astype(I32)


def project(feats, weights, params, patches, group):
    blocks = len(feats)
    rows = feats[0].shape[0]
    width = weights[0].shape[1]
    own = jax.ShapeDtypeStruct((blocks, rows // group, LANES), BF)
    return pl.pallas_call(
        functools.partial(project_kernel, blocks, patches, group),
        out_shape=[
            jax.ShapeDtypeStruct((blocks, rows, LANES), BF),
            jax.ShapeDtypeStruct((blocks, LANES, rows), BF),
            own,
            own,
            jax.ShapeDtypeStruct((1,), I32),
        ],
        in_specs=[VMEM] * (1 + 2 * blocks),
        out_specs=[VMEM] * 4 + [SMEM],
        scratch_shapes=[pltpu.VMEM((rows, width), BF)],
        compiler_params=grant(14),
        cost_estimate=pl.CostEstimate(
            flops=6 * rows * width * width, bytes_accessed=8 * rows * width, transcendentals=0
        ),
        name="project",
    )(params, *feats, *weights)


def attend_kernel(low, high, half, tile, small, keys, values, query, out, even, odd):
    rows = keys.shape[1]
    queries = query.shape[1] // 2
    lane = lax.broadcasted_iota(I32, (1, LANES), 1)
    per_block = LANES // HEAD_DIM // 2
    steps = (high - low) * per_block

    def select(index):
        b, j = low + index // per_block, index % per_block
        own = query[b, pl.ds(half * queries, queries), :]
        zero = jnp.zeros((), BF)
        return jnp.concatenate(
            [jnp.where(lane // HEAD_DIM == 2 * j + n, own, zero) for n in range(2)], axis=0
        )

    def step(index, scores, top, coming, next_scores):
        b, j = index // per_block, index % per_block
        at = [
            pl.ds(pl.multiple_of((2 * j + n) * HEAD_DIM, HEAD_DIM), HEAD_DIM) for n in range(2)
        ]
        own = select(coming)
        next_keys = low + coming // per_block
        summed, next_top = [None, None], None
        for i in range(rows // tile):
            part = pl.ds(i * tile, tile)
            found = dot(keys[next_keys, part, :], own, (1, 1))
            next_scores[part, :] = found
            most = jnp.max(found, axis=0, keepdims=True)
            next_top = most if i == 0 else jnp.maximum(next_top, most)
            if top is not None:
                raised = jnp.exp2(scores[part, :] - top).astype(BF)
                for n in range(2):
                    lhs = jnp.concatenate(
                        [
                            values[low + b, at[n], i * tile : (i + 1) * tile],
                            jnp.ones((HEAD_DIM, tile), BF),
                        ],
                        axis=0,
                    )
                    more = dot(lhs, raised[:, n * queries : (n + 1) * queries])
                    summed[n] = more if i == 0 else summed[n] + more
        if top is not None:
            for n in range(2):
                out[b, at[n], :] = (summed[n][:HEAD_DIM] / summed[n][HEAD_DIM:]).astype(BF)
        return next_top

    def pair(i, top):
        once = jnp.minimum(i, 0) + 1
        next_top = lax.fori_loop(
            0, once, lambda _, most: step(2 * i, even, top, 2 * i + 1, odd), top
        )
        following = jnp.minimum(2 * i + 2, steps - 1)
        return lax.fori_loop(
            0, once, lambda _, most: step(2 * i + 1, odd, next_top, following, even), next_top
        )

    @pl.when(small[0] == 0)
    def _():
        lax.fori_loop(0, steps // 2, pair, step(0, None, None, 0, even))

    fast_tile = min(FAST_TILE, rows)
    tiles = rows // fast_tile

    def several(i, carry):
        indexes = [UNROLL * i + u for u in range(UNROLL)]
        plan = [(u, t) for u in range(UNROLL) for t in range(tiles)]
        owns = [None] * UNROLL

        def score(u, t):
            if t == 0:
                owns[u] = select(indexes[u])
            part = pl.ds(t * fast_tile, fast_tile)
            return dot(keys[low + indexes[u] // per_block, part, :], owns[u], (1, 1))

        waiting = [score(*plan[n]) for n in range(min(AHEAD, len(plan)))]
        summed = [None, None]
        for n, (u, t) in enumerate(plan):
            if n + AHEAD < len(plan):
                waiting.append(score(*plan[n + AHEAD]))
            raised = jnp.exp2(waiting[n]).astype(BF)
            b, j = indexes[u] // per_block, indexes[u] % per_block
            for m in range(2):
                at = pl.ds(pl.multiple_of((2 * j + m) * HEAD_DIM, HEAD_DIM), HEAD_DIM)
                lhs = jnp.concatenate(
                    [
                        values[low + b, at, t * fast_tile : (t + 1) * fast_tile],
                        jnp.ones((HEAD_DIM, fast_tile), BF),
                    ],
                    axis=0,
                )
                more = dot(lhs, raised[:, m * queries : (m + 1) * queries])
                summed[m] = more if t == 0 else summed[m] + more
                if t == tiles - 1:
                    out[b, at, :] = (summed[m][:HEAD_DIM] / summed[m][HEAD_DIM:]).astype(BF)
        return carry

    @pl.when(small[0] != 0)
    def _():
        lax.fori_loop(0, steps // UNROLL, several, 0)


def attend(small, keys, values, query, low, high, half):
    rows = keys.shape[1]
    queries = query.shape[1] // 2
    return pl.pallas_call(
        functools.partial(attend_kernel, low, high, half, min(TILE, rows)),
        out_shape=jax.ShapeDtypeStruct((high - low, LANES, queries), BF),
        in_specs=[SMEM] + [VMEM] * 3,
        out_specs=VMEM,
        scratch_shapes=[pltpu.VMEM((rows, 2 * queries), F32)] * 2,
        compiler_params=grant(14),
        cost_estimate=pl.CostEstimate(
            flops=4 * queries * rows * LANES * (high - low) * (LANES // HEAD_DIM),
            bytes_accessed=4 * rows * LANES * (high - low),
            transcendentals=0,
        ),
        name="attend",
    )(small, keys, values, query)


def mlp_kernel(blocks, members, patches, sends, chunk, half, pieces_of, params, kept, *refs):
    mixed = refs[:pieces_of]
    refs = refs[pieces_of:]
    projs = refs[:blocks]
    ups = refs[blocks : blocks + members]
    downs = refs[blocks + members : blocks + 2 * members]
    vectors = refs[blocks + 2 * members : blocks + 3 * members]
    results = refs[blocks + 3 * members : blocks + 3 * members + sends]
    proj, vector, final = refs[blocks + 3 * members + sends :]
    rows = kept.shape[1] // 2
    width = blocks * LANES
    share = width // members
    group = members // patches
    spots = arrival_order(patches, group)
    places = block_places(blocks, patches, group)
    for k in range(blocks):
        cols = pl.ds(pl.multiple_of(places[k] * LANES, LANES), LANES)
        for r in range(blocks):
            from_rows = pl.ds(pl.multiple_of(places[r] * LANES, LANES), LANES)
            proj[r * LANES : (r + 1) * LANES, cols] = projs[k][from_rows, :]
    for k in range(members):
        vector[spots[k]] = vectors[k][...]
    out_bias = jnp.concatenate([vector[k, :, :share] for k in range(members)], axis=1)
    down_bias = jnp.concatenate([vector[k, :, share : 2 * share] for k in range(members)], axis=1)
    root_half = 0.5 ** 0.5

    def one(i, carry):
        at = pl.ds(pl.multiple_of(i * chunk, chunk), chunk)
        attended = jnp.concatenate(
            [m[b, :, at] for m in mixed for b in range(m.shape[0])], axis=0
        )
        own = pl.ds(pl.multiple_of(half * rows + i * chunk, chunk), chunk)
        features = jnp.concatenate([kept[b, own, :] for b in range(blocks)], axis=1)
        residual = (features.astype(F32) + dot(attended, proj[...], (0, 0)) + out_bias).astype(BF)
        wide = residual.astype(F32)
        mean, scale = row_stats([wide], width)
        normed = ((wide - mean) * scale * params[2:3, :] + params[3:4, :]).astype(BF)
        total = wide + down_bias
        for k in range(members):
            spot = spots[k]
            before = dot(normed, ups[k][...]) + vector[spot, :, 2 * share :]
            hidden = (0.5 * before * (1.0 + lax.erf(before * root_half))).astype(BF)
            total = total + dot(hidden, downs[k][...])
        for b in range(blocks):
            final[b, at, :] = total[:, b * LANES : (b + 1) * LANES].astype(BF)
        return carry

    lax.fori_loop(0, rows // chunk, one, 0)
    if sends > 1:
        me = lax.axis_index("head")
        for k in range(sends):
            results[k][...] = final[lax.rem(me + k, sends)]
    else:
        results[0][...] = final[...]


def mlp(patches, half, params, mixed, kept, projs, ups, downs, vectors):
    blocks, rows = kept.shape[0], kept.shape[1] // 2
    members = len(ups)
    width = blocks * LANES
    hidden_here = ups[0].shape[1]
    sends = members if members == blocks else 1
    shape = (rows, LANES) if sends > 1 else (blocks, rows, LANES)
    chunk = min(256, rows)
    return pl.pallas_call(
        functools.partial(
            mlp_kernel, blocks, members, patches, sends, chunk, half, len(mixed)
        ),
        out_shape=[jax.ShapeDtypeStruct(shape, BF)] * sends,
        in_specs=[VMEM] * (2 + len(mixed) + blocks + 3 * members),
        out_specs=[VMEM] * sends,
        scratch_shapes=[
            pltpu.VMEM((width, width), BF),
            pltpu.VMEM((members, 1, vectors[0].shape[1]), F32),
            pltpu.VMEM((blocks, rows, LANES), BF),
        ],
        cost_estimate=pl.CostEstimate(
            flops=4 * rows * width * hidden_here * members,
            bytes_accessed=4 * width * hidden_here * members,
            transcendentals=0,
        ),
        compiler_params=grant(22),
        name="mlp",
    )(params, kept, *mixed, *projs, *ups, *downs, *vectors)


def shift(array, axis, size, step):
    return lax.ppermute(array, axis, [(i, (i + step) % size) for i in range(size)])


def exchange(blocks, axis, size):
    if size <= DIRECT:
        return [blocks[0]] + [shift(blocks[k], axis, size, k) for k in range(1, size)]
    me = lax.axis_index(axis)
    steps = jnp.arange(size, dtype=I32)
    stacked = jnp.stack(blocks)[(steps - me) % size]
    got = lax.all_to_all(stacked, axis, 0, 0, tiled=True)[(me - steps) % size]
    return [got[k] for k in range(size)]


def arrival_order(groups, group):
    member = lax.axis_index("head")
    return [
        lax.rem(member // group - k + groups, groups) * group
        + lax.rem(lax.rem(member, group) - j + group, group)
        for k in range(groups)
        for j in range(group)
    ]


def group_shift(array, groups, group, step):
    size = groups * group
    pairs = [(i, (i // group + step) % groups * group + i % group) for i in range(size)]
    return lax.ppermute(array, "head", pairs)


def member_shift(array, groups, group, step):
    size = groups * group
    pairs = [(i, i // group * group + (i % group + step) % group) for i in range(size)]
    return lax.ppermute(array, "head", pairs)


def gather_members(sources, groups, group):
    found = []
    for k in range(groups):
        moved = sources[k]
        if k > 0:
            moved = group_shift(moved, groups, group, k)
        for j in range(group):
            found.append(moved if j == 0 else member_shift(moved, groups, group, j))
    return found


def body(
    z_feat,
    shard_count,
    hilbert_rank,
    z_slot,
    ln1_gain,
    ln1_bias,
    w_qkv,
    w_out,
    b_out,
    ln2_gain,
    ln2_bias,
    w_up,
    b_up,
    w_down,
    b_down,
):
    shards = lax.axis_size("pts")
    members = lax.axis_size("head")
    rows_here = z_slot.shape[0]
    zone_rows, full_width = z_feat.shape
    width = w_out.shape[1]
    patches = rows_here // PATCH
    group = members // patches
    blocks = full_width // LANES
    skew_step = rows_here // (2 * shards * (shards - 1))
    cap = round_up(rows_here // shards + 2 * skew_step * (shards - 1), 32)
    member = lax.axis_index("head")

    def natural(found):
        spots = jnp.stack(arrival_order(patches, group)).astype(I32)
        stacked = jnp.stack(found)
        back = jnp.zeros((members,), I32).at[spots].set(jnp.arange(members, dtype=I32))
        stacked = jnp.take(stacked, back, axis=0)
        joined = jnp.concatenate([stacked[i] for i in range(members)], axis=-1)
        return [joined[..., b * LANES : (b + 1) * LANES] for b in range(blocks)]

    def everywhere(array):
        return gather_members([array] * patches, patches, group)

    qkv_found = everywhere(w_qkv)
    out_found = everywhere(w_out)
    up_found = everywhere(w_up)
    down_found = everywhere(w_down)
    vector = jnp.concatenate([b_out, b_down, b_up])[None, :]
    vectors = [vector]
    for step in range(1, members):
        k, j = step // group, step % group
        pairs = [
            (i, (i // group + k) % patches * group + (i % group + j) % group)
            for i in range(members)
        ]
        vectors.append(lax.ppermute(vector, "head", pairs))

    rank = hilbert_rank[None, :]
    if width % LANES == 0:
        z_source = z_feat
    else:
        z_source = lax.dynamic_slice_in_dim(z_feat, member * width, width, 1)
    *sends, place = pack(
        shard_count, rank, z_source, width % LANES == 0, width, shards, cap, rows_here
    )
    source = (z_slot // zone_rows).reshape(patches, PATCH, 1)
    pieces = jnp.sum((source == jnp.arange(shards, dtype=I32)).astype(I32), axis=1)
    params = jnp.stack([ln1_gain, ln1_bias, ln2_gain, ln2_bias])
    pieces, params = lax.optimization_barrier((pieces, params))
    arrived = exchange(sends, "pts", shards)
    patch_blocks = compact(pieces, arrived, patches, group)
    feats = gather_members(patch_blocks, patches, group)

    if width == LANES:
        qkv_blocks, out_blocks = qkv_found, out_found
    else:
        feats = natural(feats)
        qkv_blocks, out_blocks = natural(qkv_found), natural(out_found)

    keys, values, query, kept, small = project(feats, qkv_blocks, params, patches, group)

    def columns_back(half, mixed):
        results = mlp(
            patches, half, params, mixed, kept, out_blocks, up_found, down_found, vectors
        )
        if width != LANES:
            joined = jnp.concatenate([results[0][b] for b in range(blocks)], axis=1)
            results = [
                lax.dynamic_slice_in_dim(joined, (member + k) % members * width, width, 1)
                for k in range(members)
            ]
        return [results[0]] + [shift(results[k], "head", members, k) for k in range(1, members)]

    mixed = attend(small, keys, values, query, 0, blocks, 0)
    parts = columns_back(0, [mixed])
    middle = blocks // 2
    mixed_low = attend(small, keys, values, query, 0, middle, 1)
    outgoing = spread(pieces, parts, patches, members, shards, cap, 0)
    returned = exchange(outgoing, "pts", shards)
    mixed_high = attend(small, keys, values, query, middle, blocks, 1)
    parts = parts + columns_back(1, [mixed_low, mixed_high])
    outgoing = spread(pieces, parts, patches, members, shards, cap, 1)
    returned = returned + exchange(outgoing, "pts", shards)
    return unpack(shard_count, place, returned, zone_rows)


def solution(mesh):
    placed = (
        P(("tile", "pts"), None),
        P(("tile", "pts")),
        P(("tile", "pts")),
        P(("tile", "pts")),
        P(),
        P(),
        P(None, None, "head"),
        P(None, "head"),
        P("head"),
        P(),
        P(),
        P(None, "head"),
        P("head"),
        P("head", None),
        P("head"),
    )

    return jax.shard_map(
        body, mesh=mesh, in_specs=placed, out_specs=P(("tile", "pts"), "head"), check_vma=False
    )
```

```python
import functools
import math

import jax
import jax.numpy as jnp
from jax import lax
from jax.experimental import pallas as pl
from jax.experimental.pallas import tpu as pltpu
from jax.sharding import PartitionSpec as P

PATCH = 1024
HEAD_DIM = 16
LANES = 128
ROW_STEP = 128
TILE = 512
FAST_TILE = 256
AHEAD = 4
UNROLL = 4
SAFE_LOG2 = 96.0
DIRECT = 8
F32 = jnp.float32
BF = jnp.bfloat16
I32 = jnp.int32
SMEM = pl.BlockSpec(memory_space=pltpu.SMEM)
VMEM = pl.BlockSpec(memory_space=pltpu.VMEM)
ANY = pl.BlockSpec(memory_space=pl.ANY)


def dot(lhs, rhs, dims=(1, 0)):
    return lax.dot_general(
        lhs, rhs, (((dims[0],), (dims[1],)), ((), ())), preferred_element_type=F32
    )


def exact_dot(values, choice):
    high = jnp.floor(values * (1.0 / LANES))
    low = values - high * LANES
    return dot(high.astype(BF), choice) * LANES + dot(low.astype(BF), choice)


def round_up(value, unit):
    return (value + unit - 1) // unit * unit


def grant(mib):
    return pltpu.CompilerParams(vmem_limit_bytes=mib * 2 ** 20)


def convert_rows(source, source_at, target, target_at, rows):
    step = math.gcd(rows, 128)

    def one(i, carry):
        at = pl.multiple_of(i * step, step)
        target[pl.ds(target_at + at, step), :] = source[pl.ds(source_at + at, step), :].astype(
            target.dtype
        )
        return carry

    lax.fori_loop(0, rows // step, one, 0)


def pack_kernel(
    shards, cap, rows_here, columns_at, held, rank, z_feat, *refs
):
    sends = refs[:shards]
    place_out = refs[shards]
    place, place_smem, ranks_full, narrow, wide, packed, sems = refs[shards + 1 :]
    here, member, count = lax.axis_index("pts"), lax.axis_index("head"), held[0]
    slots = place.shape[1]
    zone_rows, width = narrow.shape
    if columns_at:
        column = pl.multiple_of(member * width, width)
        source = z_feat.at[:, pl.ds(column, width)]
    else:
        source = z_feat
    feature_copy = pltpu.make_async_copy(source, narrow, sems.at[0])
    feature_copy.start()

    grid_rows = shards * rows_here // LANES
    block = rows_here // LANES
    ranks_full[:, :zone_rows] = rank[...]
    ranks = ranks_full[...]
    occupied = lax.broadcasted_iota(I32, (1, slots), 1) < count
    major = jnp.where(occupied, ranks // LANES, -1)
    minor = ranks % LANES
    hot_major = (lax.broadcasted_iota(I32, (grid_rows, slots), 0) == major).astype(BF)
    hot_minor = (lax.broadcasted_iota(I32, (LANES, slots), 0) == minor).astype(BF)
    members = dot(hot_minor, hot_major, (1, 1)).astype(BF)
    minor_r = lax.broadcasted_iota(I32, (LANES, LANES), 0)
    minor_c = lax.broadcasted_iota(I32, (LANES, LANES), 1)
    below = (minor_c < minor_r).astype(BF)
    ones = jnp.ones((LANES, LANES), BF)
    major_r = lax.broadcasted_iota(I32, (grid_rows, grid_rows), 0)
    major_c = lax.broadcasted_iota(I32, (grid_rows, grid_rows), 1)
    group = PATCH // LANES
    same_group = major_r // group == major_c // group
    earlier_row = (same_group & (major_r < major_c)).astype(BF)
    earlier_group = (
        (major_r // block == major_c // block)
        & (major_r // group < major_c // group)
        & (major_r % group == 0)
    ).astype(BF)
    before = dot(below, members) + dot(ones, dot(members, earlier_row).astype(BF))
    total = dot(ones, dot(members, same_group.astype(BF)).astype(BF))
    first_half = jnp.floor(total * 0.5)
    second_half = total - first_half
    first_base = exact_dot(first_half, earlier_group)
    second_base = exact_dot(second_half, earlier_group)
    target = lax.broadcasted_iota(I32, (LANES, grid_rows), 1) // block * cap
    spot = target.astype(F32) + jnp.where(
        before < first_half,
        first_base + before,
        second_base + before - first_half + cap // 2,
    )
    spread_out = exact_dot(spot, hot_major)
    found = jnp.sum(jnp.where(hot_minor > 0, spread_out, 0.0), axis=0, keepdims=True)
    place[...] = jnp.where(occupied, found.astype(I32), shards * cap)
    to_smem = pltpu.make_async_copy(place, place_smem, sems.at[1])
    to_smem.start()
    to_out = pltpu.make_async_copy(place, place_out, sems.at[2])
    to_out.start()
    feature_copy.wait()
    whole_rows = zone_rows // LANES * LANES
    convert_rows(narrow, 0, wide, 0, whole_rows)
    if whole_rows < zone_rows:
        wide[pl.ds(whole_rows, zone_rows - whole_rows), :] = narrow[
            pl.ds(whole_rows, zone_rows - whole_rows), :
        ].astype(F32)
    to_smem.wait()

    stride = slots // ROW_STEP

    def place_rows(i, carry):
        for k in range(ROW_STEP):
            target = place_smem.at[:, pl.ds(k * stride, stride)][0, i]
            packed[pl.ds(target, 1), :] = wide.at[pl.ds(k * stride, stride)][pl.ds(i, 1), :]
        return carry

    lax.fori_loop(0, stride, place_rows, 0)
    for k in range(shards):
        at = pl.multiple_of(lax.rem(here + k, shards) * cap, cap)
        convert_rows(packed, at, sends[k], 0, cap)
    to_out.wait()


def pack(held, rank, z_feat, columns_at, width, shards, cap, rows_here):
    zone_rows = z_feat.shape[0]
    slots = round_up(zone_rows, LANES)
    return pl.pallas_call(
        functools.partial(pack_kernel, shards, cap, rows_here, columns_at),
        out_shape=[jax.ShapeDtypeStruct((cap, width), BF)] * shards
        + [jax.ShapeDtypeStruct((1, slots), I32)],
        in_specs=[SMEM, VMEM, ANY],
        out_specs=[VMEM] * shards + [ANY],
        scratch_shapes=[
            pltpu.VMEM((1, slots), I32),
            pltpu.SMEM((1, slots), I32),
            pltpu.VMEM((1, slots), I32),
            pltpu.VMEM((zone_rows, width), BF),
            pltpu.VMEM((slots, width), F32),
            pltpu.VMEM((shards * cap + 8, width), F32),
            pltpu.SemaphoreType.DMA((3,)),
        ],
        name="pack",
    )(held, rank, z_feat)


def keep_kernel(block, out):
    out[...] = block[...]


def keep(block):
    return pl.pallas_call(
        keep_kernel,
        out_shape=jax.ShapeDtypeStruct(block.shape, block.dtype),
        in_specs=[VMEM],
        out_specs=VMEM,
        compiler_params=grant(2),
        name="keep",
    )(block)


def move_segment(source, source_at, target, target_at, length):
    def one(i, carry):
        for k in range(4):
            target[pl.ds(target_at + i * 32 + k * 8, 8), :] = source[
                pl.ds(source_at + i * 32 + k * 8, 8), :
            ]
        return carry

    lax.fori_loop(0, (length + 31) // 32, one, 0)


def segment_table(pieces, patches, shards, cap):
    packed_at, patch_at, lengths = {}, {}, {}
    for s in range(shards):
        ends = [s * cap, s * cap + cap // 2]
        for p in range(patches):
            count = pieces[p, s]
            lengths[0, p, s] = lax.shift_right_logical(count, 1)
            lengths[1, p, s] = count - lengths[0, p, s]
            for half in range(2):
                packed_at[half, p, s] = ends[half]
                ends[half] = ends[half] + lengths[half, p, s]
    for p in range(patches):
        at = p * PATCH
        for half in range(2):
            for s in range(shards):
                patch_at[half, p, s] = at
                at = at + lengths[half, p, s]
    return packed_at, patch_at, lengths


def compact_kernel(shards, patches, group, cap, pieces, *refs):
    blocks = refs[:shards]
    outs = refs[shards : shards + patches]
    wide, patch_rows = refs[shards + patches :]
    here, member = lax.axis_index("pts"), lax.axis_index("head")
    for k in range(shards):
        at = pl.multiple_of(lax.rem(here - k + shards, shards) * cap, cap)
        convert_rows(blocks[k], 0, wide, at, cap)
    packed_at, patch_at, lengths = segment_table(pieces, patches, shards, cap)
    for p in range(patches):
        for half in range(2):
            for s in range(shards):
                key = half, p, s
                move_segment(wide, packed_at[key], patch_rows, patch_at[key], lengths[key])
    own_group = member // group
    for k in range(patches):
        at = pl.multiple_of(lax.rem(own_group + k, patches) * PATCH, PATCH)
        convert_rows(patch_rows, at, outs[k], 0, PATCH)


def compact(pieces, blocks, patches, group):
    shards = len(blocks)
    cap, width = blocks[0].shape
    return pl.pallas_call(
        functools.partial(compact_kernel, shards, patches, group, cap),
        out_shape=[jax.ShapeDtypeStruct((PATCH, width), BF)] * patches,
        in_specs=[SMEM] + [VMEM] * shards,
        out_specs=[VMEM] * patches,
        scratch_shapes=[
            pltpu.VMEM((shards * cap + 64, width), F32),
            pltpu.VMEM((patches * PATCH + 64, width), F32),
        ],
        compiler_params=grant(12),
        name="compact",
    )(pieces, *blocks)


def spread_kernel(shards, patches, members, cap, half, pieces, *refs):
    given = members * (half + 1)
    blocks = refs[:given]
    sends = refs[given : given + shards]
    patch_rows, wide = refs[given + shards :]
    here, member = lax.axis_index("pts"), lax.axis_index("head")
    group = members // patches
    part_rows = blocks[0].shape[0]
    for phase in range(half + 1):
        for k in range(members):
            source = lax.rem(member - k + members, members)
            at = source // group * PATCH + phase * (PATCH // 2)
            at = pl.multiple_of(at + lax.rem(source, group) * part_rows, part_rows)
            convert_rows(blocks[phase * members + k], 0, patch_rows, at, part_rows)
    packed_at, patch_at, lengths = segment_table(pieces, patches, shards, cap)
    size = cap // 2
    for s in range(shards):
        for p in range(patches):
            key = half, p, s
            move_segment(
                patch_rows,
                patch_at[key],
                wide,
                packed_at[key] - s * cap - half * size + s * size,
                lengths[key],
            )
    for k in range(shards):
        at = pl.multiple_of(lax.rem(here + k, shards) * size, size)
        convert_rows(wide, at, sends[k], 0, size)


def spread(pieces, blocks, patches, members, shards, cap, half):
    width = blocks[0].shape[1]
    return pl.pallas_call(
        functools.partial(spread_kernel, shards, patches, members, cap, half),
        out_shape=[jax.ShapeDtypeStruct((cap // 2, width), BF)] * shards,
        in_specs=[SMEM] + [VMEM] * len(blocks),
        out_specs=[VMEM] * shards,
        scratch_shapes=[
            pltpu.VMEM((patches * PATCH + 64, width), F32),
            pltpu.VMEM((shards * cap // 2 + 64, width), F32),
        ],
        compiler_params=grant(12),
        name="spread",
    )(pieces, *blocks)


def unpack_kernel(shards, cap, held, place, *refs):
    blocks = refs[: 2 * shards]
    out = refs[2 * shards]
    wide, picked = refs[2 * shards + 1 :]
    here, count = lax.axis_index("pts"), held[0]
    zone_rows, width = out.shape
    size = cap // 2
    for half in range(2):
        for k in range(shards):
            at = lax.rem(here - k + shards, shards) * cap + half * size
            convert_rows(blocks[half * shards + k], 0, wide, pl.multiple_of(at, size), size)

    stride = picked.shape[0] // ROW_STEP

    def pick_rows(i, carry):
        for k in range(ROW_STEP):
            source = place.at[:, pl.ds(k * stride, stride)][0, i]
            picked.at[pl.ds(k * stride, stride)][pl.ds(i, 1), :] = wide[pl.ds(source, 1), :]
        return carry

    lax.fori_loop(0, stride, pick_rows, 0)

    def masked(at, rows):
        slot = at + lax.broadcasted_iota(I32, (rows, width), 0)
        out[pl.ds(at, rows), :] = jnp.where(slot < count, picked[pl.ds(at, rows), :], 0.0).astype(
            BF
        )

    def one(i, carry):
        masked(pl.multiple_of(i * LANES, LANES), LANES)
        return carry

    whole_rows = zone_rows // LANES * LANES
    lax.fori_loop(0, whole_rows // LANES, one, 0)
    if whole_rows < zone_rows:
        masked(whole_rows, zone_rows - whole_rows)


def unpack(held, place, blocks, zone_rows):
    shards = len(blocks) // 2
    size, width = blocks[0].shape
    cap = 2 * size
    slots = place.shape[1]
    return pl.pallas_call(
        functools.partial(unpack_kernel, shards, cap),
        out_shape=jax.ShapeDtypeStruct((zone_rows, width), BF),
        in_specs=[SMEM, SMEM] + [VMEM] * (2 * shards),
        out_specs=VMEM,
        scratch_shapes=[
            pltpu.VMEM((shards * cap + 8, width), F32),
            pltpu.VMEM((slots, width), F32),
        ],
        compiler_params=grant(14),
        name="unpack",
    )(held, place, *blocks)


def row_stats(parts, width):
    total = jnp.sum(sum(parts[1:], parts[0]), axis=1, keepdims=True)
    squares = jnp.sum(
        sum((x * x for x in parts[1:]), parts[0] * parts[0]), axis=1, keepdims=True
    )
    mean = total / width
    var = squares / width - mean * mean
    return mean, lax.rsqrt(var + 1e-05)


def block_places(blocks, patches, group):
    if blocks == patches * group:
        return arrival_order(patches, group)
    return list(range(blocks))


def project_kernel(blocks, patches, group, params, *refs):
    feats = refs[:blocks]
    weights = refs[blocks : 2 * blocks]
    keys, values, query, kept, small, normed = refs[2 * blocks :]
    rows = feats[0].shape[0]
    width = blocks * LANES
    queries = query.shape[1] // 2
    places = block_places(blocks, patches, group)
    part = lax.rem(lax.axis_index("head"), group)

    def norm(i, carry):
        at = pl.ds(pl.multiple_of(i * 128, 128), 128)
        parts = [feats[b][at, :].astype(F32) for b in range(blocks)]
        mean, scale = row_stats(parts, width)
        for b in range(blocks):
            cols = pl.ds(pl.multiple_of(places[b] * LANES, LANES), LANES)
            normed[at, cols] = (
                (parts[b] - mean) * scale * params[0:1, cols] + params[1:2, cols]
            ).astype(BF)
        return carry

    lax.fori_loop(0, rows // 128, norm, 0, unroll=2)
    starts = [
        pl.multiple_of(part * queries + half * (rows // 2), queries) for half in range(2)
    ]
    for b in range(blocks):
        for half in range(2):
            kept[places[b], pl.ds(half * queries, queries), :] = feats[b][
                pl.ds(starts[half], queries), :
            ]
    score_scale = HEAD_DIM ** (-0.5) * math.log2(math.e)
    pair_of = 2 if blocks % 2 == 0 else 1
    span = pair_of * LANES
    head_r = lax.broadcasted_iota(I32, (span, span), 0) // HEAD_DIM
    head_c = lax.broadcasted_iota(I32, (span, span), 1) // HEAD_DIM
    same_head = (head_r == head_c).astype(BF)

    def largest(found):
        return jnp.max(jnp.abs(found), axis=0, keepdims=True)

    worst = None
    for b in range(0, blocks, pair_of):
        both = range(b, b + pair_of)
        key_most, query_most = None, None
        q_weight, k_weight, v_weight = (
            jnp.concatenate([weights[c][t] for c in both], axis=1) for t in range(3)
        )
        for i in range(rows // 256):
            at = pl.ds(i * 256, 256)
            found = dot(normed[at, :], k_weight)
            most = largest(found)
            key_most = most if i == 0 else jnp.maximum(key_most, most)
            found = found.astype(BF)
            turned = dot(v_weight, normed[at, :], (0, 1)).astype(BF)
            for n, c in enumerate(both):
                keys[c, at, :] = found[:, n * LANES : (n + 1) * LANES]
                values[c, :, i * 256 : (i + 1) * 256] = turned[n * LANES : (n + 1) * LANES]
        for half in range(2):
            at = pl.ds(starts[half], queries)
            found = dot(normed[at, :], q_weight) * score_scale
            most = largest(found)
            query_most = most if half == 0 else jnp.maximum(query_most, most)
            found = found.astype(BF)
            for n, c in enumerate(both):
                query[c, pl.ds(half * queries, queries), :] = found[
                    :, n * LANES : (n + 1) * LANES
                ]
        product = jnp.broadcast_to(key_most * query_most, (8, span)).astype(BF)
        bound = dot(product, same_head)
        worst = bound if b == 0 else jnp.maximum(worst, bound)
    small[0] = (jnp.max(worst) * 1.05 < SAFE_LOG2).astype(I32)


def project(feats, weights, params, patches, group):
    blocks = len(feats)
    rows = feats[0].shape[0]
    width = weights[0].shape[1]
    own = jax.ShapeDtypeStruct((blocks, rows // group, LANES), BF)
    return pl.pallas_call(
        functools.partial(project_kernel, blocks, patches, group),
        out_shape=[
            jax.ShapeDtypeStruct((blocks, rows, LANES), BF),
            jax.ShapeDtypeStruct((blocks, LANES, rows), BF),
            own,
            own,
            jax.ShapeDtypeStruct((1,), I32),
        ],
        in_specs=[VMEM] * (1 + 2 * blocks),
        out_specs=[VMEM] * 4 + [SMEM],
        scratch_shapes=[pltpu.VMEM((rows, width), BF)],
        compiler_params=grant(14),
        cost_estimate=pl.CostEstimate(
            flops=6 * rows * width * width, bytes_accessed=8 * rows * width, transcendentals=0
        ),
        name="project",
    )(params, *feats, *weights)


def attend_kernel(low, high, half, tile, small, keys, values, query, out, even, odd):
    rows = keys.shape[1]
    queries = query.shape[1] // 2
    lane = lax.broadcasted_iota(I32, (1, LANES), 1)
    per_block = LANES // HEAD_DIM // 2
    steps = (high - low) * per_block

    def select(index):
        b, j = low + index // per_block, index % per_block
        own = query[b, pl.ds(half * queries, queries), :]
        zero = jnp.zeros((), BF)
        return jnp.concatenate(
            [jnp.where(lane // HEAD_DIM == 2 * j + n, own, zero) for n in range(2)], axis=0
        )

    def step(index, scores, top, coming, next_scores):
        b, j = index // per_block, index % per_block
        at = [
            pl.ds(pl.multiple_of((2 * j + n) * HEAD_DIM, HEAD_DIM), HEAD_DIM) for n in range(2)
        ]
        own = select(coming)
        next_keys = low + coming // per_block
        summed, next_top = [None, None], None
        for i in range(rows // tile):
            part = pl.ds(i * tile, tile)
            found = dot(keys[next_keys, part, :], own, (1, 1))
            next_scores[part, :] = found
            most = jnp.max(found, axis=0, keepdims=True)
            next_top = most if i == 0 else jnp.maximum(next_top, most)
            if top is not None:
                raised = jnp.exp2(scores[part, :] - top).astype(BF)
                for n in range(2):
                    lhs = jnp.concatenate(
                        [
                            values[low + b, at[n], i * tile : (i + 1) * tile],
                            jnp.ones((HEAD_DIM, tile), BF),
                        ],
                        axis=0,
                    )
                    more = dot(lhs, raised[:, n * queries : (n + 1) * queries])
                    summed[n] = more if i == 0 else summed[n] + more
        if top is not None:
            for n in range(2):
                out[b, at[n], :] = (summed[n][:HEAD_DIM] / summed[n][HEAD_DIM:]).astype(BF)
        return next_top

    def pair(i, top):
        once = jnp.minimum(i, 0) + 1
        next_top = lax.fori_loop(
            0, once, lambda _, most: step(2 * i, even, top, 2 * i + 1, odd), top
        )
        following = jnp.minimum(2 * i + 2, steps - 1)
        return lax.fori_loop(
            0, once, lambda _, most: step(2 * i + 1, odd, next_top, following, even), next_top
        )

    @pl.when(small[0] == 0)
    def _():
        lax.fori_loop(0, steps // 2, pair, step(0, None, None, 0, even))

    fast_tile = min(FAST_TILE, rows)
    tiles = rows // fast_tile

    def several(i, carry):
        indexes = [UNROLL * i + u for u in range(UNROLL)]
        plan = [(u, t) for u in range(UNROLL) for t in range(tiles)]
        owns = [None] * UNROLL

        def score(u, t):
            if t == 0:
                owns[u] = select(indexes[u])
            part = pl.ds(t * fast_tile, fast_tile)
            return dot(keys[low + indexes[u] // per_block, part, :], owns[u], (1, 1))

        waiting = [score(*plan[n]) for n in range(min(AHEAD, len(plan)))]
        summed = [None, None]
        for n, (u, t) in enumerate(plan):
            if n + AHEAD < len(plan):
                waiting.append(score(*plan[n + AHEAD]))
            raised = jnp.exp2(waiting[n]).astype(BF)
            b, j = indexes[u] // per_block, indexes[u] % per_block
            for m in range(2):
                at = pl.ds(pl.multiple_of((2 * j + m) * HEAD_DIM, HEAD_DIM), HEAD_DIM)
                lhs = jnp.concatenate(
                    [
                        values[low + b, at, t * fast_tile : (t + 1) * fast_tile],
                        jnp.ones((HEAD_DIM, fast_tile), BF),
                    ],
                    axis=0,
                )
                more = dot(lhs, raised[:, m * queries : (m + 1) * queries])
                summed[m] = more if t == 0 else summed[m] + more
                if t == tiles - 1:
                    out[b, at, :] = (summed[m][:HEAD_DIM] / summed[m][HEAD_DIM:]).astype(BF)
        return carry

    @pl.when(small[0] != 0)
    def _():
        lax.fori_loop(0, steps // UNROLL, several, 0)


def attend(small, keys, values, query, low, high, half):
    rows = keys.shape[1]
    queries = query.shape[1] // 2
    return pl.pallas_call(
        functools.partial(attend_kernel, low, high, half, min(TILE, rows)),
        out_shape=jax.ShapeDtypeStruct((high - low, LANES, queries), BF),
        in_specs=[SMEM] + [VMEM] * 3,
        out_specs=VMEM,
        scratch_shapes=[pltpu.VMEM((rows, 2 * queries), F32)] * 2,
        compiler_params=grant(14),
        cost_estimate=pl.CostEstimate(
            flops=4 * queries * rows * LANES * (high - low) * (LANES // HEAD_DIM),
            bytes_accessed=4 * rows * LANES * (high - low),
            transcendentals=0,
        ),
        name="attend",
    )(small, keys, values, query)


def mlp_kernel(blocks, members, patches, sends, chunk, half, pieces_of, params, kept, *refs):
    mixed = refs[:pieces_of]
    refs = refs[pieces_of:]
    projs = refs[:blocks]
    ups = refs[blocks : blocks + members]
    downs = refs[blocks + members : blocks + 2 * members]
    vectors = refs[blocks + 2 * members : blocks + 3 * members]
    results = refs[blocks + 3 * members : blocks + 3 * members + sends]
    proj, vector, final = refs[blocks + 3 * members + sends :]
    rows = kept.shape[1] // 2
    width = blocks * LANES
    share = width // members
    group = members // patches
    spots = arrival_order(patches, group)
    places = block_places(blocks, patches, group)
    for k in range(blocks):
        cols = pl.ds(pl.multiple_of(places[k] * LANES, LANES), LANES)
        for r in range(blocks):
            from_rows = pl.ds(pl.multiple_of(places[r] * LANES, LANES), LANES)
            proj[r * LANES : (r + 1) * LANES, cols] = projs[k][from_rows, :]
    for k in range(members):
        vector[spots[k]] = vectors[k][...]
    out_bias = jnp.concatenate([vector[k, :, :share] for k in range(members)], axis=1)
    down_bias = jnp.concatenate([vector[k, :, share : 2 * share] for k in range(members)], axis=1)
    root_half = 0.5 ** 0.5

    def one(i, carry):
        at = pl.ds(pl.multiple_of(i * chunk, chunk), chunk)
        attended = jnp.concatenate(
            [m[b, :, at] for m in mixed for b in range(m.shape[0])], axis=0
        )
        own = pl.ds(pl.multiple_of(half * rows + i * chunk, chunk), chunk)
        features = jnp.concatenate([kept[b, own, :] for b in range(blocks)], axis=1)
        residual = (features.astype(F32) + dot(attended, proj[...], (0, 0)) + out_bias).astype(BF)
        wide = residual.astype(F32)
        mean, scale = row_stats([wide], width)
        normed = ((wide - mean) * scale * params[2:3, :] + params[3:4, :]).astype(BF)
        total = wide + down_bias
        for k in range(members):
            spot = spots[k]
            before = dot(normed, ups[k][...]) + vector[spot, :, 2 * share :]
            hidden = (0.5 * before * (1.0 + lax.erf(before * root_half))).astype(BF)
            total = total + dot(hidden, downs[k][...])
        for b in range(blocks):
            final[b, at, :] = total[:, b * LANES : (b + 1) * LANES].astype(BF)
        return carry

    lax.fori_loop(0, rows // chunk, one, 0)
    if sends > 1:
        me = lax.axis_index("head")
        for k in range(sends):
            results[k][...] = final[lax.rem(me + k, sends)]
    else:
        results[0][...] = final[...]


def mlp(patches, half, params, mixed, kept, projs, ups, downs, vectors):
    blocks, rows = kept.shape[0], kept.shape[1] // 2
    members = len(ups)
    width = blocks * LANES
    hidden_here = ups[0].shape[1]
    sends = members if members == blocks else 1
    shape = (rows, LANES) if sends > 1 else (blocks, rows, LANES)
    chunk = min(256, rows)
    return pl.pallas_call(
        functools.partial(
            mlp_kernel, blocks, members, patches, sends, chunk, half, len(mixed)
        ),
        out_shape=[jax.ShapeDtypeStruct(shape, BF)] * sends,
        in_specs=[VMEM] * (2 + len(mixed) + blocks + 3 * members),
        out_specs=[VMEM] * sends,
        scratch_shapes=[
            pltpu.VMEM((width, width), BF),
            pltpu.VMEM((members, 1, vectors[0].shape[1]), F32),
            pltpu.VMEM((blocks, rows, LANES), BF),
        ],
        cost_estimate=pl.CostEstimate(
            flops=4 * rows * width * hidden_here * members,
            bytes_accessed=4 * width * hidden_here * members,
            transcendentals=0,
        ),
        compiler_params=grant(22),
        name="mlp",
    )(params, kept, *mixed, *projs, *ups, *downs, *vectors)


def shift(array, axis, size, step):
    return lax.ppermute(array, axis, [(i, (i + step) % size) for i in range(size)])


def exchange(blocks, axis, size):
    if size <= DIRECT:
        return [blocks[0]] + [shift(blocks[k], axis, size, k) for k in range(1, size)]
    me = lax.axis_index(axis)
    steps = jnp.arange(size, dtype=I32)
    stacked = jnp.stack(blocks)[(steps - me) % size]
    got = lax.all_to_all(stacked, axis, 0, 0, tiled=True)[(me - steps) % size]
    return [got[k] for k in range(size)]


def arrival_order(groups, group):
    member = lax.axis_index("head")
    return [
        lax.rem(member // group - k + groups, groups) * group
        + lax.rem(lax.rem(member, group) - j + group, group)
        for k in range(groups)
        for j in range(group)
    ]


def group_shift(array, groups, group, step):
    size = groups * group
    pairs = [(i, (i // group + step) % groups * group + i % group) for i in range(size)]
    return lax.ppermute(array, "head", pairs)


def member_shift(array, groups, group, step):
    size = groups * group
    pairs = [(i, i // group * group + (i % group + step) % group) for i in range(size)]
    return lax.ppermute(array, "head", pairs)


def gather_members(sources, groups, group):
    found = []
    for k in range(groups):
        moved = sources[k]
        if k > 0:
            moved = group_shift(moved, groups, group, k)
        for j in range(group):
            found.append(moved if j == 0 else member_shift(moved, groups, group, j))
    return found


def body(
    z_feat,
    shard_count,
    hilbert_rank,
    z_slot,
    ln1_gain,
    ln1_bias,
    w_qkv,
    w_out,
    b_out,
    ln2_gain,
    ln2_bias,
    w_up,
    b_up,
    w_down,
    b_down,
):
    shards = lax.axis_size("pts")
    members = lax.axis_size("head")
    rows_here = z_slot.shape[0]
    zone_rows, full_width = z_feat.shape
    width = w_out.shape[1]
    patches = rows_here // PATCH
    group = members // patches
    blocks = full_width // LANES
    skew_step = rows_here // (2 * shards * (shards - 1))
    cap = round_up(rows_here // shards + 2 * skew_step * (shards - 1), 32)
    member = lax.axis_index("head")

    def natural(found):
        spots = jnp.stack(arrival_order(patches, group)).astype(I32)
        stacked = jnp.stack(found)
        back = jnp.zeros((members,), I32).at[spots].set(jnp.arange(members, dtype=I32))
        stacked = jnp.take(stacked, back, axis=0)
        joined = jnp.concatenate([stacked[i] for i in range(members)], axis=-1)
        return [joined[..., b * LANES : (b + 1) * LANES] for b in range(blocks)]

    def everywhere(array):
        return gather_members([array] * patches, patches, group)

    qkv_found = everywhere(w_qkv)
    out_found = everywhere(w_out)
    up_found = everywhere(w_up)
    down_found = everywhere(w_down)
    vector = jnp.concatenate([b_out, b_down, b_up])[None, :]
    vectors = [vector]
    for step in range(1, members):
        k, j = step // group, step % group
        pairs = [
            (i, (i // group + k) % patches * group + (i % group + j) % group)
            for i in range(members)
        ]
        vectors.append(lax.ppermute(vector, "head", pairs))

    rank = hilbert_rank[None, :]
    if width % LANES == 0:
        z_source = z_feat
    else:
        z_source = lax.dynamic_slice_in_dim(z_feat, member * width, width, 1)
    *sends, place = pack(
        shard_count, rank, z_source, width % LANES == 0, width, shards, cap, rows_here
    )
    source = (z_slot // zone_rows).reshape(patches, PATCH, 1)
    pieces = jnp.sum((source == jnp.arange(shards, dtype=I32)).astype(I32), axis=1)
    params = jnp.stack([ln1_gain, ln1_bias, ln2_gain, ln2_bias])
    pieces, params = lax.optimization_barrier((pieces, params))
    arrived = exchange(sends, "pts", shards)
    arrived[0] = keep(arrived[0])
    patch_blocks = compact(pieces, arrived, patches, group)
    feats = gather_members(patch_blocks, patches, group)

    if width == LANES:
        qkv_blocks, out_blocks = qkv_found, out_found
    else:
        feats = natural(feats)
        qkv_blocks, out_blocks = natural(qkv_found), natural(out_found)

    keys, values, query, kept, small = project(feats, qkv_blocks, params, patches, group)

    def columns_back(half, mixed):
        results = mlp(
            patches, half, params, mixed, kept, out_blocks, up_found, down_found, vectors
        )
        if width != LANES:
            joined = jnp.concatenate([results[0][b] for b in range(blocks)], axis=1)
            results = [
                lax.dynamic_slice_in_dim(joined, (member + k) % members * width, width, 1)
                for k in range(members)
            ]
        return [results[0]] + [shift(results[k], "head", members, k) for k in range(1, members)]

    mixed = attend(small, keys, values, query, 0, blocks, 0)
    parts = columns_back(0, [mixed])
    middle = blocks // 2
    mixed_low = attend(small, keys, values, query, 0, middle, 1)
    outgoing = spread(pieces, parts, patches, members, shards, cap, 0)
    returned = exchange(outgoing, "pts", shards)
    mixed_high = attend(small, keys, values, query, middle, blocks, 1)
    parts = parts + columns_back(1, [mixed_low, mixed_high])
    outgoing = spread(pieces, parts, patches, members, shards, cap, 1)
    returned = returned + exchange(outgoing, "pts", shards)
    return unpack(shard_count, place, returned, zone_rows)


def solution(mesh):
    placed = (
        P(("tile", "pts"), None),
        P(("tile", "pts")),
        P(("tile", "pts")),
        P(("tile", "pts")),
        P(),
        P(),
        P(None, None, "head"),
        P(None, "head"),
        P("head"),
        P(),
        P(),
        P(None, "head"),
        P("head"),
        P("head", None),
        P("head"),
    )

    return jax.shard_map(
        body, mesh=mesh, in_specs=placed, out_specs=P(("tile", "pts"), "head"), check_vma=False
    )
```

```python
import functools
import math

import jax
import jax.numpy as jnp
from jax import lax
from jax.experimental import pallas as pl
from jax.experimental.pallas import tpu as pltpu
from jax.sharding import PartitionSpec as P

PATCH = 1024
HEAD_DIM = 16
LANES = 128
ROW_STEP = 128
TILE = 512
FAST_TILE = 256
AHEAD = 4
UNROLL = 4
SAFE_LOG2 = 96.0
DIRECT = 8
F32 = jnp.float32
BF = jnp.bfloat16
I32 = jnp.int32
SMEM = pl.BlockSpec(memory_space=pltpu.SMEM)
VMEM = pl.BlockSpec(memory_space=pltpu.VMEM)
ANY = pl.BlockSpec(memory_space=pl.ANY)


def dot(lhs, rhs, dims=(1, 0)):
    return lax.dot_general(
        lhs, rhs, (((dims[0],), (dims[1],)), ((), ())), preferred_element_type=F32
    )


def exact_dot(values, choice):
    high = jnp.floor(values * (1.0 / LANES))
    low = values - high * LANES
    return dot(high.astype(BF), choice) * LANES + dot(low.astype(BF), choice)


def round_up(value, unit):
    return (value + unit - 1) // unit * unit


def grant(mib):
    return pltpu.CompilerParams(vmem_limit_bytes=mib * 2 ** 20)


def convert_rows(source, source_at, target, target_at, rows):
    step = math.gcd(rows, 128)

    def one(i, carry):
        at = pl.multiple_of(i * step, step)
        target[pl.ds(target_at + at, step), :] = source[pl.ds(source_at + at, step), :].astype(
            target.dtype
        )
        return carry

    lax.fori_loop(0, rows // step, one, 0)


def pack_kernel(
    shards, cap, rows_here, columns_at, held, rank, z_feat, *refs
):
    sends = refs[:shards]
    place_out = refs[shards]
    place, place_smem, ranks_full, narrow, wide, packed, sems = refs[shards + 1 :]
    here, member, count = lax.axis_index("pts"), lax.axis_index("head"), held[0]
    slots = place.shape[1]
    zone_rows, width = narrow.shape
    if columns_at:
        column = pl.multiple_of(member * width, width)
        source = z_feat.at[:, pl.ds(column, width)]
    else:
        source = z_feat
    feature_copy = pltpu.make_async_copy(source, narrow, sems.at[0])
    feature_copy.start()

    grid_rows = shards * rows_here // LANES
    block = rows_here // LANES
    ranks_full[:, :zone_rows] = rank[...]
    ranks = ranks_full[...]
    occupied = lax.broadcasted_iota(I32, (1, slots), 1) < count
    major = jnp.where(occupied, ranks // LANES, -1)
    minor = ranks % LANES
    hot_major = (lax.broadcasted_iota(I32, (grid_rows, slots), 0) == major).astype(BF)
    hot_minor = (lax.broadcasted_iota(I32, (LANES, slots), 0) == minor).astype(BF)
    members = dot(hot_minor, hot_major, (1, 1)).astype(BF)
    minor_r = lax.broadcasted_iota(I32, (LANES, LANES), 0)
    minor_c = lax.broadcasted_iota(I32, (LANES, LANES), 1)
    below = (minor_c < minor_r).astype(BF)
    ones = jnp.ones((LANES, LANES), BF)
    major_r = lax.broadcasted_iota(I32, (grid_rows, grid_rows), 0)
    major_c = lax.broadcasted_iota(I32, (grid_rows, grid_rows), 1)
    group = PATCH // LANES
    same_group = major_r // group == major_c // group
    earlier_row = (same_group & (major_r < major_c)).astype(BF)
    earlier_group = (
        (major_r // block == major_c // block)
        & (major_r // group < major_c // group)
        & (major_r % group == 0)
    ).astype(BF)
    before = dot(below, members) + dot(ones, dot(members, earlier_row).astype(BF))
    total = dot(ones, dot(members, same_group.astype(BF)).astype(BF))
    first_half = jnp.floor(total * 0.5)
    second_half = total - first_half
    first_base = exact_dot(first_half, earlier_group)
    second_base = exact_dot(second_half, earlier_group)
    target = lax.broadcasted_iota(I32, (LANES, grid_rows), 1) // block * cap
    spot = target.astype(F32) + jnp.where(
        before < first_half,
        first_base + before,
        second_base + before - first_half + cap // 2,
    )
    spread_out = exact_dot(spot, hot_major)
    found = jnp.sum(jnp.where(hot_minor > 0, spread_out, 0.0), axis=0, keepdims=True)
    place[...] = jnp.where(occupied, found.astype(I32), shards * cap)
    to_smem = pltpu.make_async_copy(place, place_smem, sems.at[1])
    to_smem.start()
    to_out = pltpu.make_async_copy(place, place_out, sems.at[2])
    to_out.start()
    feature_copy.wait()
    whole_rows = zone_rows // LANES * LANES
    convert_rows(narrow, 0, wide, 0, whole_rows)
    if whole_rows < zone_rows:
        wide[pl.ds(whole_rows, zone_rows - whole_rows), :] = narrow[
            pl.ds(whole_rows, zone_rows - whole_rows), :
        ].astype(F32)
    to_smem.wait()

    stride = slots // ROW_STEP

    def place_rows(i, carry):
        for k in range(ROW_STEP):
            target = place_smem.at[:, pl.ds(k * stride, stride)][0, i]
            packed[pl.ds(target, 1), :] = wide.at[pl.ds(k * stride, stride)][pl.ds(i, 1), :]
        return carry

    lax.fori_loop(0, stride, place_rows, 0)
    for k in range(shards):
        at = pl.multiple_of(lax.rem(here + k, shards) * cap, cap)
        convert_rows(packed, at, sends[k], 0, cap)
    to_out.wait()


def pack(held, rank, z_feat, columns_at, width, shards, cap, rows_here):
    zone_rows = z_feat.shape[0]
    slots = round_up(zone_rows, LANES)
    return pl.pallas_call(
        functools.partial(pack_kernel, shards, cap, rows_here, columns_at),
        out_shape=[jax.ShapeDtypeStruct((cap, width), BF)] * shards
        + [jax.ShapeDtypeStruct((1, slots), I32)],
        in_specs=[SMEM, VMEM, ANY],
        out_specs=[VMEM] * shards + [ANY],
        scratch_shapes=[
            pltpu.VMEM((1, slots), I32),
            pltpu.SMEM((1, slots), I32),
            pltpu.VMEM((1, slots), I32),
            pltpu.VMEM((zone_rows, width), BF),
            pltpu.VMEM((slots, width), F32),
            pltpu.VMEM((shards * cap + 8, width), F32),
            pltpu.SemaphoreType.DMA((3,)),
        ],
        name="pack",
    )(held, rank, z_feat)


def keep_kernel(block, out):
    out[...] = block[...]


def keep(block):
    return pl.pallas_call(
        keep_kernel,
        out_shape=jax.ShapeDtypeStruct(block.shape, block.dtype),
        in_specs=[VMEM],
        out_specs=VMEM,
        compiler_params=grant(2),
        name="keep",
    )(block)


def move_segment(source, source_at, target, target_at, length):
    def one(i, carry):
        for k in range(4):
            target[pl.ds(target_at + i * 32 + k * 8, 8), :] = source[
                pl.ds(source_at + i * 32 + k * 8, 8), :
            ]
        return carry

    lax.fori_loop(0, (length + 31) // 32, one, 0)


def segment_table(pieces, patches, shards, cap):
    packed_at, patch_at, lengths = {}, {}, {}
    for s in range(shards):
        ends = [s * cap, s * cap + cap // 2]
        for p in range(patches):
            count = pieces[p, s]
            lengths[0, p, s] = lax.shift_right_logical(count, 1)
            lengths[1, p, s] = count - lengths[0, p, s]
            for half in range(2):
                packed_at[half, p, s] = ends[half]
                ends[half] = ends[half] + lengths[half, p, s]
    for p in range(patches):
        at = p * PATCH
        for half in range(2):
            for s in range(shards):
                patch_at[half, p, s] = at
                at = at + lengths[half, p, s]
    return packed_at, patch_at, lengths


def compact_kernel(shards, patches, group, cap, pieces, *refs):
    blocks = refs[:shards]
    outs = refs[shards : shards + patches]
    wide, patch_rows = refs[shards + patches :]
    here, member = lax.axis_index("pts"), lax.axis_index("head")
    for k in range(shards):
        at = pl.multiple_of(lax.rem(here - k + shards, shards) * cap, cap)
        convert_rows(blocks[k], 0, wide, at, cap)
    packed_at, patch_at, lengths = segment_table(pieces, patches, shards, cap)
    for p in range(patches):
        for half in range(2):
            for s in range(shards):
                key = half, p, s
                move_segment(wide, packed_at[key], patch_rows, patch_at[key], lengths[key])
    own_group = member // group
    for k in range(patches):
        at = pl.multiple_of(lax.rem(own_group + k, patches) * PATCH, PATCH)
        convert_rows(patch_rows, at, outs[k], 0, PATCH)


def compact(pieces, blocks, patches, group):
    shards = len(blocks)
    cap, width = blocks[0].shape
    return pl.pallas_call(
        functools.partial(compact_kernel, shards, patches, group, cap),
        out_shape=[jax.ShapeDtypeStruct((PATCH, width), BF)] * patches,
        in_specs=[SMEM] + [VMEM] * shards,
        out_specs=[VMEM] * patches,
        scratch_shapes=[
            pltpu.VMEM((shards * cap + 64, width), F32),
            pltpu.VMEM((patches * PATCH + 64, width), F32),
        ],
        compiler_params=grant(12),
        name="compact",
    )(pieces, *blocks)


def spread_kernel(shards, patches, members, cap, half, pieces, *refs):
    given = members * (half + 1)
    blocks = refs[:given]
    sends = refs[given : given + shards]
    patch_rows, wide = refs[given + shards :]
    here, member = lax.axis_index("pts"), lax.axis_index("head")
    group = members // patches
    part_rows = blocks[0].shape[0]
    for phase in range(half + 1):
        for k in range(members):
            source = lax.rem(member - k + members, members)
            at = source // group * PATCH + phase * (PATCH // 2)
            at = pl.multiple_of(at + lax.rem(source, group) * part_rows, part_rows)
            convert_rows(blocks[phase * members + k], 0, patch_rows, at, part_rows)
    packed_at, patch_at, lengths = segment_table(pieces, patches, shards, cap)
    size = cap // 2
    for s in range(shards):
        for p in range(patches):
            key = half, p, s
            move_segment(
                patch_rows,
                patch_at[key],
                wide,
                packed_at[key] - s * cap - half * size + s * size,
                lengths[key],
            )
    for k in range(shards):
        at = pl.multiple_of(lax.rem(here + k, shards) * size, size)
        convert_rows(wide, at, sends[k], 0, size)


def spread(pieces, blocks, patches, members, shards, cap, half):
    width = blocks[0].shape[1]
    return pl.pallas_call(
        functools.partial(spread_kernel, shards, patches, members, cap, half),
        out_shape=[jax.ShapeDtypeStruct((cap // 2, width), BF)] * shards,
        in_specs=[SMEM] + [VMEM] * len(blocks),
        out_specs=[VMEM] * shards,
        scratch_shapes=[
            pltpu.VMEM((patches * PATCH + 64, width), F32),
            pltpu.VMEM((shards * cap // 2 + 64, width), F32),
        ],
        compiler_params=grant(12),
        name="spread",
    )(pieces, *blocks)


def unpack_kernel(shards, cap, held, place, *refs):
    blocks = refs[: 2 * shards]
    out = refs[2 * shards]
    wide, picked = refs[2 * shards + 1 :]
    here, count = lax.axis_index("pts"), held[0]
    zone_rows, width = out.shape
    size = cap // 2
    for half in range(2):
        for k in range(shards):
            at = lax.rem(here - k + shards, shards) * cap + half * size
            convert_rows(blocks[half * shards + k], 0, wide, pl.multiple_of(at, size), size)

    stride = picked.shape[0] // ROW_STEP

    def pick_rows(i, carry):
        for k in range(ROW_STEP):
            source = place.at[:, pl.ds(k * stride, stride)][0, i]
            picked.at[pl.ds(k * stride, stride)][pl.ds(i, 1), :] = wide[pl.ds(source, 1), :]
        return carry

    lax.fori_loop(0, stride, pick_rows, 0)

    def masked(at, rows):
        slot = at + lax.broadcasted_iota(I32, (rows, width), 0)
        out[pl.ds(at, rows), :] = jnp.where(slot < count, picked[pl.ds(at, rows), :], 0.0).astype(
            BF
        )

    def one(i, carry):
        masked(pl.multiple_of(i * LANES, LANES), LANES)
        return carry

    whole_rows = zone_rows // LANES * LANES
    lax.fori_loop(0, whole_rows // LANES, one, 0)
    if whole_rows < zone_rows:
        masked(whole_rows, zone_rows - whole_rows)


def unpack(held, place, blocks, zone_rows):
    shards = len(blocks) // 2
    size, width = blocks[0].shape
    cap = 2 * size
    slots = place.shape[1]
    return pl.pallas_call(
        functools.partial(unpack_kernel, shards, cap),
        out_shape=jax.ShapeDtypeStruct((zone_rows, width), BF),
        in_specs=[SMEM, SMEM] + [VMEM] * (2 * shards),
        out_specs=VMEM,
        scratch_shapes=[
            pltpu.VMEM((shards * cap + 8, width), F32),
            pltpu.VMEM((slots, width), F32),
        ],
        compiler_params=grant(14),
        name="unpack",
    )(held, place, *blocks)


def row_stats(parts, width):
    total = jnp.sum(sum(parts[1:], parts[0]), axis=1, keepdims=True)
    squares = jnp.sum(
        sum((x * x for x in parts[1:]), parts[0] * parts[0]), axis=1, keepdims=True
    )
    mean = total / width
    var = squares / width - mean * mean
    return mean, lax.rsqrt(var + 1e-05)


def block_places(blocks, patches, group):
    if blocks == patches * group:
        return arrival_order(patches, group)
    return list(range(blocks))


def project_kernel(blocks, patches, group, params, *refs):
    feats = refs[:blocks]
    weights = refs[blocks : 2 * blocks]
    keys, values, query, kept, small, normed = refs[2 * blocks :]
    rows = feats[0].shape[0]
    width = blocks * LANES
    queries = query.shape[1] // 2
    places = block_places(blocks, patches, group)
    part = lax.rem(lax.axis_index("head"), group)

    def norm(i, carry):
        at = pl.ds(pl.multiple_of(i * 128, 128), 128)
        parts = [feats[b][at, :].astype(F32) for b in range(blocks)]
        mean, scale = row_stats(parts, width)
        for b in range(blocks):
            cols = pl.ds(pl.multiple_of(places[b] * LANES, LANES), LANES)
            normed[at, cols] = (
                (parts[b] - mean) * scale * params[0:1, cols] + params[1:2, cols]
            ).astype(BF)
        return carry

    lax.fori_loop(0, rows // 128, norm, 0, unroll=2)
    starts = [
        pl.multiple_of(part * queries + half * (rows // 2), queries) for half in range(2)
    ]
    for b in range(blocks):
        for half in range(2):
            kept[places[b], pl.ds(half * queries, queries), :] = feats[b][
                pl.ds(starts[half], queries), :
            ]
    score_scale = HEAD_DIM ** (-0.5) * math.log2(math.e)
    pair_of = 2 if blocks % 2 == 0 else 1
    span = pair_of * LANES
    head_r = lax.broadcasted_iota(I32, (span, span), 0) // HEAD_DIM
    head_c = lax.broadcasted_iota(I32, (span, span), 1) // HEAD_DIM
    same_head = (head_r == head_c).astype(BF)

    def largest(found):
        return jnp.max(jnp.abs(found), axis=0, keepdims=True)

    def pair_weight(b, kind):
        return jnp.concatenate([weights[c][kind] for c in range(b, b + pair_of)], axis=1)

    worst = None
    for b in range(0, blocks, pair_of):
        key_most, query_most = None, None
        k_weight, q_weight = pair_weight(b, 1), pair_weight(b, 0)
        for half in range(2):
            at = pl.ds(starts[half], queries)
            found = dot(normed[at, :], q_weight) * score_scale
            most = largest(found)
            query_most = most if half == 0 else jnp.maximum(query_most, most)
            for n in range(pair_of):
                query[b + n, pl.ds(half * queries, queries), :] = found[
                    :, n * LANES : (n + 1) * LANES
                ].astype(BF)
        for i in range(rows // 256):
            at = pl.ds(i * 256, 256)
            found = dot(normed[at, :], k_weight)
            most = largest(found)
            key_most = most if i == 0 else jnp.maximum(key_most, most)
            for n in range(pair_of):
                keys[b + n, at, :] = found[:, n * LANES : (n + 1) * LANES].astype(BF)
        product = jnp.broadcast_to(key_most * query_most, (8, span)).astype(BF)
        bound = dot(product, same_head)
        worst = bound if b == 0 else jnp.maximum(worst, bound)
    is_small = (jnp.max(worst) * 1.05 < SAFE_LOG2).astype(I32)
    for b in range(0, blocks, pair_of):
        turned = dot(pair_weight(b, 2), normed[...], (0, 1))
        for n in range(pair_of):
            values[b + n] = turned[n * LANES : (n + 1) * LANES].astype(BF)
    small[0] = is_small


def project(feats, weights, params, patches, group):
    blocks = len(feats)
    rows = feats[0].shape[0]
    width = weights[0].shape[1]
    own = jax.ShapeDtypeStruct((blocks, rows // group, LANES), BF)
    return pl.pallas_call(
        functools.partial(project_kernel, blocks, patches, group),
        out_shape=[
            jax.ShapeDtypeStruct((blocks, rows, LANES), BF),
            jax.ShapeDtypeStruct((blocks, LANES, rows), BF),
            own,
            own,
            jax.ShapeDtypeStruct((1,), I32),
        ],
        in_specs=[VMEM] * (1 + 2 * blocks),
        out_specs=[VMEM] * 4 + [SMEM],
        scratch_shapes=[pltpu.VMEM((rows, width), BF)],
        compiler_params=grant(14),
        cost_estimate=pl.CostEstimate(
            flops=6 * rows * width * width, bytes_accessed=8 * rows * width, transcendentals=0
        ),
        name="project",
    )(params, *feats, *weights)


def attend_kernel(low, high, half, tile, small, keys, values, query, out, even, odd):
    rows = keys.shape[1]
    queries = query.shape[1] // 2
    lane = lax.broadcasted_iota(I32, (1, LANES), 1)
    per_block = LANES // HEAD_DIM // 2
    steps = (high - low) * per_block

    def select(index):
        b, j = low + index // per_block, index % per_block
        own = query[b, pl.ds(half * queries, queries), :]
        zero = jnp.zeros((), BF)
        return jnp.concatenate(
            [jnp.where(lane // HEAD_DIM == 2 * j + n, own, zero) for n in range(2)], axis=0
        )

    def step(index, scores, top, coming, next_scores):
        b, j = index // per_block, index % per_block
        at = [
            pl.ds(pl.multiple_of((2 * j + n) * HEAD_DIM, HEAD_DIM), HEAD_DIM) for n in range(2)
        ]
        own = select(coming)
        next_keys = low + coming // per_block
        summed, next_top = [None, None], None
        for i in range(rows // tile):
            part = pl.ds(i * tile, tile)
            found = dot(keys[next_keys, part, :], own, (1, 1))
            next_scores[part, :] = found
            most = jnp.max(found, axis=0, keepdims=True)
            next_top = most if i == 0 else jnp.maximum(next_top, most)
            if top is not None:
                raised = jnp.exp2(scores[part, :] - top).astype(BF)
                for n in range(2):
                    lhs = jnp.concatenate(
                        [
                            values[low + b, at[n], i * tile : (i + 1) * tile],
                            jnp.ones((HEAD_DIM, tile), BF),
                        ],
                        axis=0,
                    )
                    more = dot(lhs, raised[:, n * queries : (n + 1) * queries])
                    summed[n] = more if i == 0 else summed[n] + more
        if top is not None:
            for n in range(2):
                out[b, at[n], :] = (summed[n][:HEAD_DIM] / summed[n][HEAD_DIM:]).astype(BF)
        return next_top

    def pair(i, top):
        once = jnp.minimum(i, 0) + 1
        next_top = lax.fori_loop(
            0, once, lambda _, most: step(2 * i, even, top, 2 * i + 1, odd), top
        )
        following = jnp.minimum(2 * i + 2, steps - 1)
        return lax.fori_loop(
            0, once, lambda _, most: step(2 * i + 1, odd, next_top, following, even), next_top
        )

    @pl.when(small[0] == 0)
    def _():
        lax.fori_loop(0, steps // 2, pair, step(0, None, None, 0, even))

    fast_tile = min(FAST_TILE, rows)
    tiles = rows // fast_tile

    def several(i, carry):
        indexes = [UNROLL * i + u for u in range(UNROLL)]
        plan = [(u, t) for u in range(UNROLL) for t in range(tiles)]
        owns = [None] * UNROLL

        def score(u, t):
            if t == 0:
                owns[u] = select(indexes[u])
            part = pl.ds(t * fast_tile, fast_tile)
            return dot(keys[low + indexes[u] // per_block, part, :], owns[u], (1, 1))

        waiting = [score(*plan[n]) for n in range(min(AHEAD, len(plan)))]
        summed = [None, None]
        for n, (u, t) in enumerate(plan):
            if n + AHEAD < len(plan):
                waiting.append(score(*plan[n + AHEAD]))
            raised = jnp.exp2(waiting[n]).astype(BF)
            b, j = indexes[u] // per_block, indexes[u] % per_block
            for m in range(2):
                at = pl.ds(pl.multiple_of((2 * j + m) * HEAD_DIM, HEAD_DIM), HEAD_DIM)
                lhs = jnp.concatenate(
                    [
                        values[low + b, at, t * fast_tile : (t + 1) * fast_tile],
                        jnp.ones((HEAD_DIM, fast_tile), BF),
                    ],
                    axis=0,
                )
                more = dot(lhs, raised[:, m * queries : (m + 1) * queries])
                summed[m] = more if t == 0 else summed[m] + more
                if t == tiles - 1:
                    out[b, at, :] = (summed[m][:HEAD_DIM] / summed[m][HEAD_DIM:]).astype(BF)
        return carry

    @pl.when(small[0] != 0)
    def _():
        lax.fori_loop(0, steps // UNROLL, several, 0)


def attend(small, keys, values, query, low, high, half):
    rows = keys.shape[1]
    queries = query.shape[1] // 2
    return pl.pallas_call(
        functools.partial(attend_kernel, low, high, half, min(TILE, rows)),
        out_shape=jax.ShapeDtypeStruct((high - low, LANES, queries), BF),
        in_specs=[SMEM] + [VMEM] * 3,
        out_specs=VMEM,
        scratch_shapes=[pltpu.VMEM((rows, 2 * queries), F32)] * 2,
        compiler_params=grant(14),
        cost_estimate=pl.CostEstimate(
            flops=4 * queries * rows * LANES * (high - low) * (LANES // HEAD_DIM),
            bytes_accessed=4 * rows * LANES * (high - low),
            transcendentals=0,
        ),
        name="attend",
    )(small, keys, values, query)


def mlp_kernel(blocks, members, patches, sends, chunk, half, pieces_of, params, kept, *refs):
    mixed = refs[:pieces_of]
    refs = refs[pieces_of:]
    projs = refs[:blocks]
    ups = refs[blocks : blocks + members]
    downs = refs[blocks + members : blocks + 2 * members]
    vectors = refs[blocks + 2 * members : blocks + 3 * members]
    results = refs[blocks + 3 * members : blocks + 3 * members + sends]
    proj, vector, final = refs[blocks + 3 * members + sends :]
    rows = kept.shape[1] // 2
    width = blocks * LANES
    share = width // members
    group = members // patches
    spots = arrival_order(patches, group)
    places = block_places(blocks, patches, group)
    for k in range(blocks):
        cols = pl.ds(pl.multiple_of(places[k] * LANES, LANES), LANES)
        for r in range(blocks):
            from_rows = pl.ds(pl.multiple_of(places[r] * LANES, LANES), LANES)
            proj[r * LANES : (r + 1) * LANES, cols] = projs[k][from_rows, :]
    for k in range(members):
        vector[spots[k]] = vectors[k][...]
    out_bias = jnp.concatenate([vector[k, :, :share] for k in range(members)], axis=1)
    down_bias = jnp.concatenate([vector[k, :, share : 2 * share] for k in range(members)], axis=1)
    root_half = 0.5 ** 0.5

    def one(i, carry):
        at = pl.ds(pl.multiple_of(i * chunk, chunk), chunk)
        attended = jnp.concatenate(
            [m[b, :, at] for m in mixed for b in range(m.shape[0])], axis=0
        )
        own = pl.ds(pl.multiple_of(half * rows + i * chunk, chunk), chunk)
        features = jnp.concatenate([kept[b, own, :] for b in range(blocks)], axis=1)
        residual = (features.astype(F32) + dot(attended, proj[...], (0, 0)) + out_bias).astype(BF)
        wide = residual.astype(F32)
        mean, scale = row_stats([wide], width)
        normed = ((wide - mean) * scale * params[2:3, :] + params[3:4, :]).astype(BF)
        total = wide + down_bias
        for k in range(members):
            spot = spots[k]
            before = dot(normed, ups[k][...]) + vector[spot, :, 2 * share :]
            hidden = (0.5 * before * (1.0 + lax.erf(before * root_half))).astype(BF)
            total = total + dot(hidden, downs[k][...])
        for b in range(blocks):
            final[b, at, :] = total[:, b * LANES : (b + 1) * LANES].astype(BF)
        return carry

    lax.fori_loop(0, rows // chunk, one, 0)
    if sends > 1:
        me = lax.axis_index("head")
        for k in range(sends):
            results[k][...] = final[lax.rem(me + k, sends)]
    else:
        results[0][...] = final[...]


def mlp(patches, half, params, mixed, kept, projs, ups, downs, vectors):
    blocks, rows = kept.shape[0], kept.shape[1] // 2
    members = len(ups)
    width = blocks * LANES
    hidden_here = ups[0].shape[1]
    sends = members if members == blocks else 1
    shape = (rows, LANES) if sends > 1 else (blocks, rows, LANES)
    chunk = min(256, rows)
    return pl.pallas_call(
        functools.partial(
            mlp_kernel, blocks, members, patches, sends, chunk, half, len(mixed)
        ),
        out_shape=[jax.ShapeDtypeStruct(shape, BF)] * sends,
        in_specs=[VMEM] * (2 + len(mixed) + blocks + 3 * members),
        out_specs=[VMEM] * sends,
        scratch_shapes=[
            pltpu.VMEM((width, width), BF),
            pltpu.VMEM((members, 1, vectors[0].shape[1]), F32),
            pltpu.VMEM((blocks, rows, LANES), BF),
        ],
        cost_estimate=pl.CostEstimate(
            flops=4 * rows * width * hidden_here * members,
            bytes_accessed=4 * width * hidden_here * members,
            transcendentals=0,
        ),
        compiler_params=grant(22),
        name="mlp",
    )(params, kept, *mixed, *projs, *ups, *downs, *vectors)


def shift(array, axis, size, step):
    return lax.ppermute(array, axis, [(i, (i + step) % size) for i in range(size)])


def exchange(blocks, axis, size):
    if size <= DIRECT:
        return [blocks[0]] + [shift(blocks[k], axis, size, k) for k in range(1, size)]
    me = lax.axis_index(axis)
    steps = jnp.arange(size, dtype=I32)
    stacked = jnp.stack(blocks)[(steps - me) % size]
    got = lax.all_to_all(stacked, axis, 0, 0, tiled=True)[(me - steps) % size]
    return [got[k] for k in range(size)]


def arrival_order(groups, group):
    member = lax.axis_index("head")
    return [
        lax.rem(member // group - k + groups, groups) * group
        + lax.rem(lax.rem(member, group) - j + group, group)
        for k in range(groups)
        for j in range(group)
    ]


def group_shift(array, groups, group, step):
    size = groups * group
    pairs = [(i, (i // group + step) % groups * group + i % group) for i in range(size)]
    return lax.ppermute(array, "head", pairs)


def member_shift(array, groups, group, step):
    size = groups * group
    pairs = [(i, i // group * group + (i % group + step) % group) for i in range(size)]
    return lax.ppermute(array, "head", pairs)


def gather_members(sources, groups, group):
    found = []
    for k in range(groups):
        moved = sources[k]
        if k > 0:
            moved = group_shift(moved, groups, group, k)
        for j in range(group):
            found.append(moved if j == 0 else member_shift(moved, groups, group, j))
    return found


def body(
    z_feat,
    shard_count,
    hilbert_rank,
    z_slot,
    ln1_gain,
    ln1_bias,
    w_qkv,
    w_out,
    b_out,
    ln2_gain,
    ln2_bias,
    w_up,
    b_up,
    w_down,
    b_down,
):
    shards = lax.axis_size("pts")
    members = lax.axis_size("head")
    rows_here = z_slot.shape[0]
    zone_rows, full_width = z_feat.shape
    width = w_out.shape[1]
    patches = rows_here // PATCH
    group = members // patches
    blocks = full_width // LANES
    skew_step = rows_here // (2 * shards * (shards - 1))
    cap = round_up(rows_here // shards + 2 * skew_step * (shards - 1), 32)
    member = lax.axis_index("head")

    def natural(found):
        spots = jnp.stack(arrival_order(patches, group)).astype(I32)
        stacked = jnp.stack(found)
        back = jnp.zeros((members,), I32).at[spots].set(jnp.arange(members, dtype=I32))
        stacked = jnp.take(stacked, back, axis=0)
        joined = jnp.concatenate([stacked[i] for i in range(members)], axis=-1)
        return [joined[..., b * LANES : (b + 1) * LANES] for b in range(blocks)]

    def everywhere(array):
        return gather_members([array] * patches, patches, group)

    qkv_found = everywhere(w_qkv)
    out_found = everywhere(w_out)
    up_found = everywhere(w_up)
    down_found = everywhere(w_down)
    vector = jnp.concatenate([b_out, b_down, b_up])[None, :]
    vectors = [vector]
    for step in range(1, members):
        k, j = step // group, step % group
        pairs = [
            (i, (i // group + k) % patches * group + (i % group + j) % group)
            for i in range(members)
        ]
        vectors.append(lax.ppermute(vector, "head", pairs))

    rank = hilbert_rank[None, :]
    if width % LANES == 0:
        z_source = z_feat
    else:
        z_source = lax.dynamic_slice_in_dim(z_feat, member * width, width, 1)
    *sends, place = pack(
        shard_count, rank, z_source, width % LANES == 0, width, shards, cap, rows_here
    )
    source = (z_slot // zone_rows).reshape(patches, PATCH, 1)
    pieces = jnp.sum((source == jnp.arange(shards, dtype=I32)).astype(I32), axis=1)
    params = jnp.stack([ln1_gain, ln1_bias, ln2_gain, ln2_bias])
    pieces, params = lax.optimization_barrier((pieces, params))
    arrived = exchange(sends, "pts", shards)
    arrived[0] = keep(arrived[0])
    patch_blocks = compact(pieces, arrived, patches, group)
    feats = gather_members(patch_blocks, patches, group)

    if width == LANES:
        qkv_blocks, out_blocks = qkv_found, out_found
    else:
        feats = natural(feats)
        qkv_blocks, out_blocks = natural(qkv_found), natural(out_found)

    keys, values, query, kept, small = project(feats, qkv_blocks, params, patches, group)

    def columns_back(half, mixed):
        results = mlp(
            patches, half, params, mixed, kept, out_blocks, up_found, down_found, vectors
        )
        if width != LANES:
            joined = jnp.concatenate([results[0][b] for b in range(blocks)], axis=1)
            results = [
                lax.dynamic_slice_in_dim(joined, (member + k) % members * width, width, 1)
                for k in range(members)
            ]
        return [results[0]] + [shift(results[k], "head", members, k) for k in range(1, members)]

    mixed = attend(small, keys, values, query, 0, blocks, 0)
    parts = columns_back(0, [mixed])
    middle = blocks // 2
    mixed_low = attend(small, keys, values, query, 0, middle, 1)
    outgoing = spread(pieces, parts, patches, members, shards, cap, 0)
    returned = exchange(outgoing, "pts", shards)
    mixed_high = attend(small, keys, values, query, middle, blocks, 1)
    parts = parts + columns_back(1, [mixed_low, mixed_high])
    outgoing = spread(pieces, parts, patches, members, shards, cap, 1)
    returned = returned + exchange(outgoing, "pts", shards)
    return unpack(shard_count, place, returned, zone_rows)


def solution(mesh):
    placed = (
        P(("tile", "pts"), None),
        P(("tile", "pts")),
        P(("tile", "pts")),
        P(("tile", "pts")),
        P(),
        P(),
        P(None, None, "head"),
        P(None, "head"),
        P("head"),
        P(),
        P(),
        P(None, "head"),
        P("head"),
        P("head", None),
        P("head"),
    )

    return jax.shard_map(
        body, mesh=mesh, in_specs=placed, out_specs=P(("tile", "pts"), "head"), check_vma=False
    )
```

```python
import functools
import math

import jax
import jax.numpy as jnp
from jax import lax
from jax.experimental import pallas as pl
from jax.experimental.pallas import tpu as pltpu
from jax.sharding import PartitionSpec as P

PATCH = 1024
HEAD_DIM = 16
LANES = 128
ROW_STEP = 128
TILE = 512
FAST_TILE = 256
AHEAD = 4
UNROLL = 4
SAFE_LOG2 = 96.0
DIRECT = 8
F32 = jnp.float32
BF = jnp.bfloat16
I32 = jnp.int32
SMEM = pl.BlockSpec(memory_space=pltpu.SMEM)
VMEM = pl.BlockSpec(memory_space=pltpu.VMEM)
ANY = pl.BlockSpec(memory_space=pl.ANY)


def dot(lhs, rhs, dims=(1, 0)):
    return lax.dot_general(
        lhs, rhs, (((dims[0],), (dims[1],)), ((), ())), preferred_element_type=F32
    )


def exact_dot(values, choice):
    high = jnp.floor(values * (1.0 / LANES))
    low = values - high * LANES
    return dot(high.astype(BF), choice) * LANES + dot(low.astype(BF), choice)


def round_up(value, unit):
    return (value + unit - 1) // unit * unit


def grant(mib):
    return pltpu.CompilerParams(vmem_limit_bytes=mib * 2 ** 20)


def convert_rows(source, source_at, target, target_at, rows):
    step = math.gcd(rows, 128)

    def one(i, carry):
        at = pl.multiple_of(i * step, step)
        target[pl.ds(target_at + at, step), :] = source[pl.ds(source_at + at, step), :].astype(
            target.dtype
        )
        return carry

    lax.fori_loop(0, rows // step, one, 0)


def pack_kernel(
    shards, cap, rows_here, columns_at, held, rank, z_feat, *refs
):
    sends = refs[:shards]
    place_out = refs[shards]
    place, place_smem, ranks_full, narrow, wide, packed, sems = refs[shards + 1 :]
    here, member, count = lax.axis_index("pts"), lax.axis_index("head"), held[0]
    slots = place.shape[1]
    zone_rows, width = narrow.shape
    if columns_at:
        column = pl.multiple_of(member * width, width)
        source = z_feat.at[:, pl.ds(column, width)]
    else:
        source = z_feat
    feature_copy = pltpu.make_async_copy(source, narrow, sems.at[0])
    feature_copy.start()

    grid_rows = shards * rows_here // LANES
    block = rows_here // LANES
    ranks_full[:, :zone_rows] = rank[...]
    ranks = ranks_full[...]
    occupied = lax.broadcasted_iota(I32, (1, slots), 1) < count
    major = jnp.where(occupied, ranks // LANES, -1)
    minor = ranks % LANES
    hot_major = (lax.broadcasted_iota(I32, (grid_rows, slots), 0) == major).astype(BF)
    hot_minor = (lax.broadcasted_iota(I32, (LANES, slots), 0) == minor).astype(BF)
    members = dot(hot_minor, hot_major, (1, 1)).astype(BF)
    minor_r = lax.broadcasted_iota(I32, (LANES, LANES), 0)
    minor_c = lax.broadcasted_iota(I32, (LANES, LANES), 1)
    below = (minor_c < minor_r).astype(BF)
    ones = jnp.ones((LANES, LANES), BF)
    major_r = lax.broadcasted_iota(I32, (grid_rows, grid_rows), 0)
    major_c = lax.broadcasted_iota(I32, (grid_rows, grid_rows), 1)
    group = PATCH // LANES
    same_group = major_r // group == major_c // group
    earlier_row = (same_group & (major_r < major_c)).astype(BF)
    earlier_group = (
        (major_r // block == major_c // block)
        & (major_r // group < major_c // group)
        & (major_r % group == 0)
    ).astype(BF)
    before = dot(below, members) + dot(ones, dot(members, earlier_row).astype(BF))
    total = dot(ones, dot(members, same_group.astype(BF)).astype(BF))
    first_half = jnp.floor(total * 0.5)
    second_half = total - first_half
    first_base = exact_dot(first_half, earlier_group)
    second_base = exact_dot(second_half, earlier_group)
    target = lax.broadcasted_iota(I32, (LANES, grid_rows), 1) // block * cap
    spot = target.astype(F32) + jnp.where(
        before < first_half,
        first_base + before,
        second_base + before - first_half + cap // 2,
    )
    spread_out = exact_dot(spot, hot_major)
    found = jnp.sum(jnp.where(hot_minor > 0, spread_out, 0.0), axis=0, keepdims=True)
    place[...] = jnp.where(occupied, found.astype(I32), shards * cap)
    to_smem = pltpu.make_async_copy(place, place_smem, sems.at[1])
    to_smem.start()
    to_out = pltpu.make_async_copy(place, place_out, sems.at[2])
    to_out.start()
    feature_copy.wait()
    whole_rows = zone_rows // LANES * LANES
    convert_rows(narrow, 0, wide, 0, whole_rows)
    if whole_rows < zone_rows:
        wide[pl.ds(whole_rows, zone_rows - whole_rows), :] = narrow[
            pl.ds(whole_rows, zone_rows - whole_rows), :
        ].astype(F32)
    to_smem.wait()

    stride = slots // ROW_STEP

    def place_rows(i, carry):
        for k in range(ROW_STEP):
            target = place_smem.at[:, pl.ds(k * stride, stride)][0, i]
            packed[pl.ds(target, 1), :] = wide.at[pl.ds(k * stride, stride)][pl.ds(i, 1), :]
        return carry

    lax.fori_loop(0, stride, place_rows, 0)
    for k in range(shards):
        at = pl.multiple_of(lax.rem(here + k, shards) * cap, cap)
        convert_rows(packed, at, sends[k], 0, cap)
    to_out.wait()


def pack(held, rank, z_feat, columns_at, width, shards, cap, rows_here):
    zone_rows = z_feat.shape[0]
    slots = round_up(zone_rows, LANES)
    return pl.pallas_call(
        functools.partial(pack_kernel, shards, cap, rows_here, columns_at),
        out_shape=[jax.ShapeDtypeStruct((cap, width), BF)] * shards
        + [jax.ShapeDtypeStruct((1, slots), I32)],
        in_specs=[SMEM, VMEM, ANY],
        out_specs=[VMEM] * shards + [ANY],
        scratch_shapes=[
            pltpu.VMEM((1, slots), I32),
            pltpu.SMEM((1, slots), I32),
            pltpu.VMEM((1, slots), I32),
            pltpu.VMEM((zone_rows, width), BF),
            pltpu.VMEM((slots, width), F32),
            pltpu.VMEM((shards * cap + 8, width), F32),
            pltpu.SemaphoreType.DMA((3,)),
        ],
        name="pack",
    )(held, rank, z_feat)


def keep_kernel(block, out):
    out[...] = block[...]


def keep(block):
    return pl.pallas_call(
        keep_kernel,
        out_shape=jax.ShapeDtypeStruct(block.shape, block.dtype),
        in_specs=[VMEM],
        out_specs=VMEM,
        compiler_params=grant(2),
        name="keep",
    )(block)


def move_segment(source, source_at, target, target_at, length):
    def one(i, carry):
        for k in range(8):
            target[pl.ds(target_at + i * 64 + k * 8, 8), :] = source[
                pl.ds(source_at + i * 64 + k * 8, 8), :
            ]
        return carry

    lax.fori_loop(0, (length + 63) // 64, one, 0)


def segment_table(pieces, patches, shards, cap):
    packed_at, patch_at, lengths = {}, {}, {}
    for s in range(shards):
        ends = [s * cap, s * cap + cap // 2]
        for p in range(patches):
            count = pieces[p, s]
            lengths[0, p, s] = lax.shift_right_logical(count, 1)
            lengths[1, p, s] = count - lengths[0, p, s]
            for half in range(2):
                packed_at[half, p, s] = ends[half]
                ends[half] = ends[half] + lengths[half, p, s]
    for p in range(patches):
        at = p * PATCH
        for half in range(2):
            for s in range(shards):
                patch_at[half, p, s] = at
                at = at + lengths[half, p, s]
    return packed_at, patch_at, lengths


def compact_kernel(shards, patches, group, cap, pieces, *refs):
    blocks = refs[:shards]
    outs = refs[shards : shards + patches]
    wide, patch_rows = refs[shards + patches :]
    here, member = lax.axis_index("pts"), lax.axis_index("head")
    for k in range(shards):
        at = pl.multiple_of(lax.rem(here - k + shards, shards) * cap, cap)
        convert_rows(blocks[k], 0, wide, at, cap)
    packed_at, patch_at, lengths = segment_table(pieces, patches, shards, cap)
    for p in range(patches):
        for half in range(2):
            for s in range(shards):
                key = half, p, s
                move_segment(wide, packed_at[key], patch_rows, patch_at[key], lengths[key])
    own_group = member // group
    for k in range(patches):
        at = pl.multiple_of(lax.rem(own_group + k, patches) * PATCH, PATCH)
        convert_rows(patch_rows, at, outs[k], 0, PATCH)


def compact(pieces, blocks, patches, group):
    shards = len(blocks)
    cap, width = blocks[0].shape
    return pl.pallas_call(
        functools.partial(compact_kernel, shards, patches, group, cap),
        out_shape=[jax.ShapeDtypeStruct((PATCH, width), BF)] * patches,
        in_specs=[SMEM] + [VMEM] * shards,
        out_specs=[VMEM] * patches,
        scratch_shapes=[
            pltpu.VMEM((shards * cap + 64, width), F32),
            pltpu.VMEM((patches * PATCH + 64, width), F32),
        ],
        compiler_params=grant(12),
        name="compact",
    )(pieces, *blocks)


def spread_kernel(shards, patches, members, cap, half, pieces, *refs):
    given = members * (half + 1)
    blocks = refs[:given]
    sends = refs[given : given + shards]
    patch_rows, wide = refs[given + shards :]
    here, member = lax.axis_index("pts"), lax.axis_index("head")
    group = members // patches
    part_rows = blocks[0].shape[0]
    for phase in range(half + 1):
        for k in range(members):
            source = lax.rem(member - k + members, members)
            at = source // group * PATCH + phase * (PATCH // 2)
            at = pl.multiple_of(at + lax.rem(source, group) * part_rows, part_rows)
            convert_rows(blocks[phase * members + k], 0, patch_rows, at, part_rows)
    packed_at, patch_at, lengths = segment_table(pieces, patches, shards, cap)
    size = cap // 2
    for s in range(shards):
        for p in range(patches):
            key = half, p, s
            move_segment(
                patch_rows,
                patch_at[key],
                wide,
                packed_at[key] - s * cap - half * size + s * size,
                lengths[key],
            )
    for k in range(shards):
        at = pl.multiple_of(lax.rem(here + k, shards) * size, size)
        convert_rows(wide, at, sends[k], 0, size)


def spread(pieces, blocks, patches, members, shards, cap, half):
    width = blocks[0].shape[1]
    return pl.pallas_call(
        functools.partial(spread_kernel, shards, patches, members, cap, half),
        out_shape=[jax.ShapeDtypeStruct((cap // 2, width), BF)] * shards,
        in_specs=[SMEM] + [VMEM] * len(blocks),
        out_specs=[VMEM] * shards,
        scratch_shapes=[
            pltpu.VMEM((patches * PATCH + 64, width), F32),
            pltpu.VMEM((shards * cap // 2 + 64, width), F32),
        ],
        compiler_params=grant(12),
        name="spread",
    )(pieces, *blocks)


def unpack_kernel(shards, cap, held, place, *refs):
    blocks = refs[: 2 * shards]
    out = refs[2 * shards]
    wide, picked = refs[2 * shards + 1 :]
    here, count = lax.axis_index("pts"), held[0]
    zone_rows, width = out.shape
    size = cap // 2
    for half in range(2):
        for k in range(shards):
            at = lax.rem(here - k + shards, shards) * cap + half * size
            convert_rows(blocks[half * shards + k], 0, wide, pl.multiple_of(at, size), size)

    stride = picked.shape[0] // ROW_STEP

    def pick_rows(i, carry):
        for k in range(ROW_STEP):
            source = place.at[:, pl.ds(k * stride, stride)][0, i]
            picked.at[pl.ds(k * stride, stride)][pl.ds(i, 1), :] = wide[pl.ds(source, 1), :]
        return carry

    lax.fori_loop(0, stride, pick_rows, 0)

    def masked(at, rows):
        slot = at + lax.broadcasted_iota(I32, (rows, width), 0)
        out[pl.ds(at, rows), :] = jnp.where(slot < count, picked[pl.ds(at, rows), :], 0.0).astype(
            BF
        )

    def one(i, carry):
        masked(pl.multiple_of(i * LANES, LANES), LANES)
        return carry

    whole_rows = zone_rows // LANES * LANES
    lax.fori_loop(0, whole_rows // LANES, one, 0)
    if whole_rows < zone_rows:
        masked(whole_rows, zone_rows - whole_rows)


def unpack(held, place, blocks, zone_rows):
    shards = len(blocks) // 2
    size, width = blocks[0].shape
    cap = 2 * size
    slots = place.shape[1]
    return pl.pallas_call(
        functools.partial(unpack_kernel, shards, cap),
        out_shape=jax.ShapeDtypeStruct((zone_rows, width), BF),
        in_specs=[SMEM, SMEM] + [VMEM] * (2 * shards),
        out_specs=VMEM,
        scratch_shapes=[
            pltpu.VMEM((shards * cap + 8, width), F32),
            pltpu.VMEM((slots, width), F32),
        ],
        compiler_params=grant(14),
        name="unpack",
    )(held, place, *blocks)


def row_stats(parts, width):
    total = jnp.sum(sum(parts[1:], parts[0]), axis=1, keepdims=True)
    squares = jnp.sum(
        sum((x * x for x in parts[1:]), parts[0] * parts[0]), axis=1, keepdims=True
    )
    mean = total / width
    var = squares / width - mean * mean
    return mean, lax.rsqrt(var + 1e-05)


def block_places(blocks, patches, group):
    if blocks == patches * group:
        return arrival_order(patches, group)
    return list(range(blocks))


def project_kernel(blocks, patches, group, params, *refs):
    feats = refs[:blocks]
    weights = refs[blocks : 2 * blocks]
    keys, values, query, kept, small, normed = refs[2 * blocks :]
    rows = feats[0].shape[0]
    width = blocks * LANES
    queries = query.shape[1] // 2
    places = block_places(blocks, patches, group)
    part = lax.rem(lax.axis_index("head"), group)

    def norm(i, carry):
        at = pl.ds(pl.multiple_of(i * 128, 128), 128)
        parts = [feats[b][at, :].astype(F32) for b in range(blocks)]
        mean, scale = row_stats(parts, width)
        for b in range(blocks):
            cols = pl.ds(pl.multiple_of(places[b] * LANES, LANES), LANES)
            normed[at, cols] = (
                (parts[b] - mean) * scale * params[0:1, cols] + params[1:2, cols]
            ).astype(BF)
        return carry

    lax.fori_loop(0, rows // 128, norm, 0, unroll=2)
    starts = [
        pl.multiple_of(part * queries + half * (rows // 2), queries) for half in range(2)
    ]
    for b in range(blocks):
        for half in range(2):
            kept[places[b], pl.ds(half * queries, queries), :] = feats[b][
                pl.ds(starts[half], queries), :
            ]
    score_scale = HEAD_DIM ** (-0.5) * math.log2(math.e)
    pair_of = 2 if blocks % 2 == 0 else 1
    span = pair_of * LANES
    head_r = lax.broadcasted_iota(I32, (span, span), 0) // HEAD_DIM
    head_c = lax.broadcasted_iota(I32, (span, span), 1) // HEAD_DIM
    same_head = (head_r == head_c).astype(BF)

    def largest(found):
        return jnp.max(jnp.abs(found), axis=0, keepdims=True)

    def pair_weight(b, kind):
        return jnp.concatenate([weights[c][kind] for c in range(b, b + pair_of)], axis=1)

    worst = None
    for b in range(0, blocks, pair_of):
        key_most, query_most = None, None
        k_weight, q_weight = pair_weight(b, 1), pair_weight(b, 0)
        for half in range(2):
            at = pl.ds(starts[half], queries)
            found = dot(normed[at, :], q_weight) * score_scale
            most = largest(found)
            query_most = most if half == 0 else jnp.maximum(query_most, most)
            for n in range(pair_of):
                query[b + n, pl.ds(half * queries, queries), :] = found[
                    :, n * LANES : (n + 1) * LANES
                ].astype(BF)
        for i in range(rows // 256):
            at = pl.ds(i * 256, 256)
            found = dot(normed[at, :], k_weight)
            most = largest(found)
            key_most = most if i == 0 else jnp.maximum(key_most, most)
            for n in range(pair_of):
                keys[b + n, at, :] = found[:, n * LANES : (n + 1) * LANES].astype(BF)
        product = jnp.broadcast_to(key_most * query_most, (8, span)).astype(BF)
        bound = dot(product, same_head)
        worst = bound if b == 0 else jnp.maximum(worst, bound)
    is_small = (jnp.max(worst) * 1.05 < SAFE_LOG2).astype(I32)
    for b in range(0, blocks, pair_of):
        turned = dot(pair_weight(b, 2), normed[...], (0, 1))
        for n in range(pair_of):
            values[b + n] = turned[n * LANES : (n + 1) * LANES].astype(BF)
    small[0] = is_small


def project(feats, weights, params, patches, group):
    blocks = len(feats)
    rows = feats[0].shape[0]
    width = weights[0].shape[1]
    own = jax.ShapeDtypeStruct((blocks, rows // group, LANES), BF)
    return pl.pallas_call(
        functools.partial(project_kernel, blocks, patches, group),
        out_shape=[
            jax.ShapeDtypeStruct((blocks, rows, LANES), BF),
            jax.ShapeDtypeStruct((blocks, LANES, rows), BF),
            own,
            own,
            jax.ShapeDtypeStruct((1,), I32),
        ],
        in_specs=[VMEM] * (1 + 2 * blocks),
        out_specs=[VMEM] * 4 + [SMEM],
        scratch_shapes=[pltpu.VMEM((rows, width), BF)],
        compiler_params=grant(14),
        cost_estimate=pl.CostEstimate(
            flops=6 * rows * width * width, bytes_accessed=8 * rows * width, transcendentals=0
        ),
        name="project",
    )(params, *feats, *weights)


def attend_kernel(low, high, half, tile, small, keys, values, query, out, even, odd):
    rows = keys.shape[1]
    queries = query.shape[1] // 2
    lane = lax.broadcasted_iota(I32, (1, LANES), 1)
    per_block = LANES // HEAD_DIM // 2
    steps = (high - low) * per_block

    def select(index):
        b, j = low + index // per_block, index % per_block
        own = query[b, pl.ds(half * queries, queries), :]
        zero = jnp.zeros((), BF)
        return jnp.concatenate(
            [jnp.where(lane // HEAD_DIM == 2 * j + n, own, zero) for n in range(2)], axis=0
        )

    def step(index, scores, top, coming, next_scores):
        b, j = index // per_block, index % per_block
        at = [
            pl.ds(pl.multiple_of((2 * j + n) * HEAD_DIM, HEAD_DIM), HEAD_DIM) for n in range(2)
        ]
        own = select(coming)
        next_keys = low + coming // per_block
        summed, next_top = [None, None], None
        for i in range(rows // tile):
            part = pl.ds(i * tile, tile)
            found = dot(keys[next_keys, part, :], own, (1, 1))
            next_scores[part, :] = found
            most = jnp.max(found, axis=0, keepdims=True)
            next_top = most if i == 0 else jnp.maximum(next_top, most)
            if top is not None:
                raised = jnp.exp2(scores[part, :] - top).astype(BF)
                for n in range(2):
                    lhs = jnp.concatenate(
                        [
                            values[low + b, at[n], i * tile : (i + 1) * tile],
                            jnp.ones((HEAD_DIM, tile), BF),
                        ],
                        axis=0,
                    )
                    more = dot(lhs, raised[:, n * queries : (n + 1) * queries])
                    summed[n] = more if i == 0 else summed[n] + more
        if top is not None:
            for n in range(2):
                out[b, at[n], :] = (summed[n][:HEAD_DIM] / summed[n][HEAD_DIM:]).astype(BF)
        return next_top

    def pair(i, top):
        once = jnp.minimum(i, 0) + 1
        next_top = lax.fori_loop(
            0, once, lambda _, most: step(2 * i, even, top, 2 * i + 1, odd), top
        )
        following = jnp.minimum(2 * i + 2, steps - 1)
        return lax.fori_loop(
            0, once, lambda _, most: step(2 * i + 1, odd, next_top, following, even), next_top
        )

    @pl.when(small[0] == 0)
    def _():
        lax.fori_loop(0, steps // 2, pair, step(0, None, None, 0, even))

    fast_tile = min(FAST_TILE, rows)
    tiles = rows // fast_tile

    def several(i, carry):
        indexes = [UNROLL * i + u for u in range(UNROLL)]
        plan = [(u, t) for u in range(UNROLL) for t in range(tiles)]
        owns = [None] * UNROLL

        def score(u, t):
            if t == 0:
                owns[u] = select(indexes[u])
            part = pl.ds(t * fast_tile, fast_tile)
            return dot(keys[low + indexes[u] // per_block, part, :], owns[u], (1, 1))

        waiting = [score(*plan[n]) for n in range(min(AHEAD, len(plan)))]
        summed = [None, None]
        for n, (u, t) in enumerate(plan):
            if n + AHEAD < len(plan):
                waiting.append(score(*plan[n + AHEAD]))
            raised = jnp.exp2(waiting[n]).astype(BF)
            b, j = indexes[u] // per_block, indexes[u] % per_block
            for m in range(2):
                at = pl.ds(pl.multiple_of((2 * j + m) * HEAD_DIM, HEAD_DIM), HEAD_DIM)
                lhs = jnp.concatenate(
                    [
                        values[low + b, at, t * fast_tile : (t + 1) * fast_tile],
                        jnp.ones((HEAD_DIM, fast_tile), BF),
                    ],
                    axis=0,
                )
                more = dot(lhs, raised[:, m * queries : (m + 1) * queries])
                summed[m] = more if t == 0 else summed[m] + more
                if t == tiles - 1:
                    out[b, at, :] = (summed[m][:HEAD_DIM] / summed[m][HEAD_DIM:]).astype(BF)
        return carry

    @pl.when(small[0] != 0)
    def _():
        lax.fori_loop(0, steps // UNROLL, several, 0)


def attend(small, keys, values, query, low, high, half):
    rows = keys.shape[1]
    queries = query.shape[1] // 2
    return pl.pallas_call(
        functools.partial(attend_kernel, low, high, half, min(TILE, rows)),
        out_shape=jax.ShapeDtypeStruct((high - low, LANES, queries), BF),
        in_specs=[SMEM] + [VMEM] * 3,
        out_specs=VMEM,
        scratch_shapes=[pltpu.VMEM((rows, 2 * queries), F32)] * 2,
        compiler_params=grant(14),
        cost_estimate=pl.CostEstimate(
            flops=4 * queries * rows * LANES * (high - low) * (LANES // HEAD_DIM),
            bytes_accessed=4 * rows * LANES * (high - low),
            transcendentals=0,
        ),
        name="attend",
    )(small, keys, values, query)


def mlp_kernel(blocks, members, patches, sends, chunk, half, pieces_of, params, kept, *refs):
    mixed = refs[:pieces_of]
    refs = refs[pieces_of:]
    projs = refs[:blocks]
    ups = refs[blocks : blocks + members]
    downs = refs[blocks + members : blocks + 2 * members]
    vectors = refs[blocks + 2 * members : blocks + 3 * members]
    results = refs[blocks + 3 * members : blocks + 3 * members + sends]
    proj, vector, final = refs[blocks + 3 * members + sends :]
    rows = kept.shape[1] // 2
    width = blocks * LANES
    share = width // members
    group = members // patches
    spots = arrival_order(patches, group)
    places = block_places(blocks, patches, group)
    for k in range(blocks):
        cols = pl.ds(pl.multiple_of(places[k] * LANES, LANES), LANES)
        for r in range(blocks):
            from_rows = pl.ds(pl.multiple_of(places[r] * LANES, LANES), LANES)
            proj[r * LANES : (r + 1) * LANES, cols] = projs[k][from_rows, :]
    for k in range(members):
        vector[spots[k]] = vectors[k][...]
    out_bias = jnp.concatenate([vector[k, :, :share] for k in range(members)], axis=1)
    down_bias = jnp.concatenate([vector[k, :, share : 2 * share] for k in range(members)], axis=1)
    root_half = 0.5 ** 0.5

    def one(i, carry):
        at = pl.ds(pl.multiple_of(i * chunk, chunk), chunk)
        attended = jnp.concatenate(
            [m[b, :, at] for m in mixed for b in range(m.shape[0])], axis=0
        )
        own = pl.ds(pl.multiple_of(half * rows + i * chunk, chunk), chunk)
        features = jnp.concatenate([kept[b, own, :] for b in range(blocks)], axis=1)
        residual = (features.astype(F32) + dot(attended, proj[...], (0, 0)) + out_bias).astype(BF)
        wide = residual.astype(F32)
        mean, scale = row_stats([wide], width)
        normed = ((wide - mean) * scale * params[2:3, :] + params[3:4, :]).astype(BF)
        total = wide + down_bias
        for k in range(members):
            spot = spots[k]
            before = dot(normed, ups[k][...]) + vector[spot, :, 2 * share :]
            hidden = (0.5 * before * (1.0 + lax.erf(before * root_half))).astype(BF)
            total = total + dot(hidden, downs[k][...])
        for b in range(blocks):
            final[b, at, :] = total[:, b * LANES : (b + 1) * LANES].astype(BF)
        return carry

    lax.fori_loop(0, rows // chunk, one, 0)
    if sends > 1:
        me = lax.axis_index("head")
        for k in range(sends):
            results[k][...] = final[lax.rem(me + k, sends)]
    else:
        results[0][...] = final[...]


def mlp(patches, half, params, mixed, kept, projs, ups, downs, vectors):
    blocks, rows = kept.shape[0], kept.shape[1] // 2
    members = len(ups)
    width = blocks * LANES
    hidden_here = ups[0].shape[1]
    sends = members if members == blocks else 1
    shape = (rows, LANES) if sends > 1 else (blocks, rows, LANES)
    chunk = min(256, rows)
    return pl.pallas_call(
        functools.partial(
            mlp_kernel, blocks, members, patches, sends, chunk, half, len(mixed)
        ),
        out_shape=[jax.ShapeDtypeStruct(shape, BF)] * sends,
        in_specs=[VMEM] * (2 + len(mixed) + blocks + 3 * members),
        out_specs=[VMEM] * sends,
        scratch_shapes=[
            pltpu.VMEM((width, width), BF),
            pltpu.VMEM((members, 1, vectors[0].shape[1]), F32),
            pltpu.VMEM((blocks, rows, LANES), BF),
        ],
        cost_estimate=pl.CostEstimate(
            flops=4 * rows * width * hidden_here * members,
            bytes_accessed=4 * width * hidden_here * members,
            transcendentals=0,
        ),
        compiler_params=grant(22),
        name="mlp",
    )(params, kept, *mixed, *projs, *ups, *downs, *vectors)


def shift(array, axis, size, step):
    return lax.ppermute(array, axis, [(i, (i + step) % size) for i in range(size)])


def exchange(blocks, axis, size):
    if size <= DIRECT:
        return [blocks[0]] + [shift(blocks[k], axis, size, k) for k in range(1, size)]
    me = lax.axis_index(axis)
    steps = jnp.arange(size, dtype=I32)
    stacked = jnp.stack(blocks)[(steps - me) % size]
    got = lax.all_to_all(stacked, axis, 0, 0, tiled=True)[(me - steps) % size]
    return [got[k] for k in range(size)]


def arrival_order(groups, group):
    member = lax.axis_index("head")
    return [
        lax.rem(member // group - k + groups, groups) * group
        + lax.rem(lax.rem(member, group) - j + group, group)
        for k in range(groups)
        for j in range(group)
    ]


def group_shift(array, groups, group, step):
    size = groups * group
    pairs = [(i, (i // group + step) % groups * group + i % group) for i in range(size)]
    return lax.ppermute(array, "head", pairs)


def member_shift(array, groups, group, step):
    size = groups * group
    pairs = [(i, i // group * group + (i % group + step) % group) for i in range(size)]
    return lax.ppermute(array, "head", pairs)


def gather_members(sources, groups, group):
    found = []
    for k in range(groups):
        moved = sources[k]
        if k > 0:
            moved = group_shift(moved, groups, group, k)
        for j in range(group):
            found.append(moved if j == 0 else member_shift(moved, groups, group, j))
    return found


def body(
    z_feat,
    shard_count,
    hilbert_rank,
    z_slot,
    ln1_gain,
    ln1_bias,
    w_qkv,
    w_out,
    b_out,
    ln2_gain,
    ln2_bias,
    w_up,
    b_up,
    w_down,
    b_down,
):
    shards = lax.axis_size("pts")
    members = lax.axis_size("head")
    rows_here = z_slot.shape[0]
    zone_rows, full_width = z_feat.shape
    width = w_out.shape[1]
    patches = rows_here // PATCH
    group = members // patches
    blocks = full_width // LANES
    skew_step = rows_here // (2 * shards * (shards - 1))
    cap = round_up(rows_here // shards + 2 * skew_step * (shards - 1), 32)
    member = lax.axis_index("head")

    def natural(found):
        spots = jnp.stack(arrival_order(patches, group)).astype(I32)
        stacked = jnp.stack(found)
        back = jnp.zeros((members,), I32).at[spots].set(jnp.arange(members, dtype=I32))
        stacked = jnp.take(stacked, back, axis=0)
        joined = jnp.concatenate([stacked[i] for i in range(members)], axis=-1)
        return [joined[..., b * LANES : (b + 1) * LANES] for b in range(blocks)]

    def everywhere(array):
        return gather_members([array] * patches, patches, group)

    qkv_found = everywhere(w_qkv)
    out_found = everywhere(w_out)
    up_found = everywhere(w_up)
    down_found = everywhere(w_down)
    vector = jnp.concatenate([b_out, b_down, b_up])[None, :]
    vectors = [vector]
    for step in range(1, members):
        k, j = step // group, step % group
        pairs = [
            (i, (i // group + k) % patches * group + (i % group + j) % group)
            for i in range(members)
        ]
        vectors.append(lax.ppermute(vector, "head", pairs))

    rank = hilbert_rank[None, :]
    if width % LANES == 0:
        z_source = z_feat
    else:
        z_source = lax.dynamic_slice_in_dim(z_feat, member * width, width, 1)
    *sends, place = pack(
        shard_count, rank, z_source, width % LANES == 0, width, shards, cap, rows_here
    )
    source = (z_slot // zone_rows).reshape(patches, PATCH, 1)
    pieces = jnp.sum((source == jnp.arange(shards, dtype=I32)).astype(I32), axis=1)
    params = jnp.stack([ln1_gain, ln1_bias, ln2_gain, ln2_bias])
    pieces, params = lax.optimization_barrier((pieces, params))
    arrived = exchange(sends, "pts", shards)
    arrived[0] = keep(arrived[0])
    patch_blocks = compact(pieces, arrived, patches, group)
    feats = gather_members(patch_blocks, patches, group)

    if width == LANES:
        qkv_blocks, out_blocks = qkv_found, out_found
    else:
        feats = natural(feats)
        qkv_blocks, out_blocks = natural(qkv_found), natural(out_found)

    keys, values, query, kept, small = project(feats, qkv_blocks, params, patches, group)

    def columns_back(half, mixed):
        results = mlp(
            patches, half, params, mixed, kept, out_blocks, up_found, down_found, vectors
        )
        if width != LANES:
            joined = jnp.concatenate([results[0][b] for b in range(blocks)], axis=1)
            results = [
                lax.dynamic_slice_in_dim(joined, (member + k) % members * width, width, 1)
                for k in range(members)
            ]
        return [results[0]] + [shift(results[k], "head", members, k) for k in range(1, members)]

    mixed = attend(small, keys, values, query, 0, blocks, 0)
    parts = columns_back(0, [mixed])
    middle = blocks // 2
    mixed_low = attend(small, keys, values, query, 0, middle, 1)
    outgoing = spread(pieces, parts, patches, members, shards, cap, 0)
    returned = exchange(outgoing, "pts", shards)
    mixed_high = attend(small, keys, values, query, middle, blocks, 1)
    parts = parts + columns_back(1, [mixed_low, mixed_high])
    outgoing = spread(pieces, parts, patches, members, shards, cap, 1)
    returned = returned + exchange(outgoing, "pts", shards)
    return unpack(shard_count, place, returned, zone_rows)


def solution(mesh):
    placed = (
        P(("tile", "pts"), None),
        P(("tile", "pts")),
        P(("tile", "pts")),
        P(("tile", "pts")),
        P(),
        P(),
        P(None, None, "head"),
        P(None, "head"),
        P("head"),
        P(),
        P(),
        P(None, "head"),
        P("head"),
        P("head", None),
        P("head"),
    )

    return jax.shard_map(
        body, mesh=mesh, in_specs=placed, out_specs=P(("tile", "pts"), "head"), check_vma=False
    )
```
